32 devices in a mesh: proto: 8 (over z, x), design: 4 (over y, core).
Axes of the slice: x: 2, y: 2, z: 4, core: 2. Of those that a mesh axis runs over, the one named last changes fastest.
Arguments:
- designs: bfloat16 [32768, 1024], P(('proto', 'design')), may hold values from -32 to 32
- prototypes: float32 [16384, 1024], P('proto'), may hold values from -6 to 6
- candidates: int32 [32, 24], P(('proto', 'design')), may hold values from 0 to 127, as said below
- positives: int32 [32768], P(('proto', 'design')), may hold values from 0 to 16383, as said below
Outputs:
- losses: float32 [32768], P(('proto', 'design'))
- design_grad: bfloat16 [32768, 1024], P(('proto', 'design'))
- proto_grad: float32 [16384, 1024], P(('proto', 'design'))
The draws below stay inside these ranges and needn't reach their ends.
Inputs may be any that keep to these rules, and one draw needn't show every extreme that they name: `candidates`: row g lists 24 distinct blocks for the designs of device g along proto+design. Block b lies in proto shard b // 16; at most 4 blocks of a row lie in one proto shard, and in every draw one shard holds exactly 4 blocks of every row. `positives`: the positive row of design i lies in one of the blocks of row i // 1024 of candidates.
All inputs are finite; a program needn't handle non-finite values.
Results may differ from the reference program's by a relative error of at most 0.0062.
Values may be sent and summed in bfloat16 or wider, within the bound.
No kernel may reach another device: no remote copies, remote signals or barrier semaphores. Data moves between devices by JAX's collectives and lax.ppermute only.
A program may use at most 128 MiB of HBM per device.

```python
import jax
import jax.numpy as jnp
from jax import lax

D = 1024
TILE = 128
B_DEV = 1024
BLOCKS_DEV = 16
CANDS = 24
DESIGNS = 32768
PROTOS = 16384
N_PROTO = 8
N_DESIGN = 4


def candidate_table(key):
    dev_count = N_PROTO * N_DESIGN
    capacity = max(2, (4 * CANDS + 3 * N_PROTO - 1) // (3 * N_PROTO))
    least_full = max(1, -((N_PROTO - CANDS) // (capacity - 1)))
    most_full = CANDS // capacity
    key_pop, key_hot, key_jitter, key_full, key_block, key_shuffle = jax.random.split(key, 6)
    owner_ids = jnp.arange(N_PROTO, dtype=jnp.int32)
    popular = jax.random.randint(key_pop, (N_PROTO,), 0, 4)
    hot_owner = jax.random.randint(key_hot, (), 0, N_PROTO)
    popular = jnp.where(owner_ids == hot_owner, 8, popular)
    jitter = jax.random.randint(key_jitter, (dev_count, N_PROTO), 0, N_PROTO)
    scores = (popular[None, :] * N_PROTO + jitter) * N_PROTO + owner_ids[None, :]
    ranking = jnp.argsort(-scores, axis=1).astype(jnp.int32)
    full_count = jax.random.randint(key_full, (dev_count, 1), least_full, most_full + 1)
    entries = jnp.arange(CANDS, dtype=jnp.int32)[None, :]
    full_slots = full_count * capacity
    rank_of = jnp.where(entries < full_slots, entries // capacity, full_count + entries - full_slots)
    copy_index = jnp.where(entries < full_slots, entries % capacity, 0)
    owners = jnp.take_along_axis(ranking, rank_of, axis=1)
    block_scores = jax.random.randint(key_block, (dev_count, N_PROTO, BLOCKS_DEV), 0, 2 ** 20) * BLOCKS_DEV + jnp.arange(BLOCKS_DEV, dtype=jnp.int32)
    block_order = jnp.argsort(block_scores, axis=2).astype(jnp.int32)
    device_ids = jnp.arange(dev_count, dtype=jnp.int32)[:, None]
    local_ids = block_order[device_ids, owners, copy_index]
    block_ids = owners * BLOCKS_DEV + local_ids
    shuffle = jnp.argsort(jax.random.randint(key_shuffle, (dev_count, CANDS), 0, 2 ** 20) * CANDS + entries, axis=1)
    return jnp.take_along_axis(block_ids, shuffle, axis=1).astype(jnp.int32)


def prototype_values(key):
    key_main = jax.random.fold_in(jax.random.fold_in(key, 21), 0)
    values = jax.random.normal(key_main, (PROTOS, D), jnp.float32)
    return jnp.clip(values, -6.0, 6.0)


def draw_candidates(key, part):
    return candidate_table(jax.random.fold_in(key, 11))


def draw_positives(key, part):
    dev_count = N_PROTO * N_DESIGN
    block_table = candidate_table(jax.random.fold_in(key, 11))
    chosen = jax.random.randint(jax.random.fold_in(key, 12), (dev_count, B_DEV), 0, CANDS)
    within = jax.random.randint(jax.random.fold_in(key, 13), (dev_count, B_DEV), 0, TILE)
    blocks = jnp.take_along_axis(block_table, chosen, axis=1)
    return (blocks * TILE + within).reshape(-1).astype(jnp.int32)


def draw_prototypes(key, part):
    return prototype_values(key)


def draw_designs(key, part):
    key_main = jax.random.fold_in(jax.random.fold_in(key, 31), 0)
    values = jax.random.normal(key_main, (DESIGNS, D), jnp.float32)
    return jnp.clip(values, -32.0, 32.0).astype(jnp.bfloat16)


def setup_inputs(seed: int = 0) -> dict:
    splits = jax.random.split(jax.random.key(seed), 5)
    return {
        "designs": draw_designs(jax.random.fold_in(splits[4], 71), 0),
        "prototypes": draw_prototypes(jax.random.fold_in(splits[4], 71), 0),
        "candidates": draw_candidates(jax.random.fold_in(splits[4], 71), 0),
        "positives": draw_positives(jax.random.fold_in(splits[4], 71), 0),
    }


def contrast(design_rows, cand_rows, block_list, positive_ids):
    logit_scale = D ** -0.5
    logits = lax.dot_general(design_rows, cand_rows, (((1,), (1,)), ((), ())), preferred_element_type=jnp.float32) * logit_scale
    cand_count = block_list.shape[0]
    block_match = (positive_ids // TILE)[:, None] == block_list[None, :]
    cand_index = jnp.sum(jnp.where(block_match, jnp.arange(cand_count, dtype=jnp.int32)[None, :], 0), axis=1)
    positive_col = cand_index * TILE + positive_ids % TILE
    columns = jnp.arange(cand_count * TILE, dtype=jnp.int32)
    target = columns[None, :] == positive_col[:, None]
    row_max = jnp.max(logits, axis=1, keepdims=True)
    log_total = row_max + jnp.log(jnp.sum(jnp.exp(logits - row_max), axis=1, keepdims=True))
    picked = jnp.sum(jnp.where(target, logits, 0.0), axis=1)
    losses = log_total[:, 0] - picked
    chances = jnp.exp(logits - log_total)
    logit_grad = (chances - target.astype(jnp.float32)).astype(jnp.bfloat16)
    design_grad = jnp.dot(logit_grad, cand_rows, preferred_element_type=jnp.float32).astype(jnp.bfloat16)
    return losses, design_grad, logit_grad


def reference(designs, prototypes, candidates, positives):
    dev_count = N_PROTO * N_DESIGN
    block_count = PROTOS // TILE
    feature_width = designs.shape[1]
    proto_table = prototypes.astype(jnp.bfloat16).reshape(block_count, TILE, feature_width)

    def visit_device(summed, inputs):
        design_rows, block_list, positive_ids = inputs
        cand_rows = jnp.take(proto_table, block_list, axis=0).reshape(-1, feature_width)
        losses, design_grad, logit_grad = contrast(design_rows, cand_rows, block_list, positive_ids)
        tile_grad = lax.dot_general(logit_grad, design_rows, (((0,), (0,)), ((), ())), preferred_element_type=jnp.float32)
        summed = summed.at[block_list].add(tile_grad.reshape(-1, TILE, feature_width))
        return summed, (losses, design_grad)

    initial = jnp.zeros((block_count, TILE, feature_width), jnp.float32)
    summed, outputs = lax.scan(visit_device, initial, (designs.reshape(dev_count, B_DEV, feature_width), candidates, positives.reshape(dev_count, B_DEV)))
    losses, design_grad = outputs
    return losses.reshape(-1), design_grad.reshape(-1, feature_width), summed.reshape(-1, feature_width)
```

```python
import functools

import jax
import jax.numpy as jnp
from jax import lax
from jax.experimental import pallas as pl
from jax.experimental.pallas import tpu as pltpu
from jax.sharding import PartitionSpec as P

D = 1024
TILE = 128
BF = jnp.bfloat16
F32 = jnp.float32
NEG = -1e30
BOTH = ("proto", "design")


def xor_proto(x, shift, count):
    return lax.ppermute(x, "proto", [(i, i ^ shift) for i in range(count)])


def xor_design(x, shift, count):
    return lax.ppermute(x, "design", [(i, i ^ shift) for i in range(count)])


def request_table(block_list, blocks_dev, capacity, proto_count):
    owners = block_list // blocks_dev
    local_ids = block_list % blocks_dev
    ids = jnp.arange(block_list.shape[0], dtype=jnp.int32)
    earlier = (owners[:, None] == owners[None, :]) & (ids[None, :] < ids[:, None])
    rank_of = jnp.sum(earlier.astype(jnp.int32), axis=1)
    slot_of = owners * capacity + rank_of
    slots = jnp.arange(proto_count * capacity, dtype=jnp.int32)
    hit = slot_of[None, :] == slots[:, None]
    return jnp.sum(jnp.where(hit, local_ids[None, :] + 1, 0), axis=1) - 1


def gather_round_kernel(tbl, src, out):
    out[...] = src[...].astype(BF)


def gather_round(table, shard):
    cap = table.shape[0]
    width = shard.shape[-1]
    return pl.pallas_call(
        gather_round_kernel,
        out_shape=jax.ShapeDtypeStruct((cap, TILE, width), BF),
        grid_spec=pltpu.PrefetchScalarGridSpec(
            num_scalar_prefetch=1,
            grid=(cap,),
            in_specs=[pl.BlockSpec((1, TILE, width), lambda i, t: (t[i], 0, 0))],
            out_specs=pl.BlockSpec((1, TILE, width), lambda i, t: (i, 0, 0)),
        ),
        name="gather_round",
    )(jnp.maximum(table, 0), shard)


def gather_far_kernel(n_src, n_out, cap, *refs):
    which, where = refs[0], refs[1]
    srcs = refs[2 : 2 + n_src]
    outs = refs[2 + n_src : 2 + n_src + n_out]
    sems = refs[2 + n_src + n_out]
    for s in range(n_out):
        for k in range(cap):
            i = s * cap + k
            for a in range(n_src):

                @pl.when(which[i] == a)
                def _():
                    pltpu.make_async_copy(
                        srcs[a].at[where[i]], outs[s].at[k], sems.at[i]
                    ).start()

    for s in range(n_out):
        for k in range(cap):
            i = s * cap + k
            pltpu.make_async_copy(srcs[0].at[0], outs[s].at[k], sems.at[i]).wait()


def gather_far(which, where, srcs, n_out, cap):
    width = srcs[0].shape[-1]
    hbm = pl.BlockSpec(memory_space=pl.ANY)
    return pl.pallas_call(
        functools.partial(gather_far_kernel, len(srcs), n_out, cap),
        out_shape=[jax.ShapeDtypeStruct((cap, TILE, width), BF)] * n_out,
        grid_spec=pltpu.PrefetchScalarGridSpec(
            num_scalar_prefetch=2,
            grid=(1,),
            in_specs=[hbm] * len(srcs),
            out_specs=[hbm] * n_out,
            scratch_shapes=[pltpu.SemaphoreType.DMA((n_out * cap,))],
        ),
        name="gather_far",
    )(which, where, *srcs)


def soften_kernel(group, *refs):
    designs, ids, pos = refs[0], refs[1], refs[2]
    own = refs[3 : 3 + group]
    rows = refs[3 + group : 3 + 2 * group]
    losses = refs[3 + 2 * group]
    grads = refs[4 + 2 * group :]
    width = own[0].shape[1]
    scale = D ** (-0.5)
    x = designs[...]
    pos_v = pos[...]
    pieces = []
    for s in range(group):
        far = lax.dot_general(
            x, rows[s][...], (((1,), (1,)), ((), ())), preferred_element_type=F32
        )
        pieces.append((group + s, far * scale))
    for s in range(group):
        pieces.append((s, own[s][...]))
    row_max = None
    picked = None
    masked = []
    for n, piece in pieces:
        id_row = ids[:, n * width : (n + 1) * width]
        target = pos_v == id_row
        hit = jnp.sum(jnp.where(target, piece, 0.0), axis=1, keepdims=True)
        piece = jnp.where(id_row >= 0, piece, NEG)
        top = jnp.max(piece, axis=1, keepdims=True)
        row_max = top if row_max is None else jnp.maximum(row_max, top)
        picked = hit if picked is None else picked + hit
        masked.append((n, piece))
    total = None
    powers = []
    for n, piece in masked:
        e = jnp.exp(piece - row_max)
        part = jnp.sum(e, axis=1, keepdims=True)
        total = part if total is None else total + part
        powers.append((n, e))
    losses[...] = row_max + jnp.log(total) - picked
    inv = 1.0 / total
    for n, e in powers:
        id_row = ids[:, n * width : (n + 1) * width]
        target = (pos_v == id_row).astype(F32)
        grads[n][...] = (e * inv - target).astype(BF)


def soften(designs, ids, pos, own, rows, chunk=128):
    group = len(own)
    count, width = designs.shape
    cols = own[0].shape[1]
    return pl.pallas_call(
        functools.partial(soften_kernel, group),
        out_shape=[jax.ShapeDtypeStruct((count, 1), F32)]
        + [jax.ShapeDtypeStruct((count, cols), BF)] * (2 * group),
        grid=(count // chunk,),
        in_specs=[
            pl.BlockSpec((chunk, width), lambda i: (i, 0)),
            pl.BlockSpec(ids.shape, lambda i: (0, 0)),
            pl.BlockSpec((chunk, 1), lambda i: (i, 0)),
        ]
        + [pl.BlockSpec((chunk, cols), lambda i: (i, 0))] * group
        + [pl.BlockSpec(rows[0].shape, lambda i: (0, 0))] * group,
        out_specs=[pl.BlockSpec((chunk, 1), lambda i: (i, 0))]
        + [pl.BlockSpec((chunk, cols), lambda i: (i, 0))] * (2 * group),
        compiler_params=pltpu.CompilerParams(vmem_limit_bytes=56 << 20),
        name="soften",
    )(designs, ids, pos, *own, *rows)


def tile_grad_kernel(grad, designs, out):
    out[...] = lax.dot_general(
        grad[...], designs[...], (((0,), (0,)), ((), ())), preferred_element_type=F32
    ).astype(BF)


def tile_grad(grad, designs, cap):
    count, cols = grad.shape
    width = designs.shape[1]
    out = pl.pallas_call(
        tile_grad_kernel,
        out_shape=jax.ShapeDtypeStruct((cols, width), BF),
        grid=(1,),
        in_specs=[
            pl.BlockSpec((count, cols), lambda i: (0, 0)),
            pl.BlockSpec((count, width), lambda i: (0, 0)),
        ],
        out_specs=pl.BlockSpec((cols, width), lambda i: (0, 0)),
        compiler_params=pltpu.CompilerParams(vmem_limit_bytes=56 << 20),
        name="tile_grad",
    )(grad, designs)
    return out.reshape(cap, TILE, width)


def design_grad_kernel(n, *refs):
    grads, rows, out = refs[:n], refs[n : 2 * n], refs[2 * n]
    acc = None
    for g, r in zip(grads, rows):
        part = jnp.dot(g[...], r[...], preferred_element_type=F32)
        acc = part if acc is None else acc + part
    out[...] = acc.astype(BF)


def design_grad(grads, rows, chunk=256):
    n = len(grads)
    count, cols = grads[0].shape
    width = rows[0].shape[1]
    return pl.pallas_call(
        functools.partial(design_grad_kernel, n),
        out_shape=jax.ShapeDtypeStruct((count, width), BF),
        grid=(count // chunk,),
        in_specs=[pl.BlockSpec((chunk, cols), lambda i: (i, 0))] * n
        + [pl.BlockSpec((cols, width), lambda i: (0, 0))] * n,
        out_specs=pl.BlockSpec((chunk, width), lambda i: (i, 0)),
        compiler_params=pltpu.CompilerParams(vmem_limit_bytes=56 << 20),
        name="design_grad",
    )(*grads, *rows)


def collect_kernel(n, cap, tbl, order, *refs):
    parts, out = refs[:n], refs[n]
    block = order[pl.program_id(0)]
    out[...] = jnp.zeros_like(out)
    for s in range(n):
        for k in range(cap):

            @pl.when(tbl[s * cap + k] == block)
            def _():
                out[0] += parts[s][k].astype(F32)


def collect(table, order, parts):
    n = len(parts)
    cap, tile, width = parts[0].shape
    return pl.pallas_call(
        functools.partial(collect_kernel, n, cap),
        out_shape=jax.ShapeDtypeStruct((order.shape[0], tile, width), F32),
        grid_spec=pltpu.PrefetchScalarGridSpec(
            num_scalar_prefetch=2,
            grid=(order.shape[0],),
            in_specs=[pl.BlockSpec((cap, tile, width), lambda i, t, o: (0, 0, 0))] * n,
            out_specs=pl.BlockSpec((1, tile, width), lambda i, t, o: (i, 0, 0)),
        ),
        compiler_params=pltpu.CompilerParams(vmem_limit_bytes=56 << 20),
        name="collect",
    )(table, order, *parts)


def body(designs, prototypes, candidates, positives):
    proto_count = lax.axis_size("proto")
    design_axis = lax.axis_size("design")
    half = proto_count // 2
    lanes = design_axis // 2
    cand_count = candidates.shape[1]
    width = designs.shape[1]
    count = designs.shape[0]
    blocks_dev = prototypes.shape[0] // TILE
    quarter = blocks_dev // design_axis
    cap = max(2, (4 * cand_count + 3 * proto_count - 1) // (3 * proto_count))
    p = lax.axis_index("proto").astype(jnp.int32)
    d = lax.axis_index("design").astype(jnp.int32)
    q = p % half
    h = p // half
    y = d // 2
    c = d % 2
    shifts = list(range(1, half))

    shard = prototypes.reshape(blocks_dev, TILE, width)
    mine = lax.dynamic_slice_in_dim(shard, d * quarter, quarter, axis=0).astype(BF)
    step = max(1, quarter // 2)
    far_parts = [
        xor_proto(mine[i : i + step], half, proto_count) for i in range(0, quarter, step)
    ]

    wanted = request_table(candidates[0], blocks_dev, cap, proto_count)
    wanted = wanted.reshape(2, half, cap)
    wanted = jnp.stack([wanted[h], wanted[1 - h]], axis=1)
    asked = [lax.dynamic_index_in_dim(wanted, q ^ s, 0, keepdims=False) for s in range(half)]
    asking = [asked[0]] + [xor_proto(asked[s], s, proto_count) for s in shifts]

    out_own = {s: gather_round(asking[s][0], shard) for s in reversed(range(half))}
    own_rows = [out_own[0]] + [xor_proto(out_own[s], s, proto_count) for s in shifts]
    own_rows = [r.reshape(cap * TILE, width) for r in own_rows]

    held = {}
    for i, part in enumerate(far_parts):
        for ys in range(lanes):
            held[0, ys, i] = part if ys == 0 else xor_design(part, 2 * ys, design_axis)
        for ys in range(lanes):
            held[1, ys, i] = xor_design(held[0, ys, i], 1, design_axis)
    keys = sorted(held)
    parts_n = len(far_parts)
    far_ids = jnp.concatenate([jnp.maximum(a[1], 0) for a in asking])
    owner = far_ids // quarter
    which = (((owner % 2) ^ c) * lanes + ((owner // 2) ^ y)) * parts_n + (
        far_ids % quarter
    ) // step
    out_far = gather_far(which, far_ids % step, [held[k] for k in keys], half, cap)
    far_rows = [out_far[0]] + [xor_proto(out_far[s], s, proto_count) for s in shifts]
    far_rows = [r.reshape(cap * TILE, width) for r in far_rows]

    ids = []
    for f in range(2):
        for s in range(half):
            first = ((h if f == 0 else 1 - h) * half + (q ^ s)) * blocks_dev
            block = jnp.where(asked[s][f] >= 0, (first + asked[s][f]) * TILE, -TILE)
            line = jnp.arange(TILE, dtype=jnp.int32)[None, :]
            ids.append(jnp.where(block[:, None] >= 0, block[:, None] + line, -1).reshape(-1))
    ids = jnp.concatenate(ids)[None, :]
    pos = positives[:, None]

    scale = D ** (-0.5)
    own_logits = [
        lax.dot_general(designs, r, (((1,), (1,)), ((), ())), preferred_element_type=F32)
        * scale
        for r in own_rows
    ]
    losses, *grads = soften(designs, ids, pos, own_logits, far_rows)

    def send_back(pieces):
        tiles = {s: tile_grad(pieces[s], designs, cap) for s in reversed(range(half))}
        return [tiles[0]] + [xor_proto(tiles[s], s, proto_count) for s in shifts]

    lane_ids = jnp.arange(lanes, dtype=jnp.int32)
    in_quarter = jnp.arange(quarter, dtype=jnp.int32)

    def reduce_shard(table, tiles):
        def order(core):
            by_shift = (lane_ids ^ y) * 2 + core
            return (by_shift[:, None] * quarter + in_quarter[None, :]).reshape(-1)

        give = collect(table, order(1 - c), tiles).astype(BF)
        keep = collect(table, order(c), tiles)
        keep = keep + xor_design(give, 1, design_axis).astype(F32)
        keep = keep.reshape(lanes, quarter, TILE, width)
        total = keep[0]
        for ys in range(1, lanes):
            total = total + xor_design(keep[ys].astype(BF), 2 * ys, design_axis).astype(F32)
        return total

    far_back = send_back(grads[half:])
    own_back = send_back(grads[:half])
    far_total = reduce_shard(jnp.concatenate([a[1] for a in asking]), far_back)
    crossed = xor_proto(far_total.astype(BF), half, proto_count)
    dgrad = design_grad(grads, own_rows + far_rows)
    own_total = reduce_shard(jnp.concatenate([a[0] for a in asking]), own_back)
    result = (own_total + crossed.astype(F32)).reshape(quarter * TILE, width)
    return (losses.reshape(count), dgrad, result)


def solution(mesh):
    return jax.shard_map(
        body,
        mesh=mesh,
        in_specs=(
            P(("proto", "design"), None),
            P("proto", None),
            P(("proto", "design"), None),
            P(("proto", "design")),
        ),
        out_specs=(
            P(("proto", "design")),
            P(("proto", "design"), None),
            P(("proto", "design"), None),
        ),
        check_vma=False,
    )
```

```python
import functools

import jax
import jax.numpy as jnp
from jax import lax
from jax.experimental import pallas as pl
from jax.experimental.pallas import tpu as pltpu
from jax.sharding import PartitionSpec as P

D = 1024
TILE = 128
BF = jnp.bfloat16
F32 = jnp.float32
NEG = -1e30
BOTH = ("proto", "design")


def xor_proto(x, shift, count):
    return lax.ppermute(x, "proto", [(i, i ^ shift) for i in range(count)])


def xor_design(x, shift, count):
    return lax.ppermute(x, "design", [(i, i ^ shift) for i in range(count)])


def request_table(block_list, blocks_dev, capacity, proto_count):
    owners = block_list // blocks_dev
    local_ids = block_list % blocks_dev
    ids = jnp.arange(block_list.shape[0], dtype=jnp.int32)
    earlier = (owners[:, None] == owners[None, :]) & (ids[None, :] < ids[:, None])
    rank_of = jnp.sum(earlier.astype(jnp.int32), axis=1)
    slot_of = owners * capacity + rank_of
    slots = jnp.arange(proto_count * capacity, dtype=jnp.int32)
    hit = slot_of[None, :] == slots[:, None]
    return jnp.sum(jnp.where(hit, local_ids[None, :] + 1, 0), axis=1) - 1


def whole(shape):
    return pl.BlockSpec(shape, lambda *_: (0,) * len(shape))


HBM = pl.BlockSpec(memory_space=pl.ANY)
PARAMS = pltpu.CompilerParams(vmem_limit_bytes=58 << 20)


def gather_round_kernel(tbl, src, out, buf, sems):
    cap = out.shape[0]
    copies = [pltpu.make_async_copy(src.at[tbl[k]], buf.at[k], sems.at[k]) for k in range(cap)]
    for copy in copies:
        copy.start()
    for k, copy in enumerate(copies):
        copy.wait()
        out[k] = buf[k].astype(BF)


def gather_round(table, shard):
    cap = table.shape[0]
    shape = (cap,) + shard.shape[1:]
    return pl.pallas_call(
        gather_round_kernel,
        out_shape=jax.ShapeDtypeStruct(shape, BF),
        grid_spec=pltpu.PrefetchScalarGridSpec(
            num_scalar_prefetch=1,
            grid=(1,),
            in_specs=[HBM],
            out_specs=whole(shape),
            scratch_shapes=[pltpu.VMEM(shape, F32), pltpu.SemaphoreType.DMA((cap,))],
        ),
        compiler_params=PARAMS,
        name="gather_round",
    )(table, shard)


def gather_far_kernel(n_src, which, where, *refs):
    srcs, out, sems = refs[:n_src], refs[n_src], refs[n_src + 1]
    cap = out.shape[0]
    for k in range(cap):
        for a in range(n_src):

            @pl.when(which[k] == a)
            def _():
                pltpu.make_async_copy(srcs[a].at[where[k]], out.at[k], sems.at[k]).start()

    for k in range(cap):
        pltpu.make_async_copy(srcs[0].at[0], out.at[k], sems.at[k]).wait()


def gather_far(which, where, srcs):
    cap = which.shape[0]
    shape = (cap,) + srcs[0].shape[1:]
    return pl.pallas_call(
        functools.partial(gather_far_kernel, len(srcs)),
        out_shape=jax.ShapeDtypeStruct(shape, BF),
        grid_spec=pltpu.PrefetchScalarGridSpec(
            num_scalar_prefetch=2,
            grid=(1,),
            in_specs=[HBM] * len(srcs),
            out_specs=whole(shape),
            scratch_shapes=[pltpu.SemaphoreType.DMA((cap,))],
        ),
        compiler_params=PARAMS,
        name="gather_far",
    )(which, where, *srcs)


EXP_SCALE = (D ** (-0.5)) * 1.4426950408889634


def fold(tile, op):
    return op(tile.reshape(tile.shape[0] // 8, 8, tile.shape[1]), axis=0)


def slot_stats(base, rel, slots):
    top = None
    hit = None
    for n, ref in slots:
        piece = ref[...]
        target = rel == base[n]
        found = fold(jnp.where(target, piece, 0.0), jnp.sum)
        piece = piece + jnp.where(base[n] < 0, NEG, 0.0)
        high = fold(piece, jnp.max)
        top = high if top is None else jnp.maximum(top, high)
        hit = found if hit is None else hit + found
    return jnp.max(top, axis=0, keepdims=True), jnp.sum(hit, axis=0, keepdims=True)


def slot_power(base, n, ref, top):
    piece = ref[...] + jnp.where(base[n] < 0, NEG, 0.0)
    return jnp.exp2((piece - top) * EXP_SCALE)


def relative(pos, lanes):
    line = lax.broadcasted_iota(jnp.int32, (TILE, lanes), 0)
    return pos - line


def own_kernel(group, cap, lanes, base, x, pos, *refs):
    rows = refs[:group]
    logits = refs[group : 2 * group]
    top_out, sum_out, hit_out = refs[2 * group :]
    count = x.shape[0]
    for j in range(0, count, lanes):
        xs = x[j : j + lanes, :]
        at = pl.ds(j, lanes)
        for s in range(group):
            logits[s][:, at] = lax.dot_general(
                rows[s][...], xs, (((1,), (1,)), ((), ())), preferred_element_type=F32
            )
        slots = [
            (s * cap + k, logits[s].at[pl.ds(k * TILE, TILE), at])
            for s in range(group)
            for k in range(cap)
        ]
        top, hit = slot_stats(base, relative(pos[:, at], lanes), slots)
        total = None
        for n, ref in slots:
            part = fold(slot_power(base, n, ref, top), jnp.sum)
            total = part if total is None else total + part
        top_out[:, at] = top
        hit_out[:, at] = hit
        sum_out[:, at] = jnp.sum(total, axis=0, keepdims=True)


def own_logits(base, x, pos, rows, cap, lanes=256):
    group = len(rows)
    count = x.shape[0]
    line = (1, count)
    shape = (rows[0].shape[0], count)
    return pl.pallas_call(
        functools.partial(own_kernel, group, cap, lanes),
        out_shape=[jax.ShapeDtypeStruct(shape, F32)] * group
        + [jax.ShapeDtypeStruct(line, F32)] * 3,
        grid_spec=pltpu.PrefetchScalarGridSpec(
            num_scalar_prefetch=1,
            grid=(1,),
            in_specs=[whole(x.shape), whole(line)] + [whole(rows[0].shape)] * group,
            out_specs=[whole(shape)] * group + [whole(line)] * 3,
        ),
        compiler_params=PARAMS,
        name="own_logits",
    )(base, x, pos, *rows)


def far_kernel(group, cap, lanes, parts, base, x, pos, top_own, sum_own, hit_own, *refs):
    rows = refs[:group]
    losses, top_out, inv_out = refs[group : group + 3]
    grads = refs[group + 3 : 2 * group + 3]
    tiles = refs[2 * group + 3 : -1]
    logits = refs[-1]
    count, width = x.shape
    scale = D ** (-0.5)
    for j in range(0, count, lanes):
        turn = (j // lanes) % 2
        xs = x[j : j + lanes, :]
        at = pl.ds(j, lanes)
        for s in range(group):
            logits[turn, s * cap * TILE : (s + 1) * cap * TILE, :] = lax.dot_general(
                rows[s][...], xs, (((1,), (1,)), ((), ())), preferred_element_type=F32
            )
        slots = [
            (n, logits.at[turn, pl.ds(n * TILE, TILE), :]) for n in range(group * cap)
        ]
        rel = relative(pos[:, at], lanes)
        top, hit = slot_stats(base, rel, slots)
        mine = top_own[:, at]
        both = jnp.maximum(top, mine)
        total = None
        for n, ref in slots:
            power = slot_power(base, n, ref, both)
            ref[...] = power
            part = fold(power, jnp.sum)
            total = part if total is None else total + part
        total = jnp.sum(total, axis=0, keepdims=True)
        total = total + sum_own[:, at] * jnp.exp2((mine - both) * EXP_SCALE)
        losses[:, at] = both * scale + jnp.log(total) - (hit + hit_own[:, at]) * scale
        inv = 1.0 / total
        top_out[:, at] = both
        inv_out[:, at] = inv
        for n, ref in slots:
            s, k = n // cap, n % cap
            target = jnp.where(rel == base[n], 1.0, 0.0)
            grads[s][k * TILE : (k + 1) * TILE, at] = (ref[...] * inv - target).astype(BF)
    step = width // parts
    for i in range(parts):
        for s in range(group):
            tiles[i * group + s][...] = jnp.dot(
                grads[s][...], x[:, i * step : (i + 1) * step], preferred_element_type=F32
            ).astype(BF)


def far_grads(base, x, pos, stats, rows, cap, parts, lanes=256):
    group = len(rows)
    count, width = x.shape
    line = (1, count)
    size = rows[0].shape[0]
    outs = [((1, count), F32)] * 3 + [((size, count), BF)] * group
    outs += [((size, width // parts), BF)] * (group * parts)
    got = pl.pallas_call(
        functools.partial(far_kernel, group, cap, lanes, parts),
        out_shape=[jax.ShapeDtypeStruct(*o) for o in outs],
        grid_spec=pltpu.PrefetchScalarGridSpec(
            num_scalar_prefetch=1,
            grid=(1,),
            in_specs=[whole(x.shape)] + [whole(line)] * 4 + [whole(rows[0].shape)] * group,
            out_specs=[whole(o[0]) for o in outs],
            scratch_shapes=[pltpu.VMEM((2, group * size, lanes), F32)],
        ),
        compiler_params=PARAMS,
        name="far_grads",
    )(base, x, pos, *stats, *rows)
    tiles = got[3 + group :]
    return got[:3], got[3 : 3 + group], [tiles[i * group : (i + 1) * group] for i in range(parts)]


def own_grad_kernel(cap, parts, base, x, pos, top, inv, logits, grad, *tiles):
    count, width = x.shape
    rel = relative(pos[...], count)
    for k in range(cap):
        ref = logits.at[pl.ds(k * TILE, TILE), :]
        power = slot_power(base, k, ref, top[...])
        target = jnp.where(rel == base[k], 1.0, 0.0)
        grad[k * TILE : (k + 1) * TILE, :] = (power * inv[...] - target).astype(BF)
    step = width // parts
    for i in range(parts):
        tiles[i][...] = jnp.dot(
            grad[...], x[:, i * step : (i + 1) * step], preferred_element_type=F32
        ).astype(BF)


def own_grad(base, x, pos, top, inv, logits, cap, parts):
    count, width = x.shape
    line = (1, count)
    size = logits.shape[0]
    outs = [((size, count), BF)] + [((size, width // parts), BF)] * parts
    got = pl.pallas_call(
        functools.partial(own_grad_kernel, cap, parts),
        out_shape=[jax.ShapeDtypeStruct(*o) for o in outs],
        grid_spec=pltpu.PrefetchScalarGridSpec(
            num_scalar_prefetch=1,
            grid=(1,),
            in_specs=[whole(x.shape)] + [whole(line)] * 3 + [whole(logits.shape)],
            out_specs=[whole(o[0]) for o in outs],
        ),
        compiler_params=PARAMS,
        name="own_grad",
    )(base, x, pos, top, inv, logits)
    return got[0], got[1:]


def design_grad_kernel(n, *refs):
    grads, rows, out = refs[:n], refs[n : 2 * n], refs[2 * n]
    acc = None
    for g, r in zip(grads, rows):
        part = lax.dot_general(
            g[...], r[...], (((0,), (0,)), ((), ())), preferred_element_type=F32
        )
        acc = part if acc is None else acc + part
    out[...] = acc.astype(BF)


def design_grad(grads, rows, chunk=256):
    n = len(grads)
    cols, count = grads[0].shape
    width = rows[0].shape[1]
    return pl.pallas_call(
        functools.partial(design_grad_kernel, n),
        out_shape=jax.ShapeDtypeStruct((count, width), BF),
        grid=(count // chunk,),
        in_specs=[pl.BlockSpec((cols, chunk), lambda i: (0, i))] * n
        + [pl.BlockSpec((cols, width), lambda i: (0, 0))] * n,
        out_specs=pl.BlockSpec((chunk, width), lambda i: (i, 0)),
        compiler_params=PARAMS,
        name="design_grad",
    )(*grads, *rows)


def collect_kernel(n, cap, spot, *refs):
    parts = refs[:n]
    keep, give, acc = refs[n:]
    kept = keep.shape[0]
    acc[...] = jnp.zeros_like(acc)
    for i in range(n * cap):

        @pl.when(spot[i] >= 0)
        def _():
            s, k = i // cap, i % cap
            acc[spot[i]] += parts[s][k * TILE : (k + 1) * TILE, :].astype(F32)

    keep[...] = acc[:kept]
    give[...] = acc[kept:].astype(BF)


def collect(spot, parts, cap, kept):
    n = len(parts)
    width = parts[0].shape[1]
    shape = (kept, TILE, width)
    return pl.pallas_call(
        functools.partial(collect_kernel, n, cap),
        out_shape=[jax.ShapeDtypeStruct(shape, F32), jax.ShapeDtypeStruct(shape, BF)],
        grid_spec=pltpu.PrefetchScalarGridSpec(
            num_scalar_prefetch=1,
            grid=(1,),
            in_specs=[whole(parts[0].shape)] * n,
            out_specs=[whole(shape)] * 2,
            scratch_shapes=[pltpu.VMEM((2 * kept, TILE, width), F32)],
        ),
        compiler_params=PARAMS,
        name="collect",
    )(spot, *parts)


def after(x, *others):
    return lax.optimization_barrier((x,) + others)[0]


def body(designs, prototypes, candidates, positives):
    proto_count = lax.axis_size("proto")
    design_axis = lax.axis_size("design")
    half = proto_count // 2
    lanes = design_axis // 2
    cand_count = candidates.shape[1]
    width = designs.shape[1]
    count = designs.shape[0]
    blocks_dev = prototypes.shape[0] // TILE
    quarter = blocks_dev // design_axis
    cap = max(2, (4 * cand_count + 3 * proto_count - 1) // (3 * proto_count))
    parts = 2
    p = lax.axis_index("proto").astype(jnp.int32)
    d = lax.axis_index("design").astype(jnp.int32)
    q = p % half
    h = p // half
    y = d // 2
    c = d % 2
    shifts = list(range(half - 1, 0, -1))

    shard = prototypes.reshape(blocks_dev, TILE, width)
    mine = lax.dynamic_slice_in_dim(shard, d * quarter, quarter, axis=0).astype(BF)
    step = max(1, quarter // 2)
    mine = [mine[i : i + step] for i in range(0, quarter, step)]
    far_parts = [xor_proto(mine[0], half, proto_count)]

    wanted = request_table(candidates[0], blocks_dev, cap, proto_count)
    wanted = wanted.reshape(2, half, cap)
    wanted = jnp.stack([wanted[h], wanted[1 - h]], axis=1)
    asked = [lax.dynamic_index_in_dim(wanted, q ^ s, 0, keepdims=False) for s in range(half)]
    asking = {0: asked[0], **{s: xor_proto(asked[s], s, proto_count) for s in shifts}}
    wants = {s: jnp.maximum(asking[s], 0) for s in asking}
    for part in mine[1:]:
        far_parts.append(xor_proto(after(part, *wants.values()), half, proto_count))

    out_own = {s: gather_round(wants[s][0], shard) for s in shifts}
    own_rows = {s: xor_proto(out_own[s], s, proto_count) for s in shifts}
    own_rows[0] = gather_round(wants[0][0], shard)
    own_rows = [own_rows[s].reshape(cap * TILE, width) for s in range(half)]

    held = {}
    for i, part in enumerate(far_parts):
        part = after(part, *out_own.values())
        for ys in range(lanes):
            held[0, ys, i] = part if ys == 0 else xor_design(part, 2 * ys, design_axis)
        for ys in range(lanes):
            held[1, ys, i] = xor_design(held[0, ys, i], 1, design_axis)
    srcs = [held[k] for k in sorted(held)]

    def gather_other(ids):
        owner = ids // quarter
        which = ((owner % 2) ^ c) * lanes + ((owner // 2) ^ y)
        which = which * len(far_parts) + (ids % quarter) // step
        return gather_far(which, ids % step, srcs)

    out_far = {s: gather_other(wants[s][1]) for s in shifts}
    far_rows = {s: xor_proto(out_far[s], s, proto_count) for s in shifts}
    far_rows[0] = gather_other(wants[0][1])
    far_rows = [far_rows[s].reshape(cap * TILE, width) for s in range(half)]

    def bases(f):
        out = []
        for s in range(half):
            first = ((h if f == 0 else 1 - h) * half + (q ^ s)) * blocks_dev
            out.append(jnp.where(asked[s][f] >= 0, (first + asked[s][f]) * TILE, -(2**30)))
        return jnp.concatenate(out)

    pos = positives.reshape(1, count)
    own_base = bases(0)
    *logits, top, total, hit = own_logits(own_base, designs, pos, own_rows, cap)
    stats, far_g, far_tiles = far_grads(
        bases(1), designs, pos, (top, total, hit), far_rows, cap, parts
    )
    losses, top, inv = stats
    own_base = own_base.reshape(half, cap)
    own_g, own_tiles = [], []
    for s in range(half):
        g, t = own_grad(own_base[s], designs, pos, top, inv, logits[s], cap, parts)
        own_g.append(g)
        own_tiles.append(t)
    own_tiles = [[own_tiles[s][i] for s in range(half)] for i in range(parts)]

    kept = lanes * quarter

    def spots(f):
        table = jnp.concatenate([asking[s][f] for s in range(half)])
        owner = table // quarter
        at = ((owner // 2) ^ y) * quarter + table % quarter
        at = at + jnp.where(owner % 2 == c, 0, kept)
        return jnp.where(table >= 0, at, -1)

    def send_back(tiles):
        got = {s: xor_proto(tiles[s], s, proto_count) for s in shifts}
        return [tiles[0]] + [got[s] for s in range(1, half)]

    def reduce_shard(spot, tiles):
        keep, give = collect(spot, tiles, cap, kept)
        keep = keep + xor_design(give, 1, design_axis).astype(F32)
        keep = keep.reshape(lanes, quarter, TILE, keep.shape[-1])
        total = keep[0]
        for ys in range(1, lanes):
            total = total + xor_design(keep[ys].astype(BF), 2 * ys, design_axis).astype(F32)
        return total

    far_back = [send_back(t) for t in far_tiles]
    crossed = []
    for i in range(parts):
        far_total = reduce_shard(spots(1), far_back[i])
        crossed.append(xor_proto(far_total.astype(BF), half, proto_count))
    own_back = [
        send_back([after(t, *far_back[i][1:]) for t in own_tiles[i]]) for i in range(parts)
    ]
    dgrad = design_grad(own_g + list(far_g), own_rows + far_rows)
    result = []
    for i in range(parts):
        own_total = reduce_shard(spots(0), own_back[i])
        result.append(own_total + crossed[i].astype(F32))
    result = jnp.concatenate(result, axis=-1).reshape(quarter * TILE, width)
    return (losses.reshape(count), dgrad, result)


def solution(mesh):
    return jax.shard_map(
        body,
        mesh=mesh,
        in_specs=(
            P(("proto", "design"), None),
            P("proto", None),
            P(("proto", "design"), None),
            P(("proto", "design")),
        ),
        out_specs=(
            P(("proto", "design")),
            P(("proto", "design"), None),
            P(("proto", "design"), None),
        ),
        check_vma=False,
    )
```

```python
import functools

import jax
import jax.numpy as jnp
from jax import lax
from jax.experimental import pallas as pl
from jax.experimental.pallas import tpu as pltpu
from jax.sharding import PartitionSpec as P


D = 1024
TILE = 128
BF = jnp.bfloat16
F32 = jnp.float32
NEG = -1e30
PARTS = 2


def xor_proto(x, shift):
    count = lax.axis_size("proto")
    return lax.ppermute(x, "proto", [(i, i ^ shift) for i in range(count)])


def xor_design(x, shift):
    count = lax.axis_size("design")
    return lax.ppermute(x, "design", [(i, i ^ shift) for i in range(count)])


def request_table(block_list, blocks_dev, capacity, proto_count):
    owners = block_list // blocks_dev
    local_ids = block_list % blocks_dev
    ids = jnp.arange(block_list.shape[0], dtype=jnp.int32)
    earlier = (owners[:, None] == owners[None, :]) & (ids[None, :] < ids[:, None])
    rank_of = jnp.sum(earlier.astype(jnp.int32), axis=1)
    slot_of = owners * capacity + rank_of
    slots = jnp.arange(proto_count * capacity, dtype=jnp.int32)
    hit = slot_of[None, :] == slots[:, None]
    return jnp.sum(jnp.where(hit, local_ids[None, :] + 1, 0), axis=1) - 1


def whole(shape):
    return pl.BlockSpec(shape, lambda *_: (0,) * len(shape))


HBM = pl.BlockSpec(memory_space=pl.ANY)
PARAMS = pltpu.CompilerParams(vmem_limit_bytes=58 << 20)


def gather_round_kernel(tbl, src, *refs):
    outs, buf, sems = refs[:-2], refs[-2], refs[-1]
    cap = outs[0].shape[0]
    copies = [
        pltpu.make_async_copy(src.at[tbl[i]], buf.at[i], sems.at[i])
        for i in range(len(outs) * cap)
    ]
    for copy in copies:
        copy.start()
    for i, copy in enumerate(copies):
        copy.wait()
        outs[i // cap][i % cap] = buf[i].astype(BF)


def gather_round(tables, shard):
    n = len(tables)
    cap = tables[0].shape[0]
    shape = (cap,) + shard.shape[1:]
    return pl.pallas_call(
        gather_round_kernel,
        out_shape=[jax.ShapeDtypeStruct(shape, BF)] * n,
        grid_spec=pltpu.PrefetchScalarGridSpec(
            num_scalar_prefetch=1,
            grid=(1,),
            in_specs=[HBM],
            out_specs=[whole(shape)] * n,
            scratch_shapes=[
                pltpu.VMEM((n * cap,) + shard.shape[1:], F32),
                pltpu.SemaphoreType.DMA((n * cap,)),
            ],
        ),
        compiler_params=PARAMS,
        name="gather_round",
    )(jnp.concatenate(tables), shard)


def gather_far_kernel(n_src, n_out, which, where, *refs):
    srcs, outs, sems = refs[:n_src], refs[n_src : n_src + n_out], refs[n_src + n_out]
    cap = outs[0].shape[0]
    for i in range(n_out * cap):
        for a in range(n_src):

            @pl.when(which[i] == a)
            def _():
                pltpu.make_async_copy(
                    srcs[a].at[where[i]], outs[i // cap].at[i % cap], sems.at[i]
                ).start()

    for i in range(n_out * cap):
        pltpu.make_async_copy(srcs[0].at[0], outs[i // cap].at[i % cap], sems.at[i]).wait()


def gather_far(which, where, srcs, cap):
    n = which.shape[0] // cap
    shape = (cap,) + srcs[0].shape[1:]
    return pl.pallas_call(
        functools.partial(gather_far_kernel, len(srcs), n),
        out_shape=[jax.ShapeDtypeStruct(shape, BF)] * n,
        grid_spec=pltpu.PrefetchScalarGridSpec(
            num_scalar_prefetch=2,
            grid=(1,),
            in_specs=[HBM] * len(srcs),
            out_specs=[whole(shape)] * n,
            scratch_shapes=[pltpu.SemaphoreType.DMA((n * cap,))],
        ),
        compiler_params=PARAMS,
        name="gather_far",
    )(which, where, *srcs)


EXP_SCALE = (D ** (-0.5)) * 1.4426950408889634


def fold(tile, op):
    return op(tile.reshape(tile.shape[0] // 8, 8, tile.shape[1]), axis=0)


def slot_stats(base, rel, slots):
    top = None
    hit = None
    for n, ref in slots:
        piece = ref[...]
        target = rel == base[n]
        found = fold(jnp.where(target, piece, 0.0), jnp.sum)
        piece = piece + jnp.where(base[n] < 0, NEG, 0.0)
        high = fold(piece, jnp.max)
        top = high if top is None else jnp.maximum(top, high)
        hit = found if hit is None else hit + found
    return jnp.max(top, axis=0, keepdims=True), jnp.sum(hit, axis=0, keepdims=True)


def slot_power(base, n, ref, top):
    piece = ref[...] + jnp.where(base[n] < 0, NEG, 0.0)
    return jnp.exp2((piece - top) * EXP_SCALE)


def relative(pos, lanes):
    line = lax.broadcasted_iota(jnp.int32, (TILE, lanes), 0)
    return pos - line


def own_kernel(group, cap, lanes, base, x, pos, *refs):
    rows = refs[:group]
    logits = refs[group : 2 * group]
    top_out, sum_out, hit_out = refs[2 * group :]
    count = x.shape[0]
    for j in range(0, count, lanes):
        xs = x[j : j + lanes, :]
        at = pl.ds(j, lanes)
        for s in range(group):
            logits[s][:, at] = lax.dot_general(
                rows[s][...], xs, (((1,), (1,)), ((), ())), preferred_element_type=F32
            )
        slots = [
            (s * cap + k, logits[s].at[pl.ds(k * TILE, TILE), at])
            for s in range(group)
            for k in range(cap)
        ]
        top, hit = slot_stats(base, relative(pos[:, at], lanes), slots)
        total = None
        for n, ref in slots:
            part = fold(slot_power(base, n, ref, top), jnp.sum)
            total = part if total is None else total + part
        top_out[:, at] = top
        hit_out[:, at] = hit
        sum_out[:, at] = jnp.sum(total, axis=0, keepdims=True)


def own_logits(base, x, pos, rows, cap, lanes=256):
    group = len(rows)
    count = x.shape[0]
    line = (1, count)
    shape = (rows[0].shape[0], count)
    return pl.pallas_call(
        functools.partial(own_kernel, group, cap, lanes),
        out_shape=[jax.ShapeDtypeStruct(shape, F32)] * group
        + [jax.ShapeDtypeStruct(line, F32)] * 3,
        grid_spec=pltpu.PrefetchScalarGridSpec(
            num_scalar_prefetch=1,
            grid=(1,),
            in_specs=[whole(x.shape), whole(line)] + [whole(rows[0].shape)] * group,
            out_specs=[whole(shape)] * group + [whole(line)] * 3,
        ),
        compiler_params=PARAMS,
        name="own_logits",
    )(base, x, pos, *rows)


def far_kernel(group, cap, lanes, parts, base, x, pos, top_own, sum_own, hit_own, *refs):
    rows = refs[:group]
    losses, top_out, inv_out = refs[group : group + 3]
    grads = refs[group + 3 : 2 * group + 3]
    tiles = refs[2 * group + 3 : -1]
    logits = refs[-1]
    count, width = x.shape
    scale = D ** (-0.5)
    for j in range(0, count, lanes):
        turn = (j // lanes) % 2
        xs = x[j : j + lanes, :]
        at = pl.ds(j, lanes)
        for s in range(group):
            logits[turn, s * cap * TILE : (s + 1) * cap * TILE, :] = lax.dot_general(
                rows[s][...], xs, (((1,), (1,)), ((), ())), preferred_element_type=F32
            )
        slots = [
            (n, logits.at[turn, pl.ds(n * TILE, TILE), :]) for n in range(group * cap)
        ]
        rel = relative(pos[:, at], lanes)
        top, hit = slot_stats(base, rel, slots)
        mine = top_own[:, at]
        both = jnp.maximum(top, mine)
        total = None
        for n, ref in slots:
            power = slot_power(base, n, ref, both)
            ref[...] = power
            part = fold(power, jnp.sum)
            total = part if total is None else total + part
        total = jnp.sum(total, axis=0, keepdims=True)
        total = total + sum_own[:, at] * jnp.exp2((mine - both) * EXP_SCALE)
        losses[:, at] = both * scale + jnp.log(total) - (hit + hit_own[:, at]) * scale
        inv = 1.0 / total
        top_out[:, at] = both
        inv_out[:, at] = inv
        for n, ref in slots:
            s, k = n // cap, n % cap
            target = jnp.where(rel == base[n], 1.0, 0.0)
            grads[s][k * TILE : (k + 1) * TILE, at] = (ref[...] * inv - target).astype(BF)
    step = width // parts
    for i in range(parts):
        for s in range(group):
            tiles[i * group + s][...] = jnp.dot(
                grads[s][...], x[:, i * step : (i + 1) * step], preferred_element_type=F32
            ).astype(BF)


def far_grads(base, x, pos, stats, rows, cap, parts, lanes=256):
    group = len(rows)
    count, width = x.shape
    line = (1, count)
    size = rows[0].shape[0]
    outs = [((1, count), F32)] * 3 + [((size, count), BF)] * group
    outs += [((size, width // parts), BF)] * (group * parts)
    got = pl.pallas_call(
        functools.partial(far_kernel, group, cap, lanes, parts),
        out_shape=[jax.ShapeDtypeStruct(*o) for o in outs],
        grid_spec=pltpu.PrefetchScalarGridSpec(
            num_scalar_prefetch=1,
            grid=(1,),
            in_specs=[whole(x.shape)] + [whole(line)] * 4 + [whole(rows[0].shape)] * group,
            out_specs=[whole(o[0]) for o in outs],
            scratch_shapes=[pltpu.VMEM((2, group * size, lanes), F32)],
        ),
        compiler_params=PARAMS,
        name="far_grads",
    )(base, x, pos, *stats, *rows)
    tiles = got[3 + group :]
    return got[:3], got[3 : 3 + group], [tiles[i * group : (i + 1) * group] for i in range(parts)]


def own_grad_kernel(cap, parts, base, x, pos, top, inv, logits, grad, *tiles):
    count, width = x.shape
    rel = relative(pos[...], count)
    for k in range(cap):
        ref = logits.at[pl.ds(k * TILE, TILE), :]
        power = slot_power(base, k, ref, top[...])
        target = jnp.where(rel == base[k], 1.0, 0.0)
        grad[k * TILE : (k + 1) * TILE, :] = (power * inv[...] - target).astype(BF)
    step = width // parts
    for i in range(parts):
        tiles[i][...] = jnp.dot(
            grad[...], x[:, i * step : (i + 1) * step], preferred_element_type=F32
        ).astype(BF)


def own_grad(base, x, pos, top, inv, logits, cap, parts):
    count, width = x.shape
    line = (1, count)
    size = logits.shape[0]
    outs = [((size, count), BF)] + [((size, width // parts), BF)] * parts
    got = pl.pallas_call(
        functools.partial(own_grad_kernel, cap, parts),
        out_shape=[jax.ShapeDtypeStruct(*o) for o in outs],
        grid_spec=pltpu.PrefetchScalarGridSpec(
            num_scalar_prefetch=1,
            grid=(1,),
            in_specs=[whole(x.shape)] + [whole(line)] * 3 + [whole(logits.shape)],
            out_specs=[whole(o[0]) for o in outs],
        ),
        compiler_params=PARAMS,
        name="own_grad",
    )(base, x, pos, top, inv, logits)
    return got[0], got[1:]


def design_grad_kernel(n, *refs):
    grads, rows, out = refs[:n], refs[n : 2 * n], refs[2 * n]
    acc = None
    for g, r in zip(grads, rows):
        part = lax.dot_general(
            g[...], r[...], (((0,), (0,)), ((), ())), preferred_element_type=F32
        )
        acc = part if acc is None else acc + part
    out[...] = acc.astype(BF)


def design_grad(grads, rows, chunk=256):
    n = len(grads)
    cols, count = grads[0].shape
    width = rows[0].shape[1]
    return pl.pallas_call(
        functools.partial(design_grad_kernel, n),
        out_shape=jax.ShapeDtypeStruct((count, width), BF),
        grid=(count // chunk,),
        in_specs=[pl.BlockSpec((cols, chunk), lambda i: (0, i))] * n
        + [pl.BlockSpec((cols, width), lambda i: (0, 0))] * n,
        out_specs=pl.BlockSpec((chunk, width), lambda i: (i, 0)),
        compiler_params=PARAMS,
        name="design_grad",
    )(*grads, *rows)


def collect_kernel(n, cap, spot, *refs):
    parts = refs[:n]
    keep, give, acc = refs[n:]
    kept = keep.shape[0]
    acc[...] = jnp.zeros_like(acc)
    for i in range(n * cap):

        @pl.when(spot[i] >= 0)
        def _():
            s, k = i // cap, i % cap
            acc[spot[i]] += parts[s][k * TILE : (k + 1) * TILE, :].astype(F32)

    keep[...] = acc[:kept]
    give[...] = acc[kept:].astype(BF)


def collect(spot, parts, cap, kept):
    n = len(parts)
    width = parts[0].shape[1]
    shape = (kept, TILE, width)
    return pl.pallas_call(
        functools.partial(collect_kernel, n, cap),
        out_shape=[jax.ShapeDtypeStruct(shape, F32), jax.ShapeDtypeStruct(shape, BF)],
        grid_spec=pltpu.PrefetchScalarGridSpec(
            num_scalar_prefetch=1,
            grid=(1,),
            in_specs=[whole(parts[0].shape)] * n,
            out_specs=[whole(shape)] * 2,
            scratch_shapes=[pltpu.VMEM((2 * kept, TILE, width), F32)],
        ),
        compiler_params=PARAMS,
        name="collect",
    )(spot, *parts)


def body(designs, prototypes, candidates, positives):
    proto_count = lax.axis_size("proto")
    design_axis = lax.axis_size("design")
    half = proto_count // 2
    lanes = design_axis // 2
    cand_count = candidates.shape[1]
    width = designs.shape[1]
    count = designs.shape[0]
    blocks_dev = prototypes.shape[0] // TILE
    quarter = blocks_dev // design_axis
    cap = max(2, (4 * cand_count + 3 * proto_count - 1) // (3 * proto_count))
    parts = PARTS
    p = lax.axis_index("proto").astype(jnp.int32)
    d = lax.axis_index("design").astype(jnp.int32)
    q = p % half
    h = p // half
    y = d // 2
    c = d % 2
    shifts = list(range(half - 1, 0, -1))

    shard = prototypes.reshape(blocks_dev, TILE, width)
    mine = lax.dynamic_slice_in_dim(shard, d * quarter, quarter, axis=0).astype(BF)
    last = quarter - 1
    far_parts = [xor_proto(mine[:last], half), xor_proto(mine[last:], half)]

    wanted = request_table(candidates[0], blocks_dev, cap, proto_count)
    wanted = wanted.reshape(2, half, cap)
    wanted = jnp.stack([wanted[h], wanted[1 - h]], axis=1)
    asked = [lax.dynamic_index_in_dim(wanted, q ^ s, 0, keepdims=False) for s in range(half)]
    asking = {0: asked[0], **{s: xor_proto(asked[s], s) for s in shifts}}
    wants = {s: jnp.maximum(asking[s], 0) for s in asking}

    out_own = gather_round([wants[s][0] for s in shifts], shard)
    own_rows = {s: xor_proto(o, s) for s, o in zip(shifts, out_own)}
    (own_rows[0],) = gather_round([wants[0][0]], shard)
    own_rows = [own_rows[s].reshape(cap * TILE, width) for s in range(half)]

    held = {}
    for i, part in enumerate(far_parts):
        held[0, 0, i] = part
        for ys in range(1, lanes):
            held[0, ys, i] = xor_design(part, 2 * ys)
        for ys in range(lanes):
            held[1, ys, i] = xor_design(held[0, ys, i], 1)
    srcs = [held[k] for k in sorted(held)]

    def gather_other(tables):
        ids = jnp.concatenate(tables)
        owner = ids // quarter
        which = ((owner % 2) ^ c) * lanes + ((owner // 2) ^ y)
        inside = ids % quarter
        tail = (inside == last).astype(jnp.int32)
        return gather_far(which * 2 + tail, jnp.where(tail > 0, 0, inside), srcs, cap)

    out_far = gather_other([wants[s][1] for s in shifts])
    far_rows = {s: xor_proto(o, s) for s, o in zip(shifts, out_far)}
    (far_rows[0],) = gather_other([wants[0][1]])
    far_rows = [far_rows[s].reshape(cap * TILE, width) for s in range(half)]

    def bases(f):
        out = []
        for s in range(half):
            first = ((h if f == 0 else 1 - h) * half + (q ^ s)) * blocks_dev
            out.append(jnp.where(asked[s][f] >= 0, (first + asked[s][f]) * TILE, -(2**30)))
        return jnp.concatenate(out)

    pos = positives.reshape(1, count)
    own_base = bases(0)
    *logits, top, total, hit = own_logits(own_base, designs, pos, own_rows, cap)
    stats, far_g, far_tiles = far_grads(
        bases(1), designs, pos, (top, total, hit), far_rows, cap, parts
    )
    losses, top, inv = stats
    own_base = own_base.reshape(half, cap)
    own_g, own_tiles = [], []
    for s in range(half):
        g, t = own_grad(own_base[s], designs, pos, top, inv, logits[s], cap, parts)
        own_g.append(g)
        own_tiles.append(t)
    own_tiles = [[own_tiles[s][i] for s in range(half)] for i in range(parts)]

    kept = lanes * quarter

    def spots(f):
        table = jnp.concatenate([asking[s][f] for s in range(half)])
        owner = table // quarter
        at = ((owner // 2) ^ y) * quarter + table % quarter
        at = at + jnp.where(owner % 2 == c, 0, kept)
        return jnp.where(table >= 0, at, -1)

    def send_back(tiles):
        got = {s: xor_proto(tiles[s], s) for s in shifts}
        return [tiles[0]] + [got[s] for s in range(1, half)]

    def reduce_shard(spot, tiles):
        keep, give = collect(spot, tiles, cap, kept)
        keep = keep + xor_design(give, 1).astype(F32)
        keep = keep.reshape(lanes, quarter, TILE, keep.shape[-1])
        total = keep[0]
        for ys in range(1, lanes):
            back = xor_design(keep[ys].astype(BF), 2 * ys)
            total = total + back.astype(F32)
        return total

    crossed, result = [], []
    for i in range(parts):
        back = send_back(far_tiles[i])
        far_total = reduce_shard(spots(1), back)
        crossed.append(xor_proto(far_total.astype(BF), half))
    dgrad = design_grad(own_g + list(far_g), own_rows + far_rows)
    for i in range(parts):
        back = send_back(own_tiles[i])
        own_total = reduce_shard(spots(0), back)
        result.append(own_total + crossed[i].astype(F32))
    result = jnp.concatenate(result, axis=-1).reshape(quarter * TILE, width)
    return (losses.reshape(count), dgrad, result)


def solution(mesh):
    return jax.shard_map(
        body,
        mesh=mesh,
        in_specs=(
            P(("proto", "design"), None),
            P("proto", None),
            P(("proto", "design"), None),
            P(("proto", "design")),
        ),
        out_specs=(
            P(("proto", "design")),
            P(("proto", "design"), None),
            P(("proto", "design"), None),
        ),
        check_vma=False,
    )
```

```python
import functools

import jax
import jax.numpy as jnp
from jax import lax
from jax.experimental import pallas as pl
from jax.experimental.pallas import tpu as pltpu
from jax.sharding import PartitionSpec as P


D = 1024
TILE = 128
BF = jnp.bfloat16
F32 = jnp.float32
NEG = -1e30
PARTS = 2


def xor_proto(x, shift):
    count = lax.axis_size("proto")
    return lax.ppermute(x, "proto", [(i, i ^ shift) for i in range(count)])


def xor_design(x, shift):
    count = lax.axis_size("design")
    return lax.ppermute(x, "design", [(i, i ^ shift) for i in range(count)])


def request_table(block_list, blocks_dev, capacity, proto_count):
    owners = block_list // blocks_dev
    local_ids = block_list % blocks_dev
    ids = jnp.arange(block_list.shape[0], dtype=jnp.int32)
    earlier = (owners[:, None] == owners[None, :]) & (ids[None, :] < ids[:, None])
    rank_of = jnp.sum(earlier.astype(jnp.int32), axis=1)
    slot_of = owners * capacity + rank_of
    slots = jnp.arange(proto_count * capacity, dtype=jnp.int32)
    hit = slot_of[None, :] == slots[:, None]
    return jnp.sum(jnp.where(hit, local_ids[None, :] + 1, 0), axis=1) - 1


HBM = pl.BlockSpec(memory_space=pl.ANY)
VM = pl.BlockSpec(memory_space=pltpu.VMEM)
SM = pl.BlockSpec(memory_space=pltpu.SMEM)
WIDE = pltpu.CompilerParams(vmem_limit_bytes=40 << 20)
PARAMS = pltpu.CompilerParams(vmem_limit_bytes=16 << 20)


def gather_round_kernel(n, *refs):
    tables, src, outs, buf, sems = refs[:n], refs[n], refs[n + 1 : -2], refs[-2], refs[-1]
    cap = outs[0].shape[0]
    copies = []
    for i in range(n * cap):
        row = jnp.maximum(tables[i // cap][0, i % cap], 0)
        copies.append(pltpu.make_async_copy(src.at[row], buf.at[i], sems.at[i]))
    for copy in copies:
        copy.start()
    for i, copy in enumerate(copies):
        copy.wait()
        outs[i // cap][i % cap] = buf[i].astype(BF)


def gather_round(tables, shard):
    n = len(tables)
    cap = tables[0].shape[1]
    shape = (cap,) + shard.shape[1:]
    return pl.pallas_call(
        functools.partial(gather_round_kernel, n),
        out_shape=[jax.ShapeDtypeStruct(shape, BF)] * n,
        in_specs=[SM] * n + [HBM],
        out_specs=[VM] * n,
        scratch_shapes=[
            pltpu.VMEM((n * cap,) + shard.shape[1:], F32),
            pltpu.SemaphoreType.DMA((n * cap,)),
        ],
        compiler_params=PARAMS,
        name="gather_round",
    )(*tables, shard)


def gather_far_kernel(n_src, n_out, quarter, lanes, me, *refs):
    tables, srcs = refs[:n_out], refs[n_out : n_out + n_src]
    outs, sems = refs[n_out + n_src : -1], refs[-1]
    cap = outs[0].shape[0]
    last = quarter - 1
    y, c = me[0] // 2, me[0] % 2
    for i in range(n_out * cap):
        row = jnp.maximum(tables[i // cap][1, i % cap], 0)
        owner, inside = row // quarter, row % quarter
        tail = (inside == last).astype(jnp.int32)
        which = (((owner % 2) ^ c) * lanes + ((owner // 2) ^ y)) * 2 + tail
        where = jnp.where(tail > 0, 0, inside)
        for a in range(n_src):

            @pl.when(which == a)
            def _():
                at = where if a % 2 == 0 else 0
                pltpu.make_async_copy(
                    srcs[a].at[at], outs[i // cap].at[i % cap], sems.at[i]
                ).start()

    for i in range(n_out * cap):
        pltpu.make_async_copy(srcs[0].at[0], outs[i // cap].at[i % cap], sems.at[i]).wait()


def gather_far(me, tables, srcs, quarter, lanes):
    n = len(tables)
    cap = tables[0].shape[1]
    shape = (cap,) + srcs[0].shape[1:]
    return pl.pallas_call(
        functools.partial(gather_far_kernel, len(srcs), n, quarter, lanes),
        out_shape=[jax.ShapeDtypeStruct(shape, BF)] * n,
        in_specs=[SM] * (n + 1) + [HBM] * len(srcs),
        out_specs=[VM] * n,
        scratch_shapes=[pltpu.SemaphoreType.DMA((n * cap,))],
        compiler_params=PARAMS,
        name="gather_far",
    )(me, *tables, *srcs)


EXP_SCALE = (D ** (-0.5)) * 1.4426950408889634


def fold(tile, op):
    return op(tile.reshape(tile.shape[0] // 8, 8, tile.shape[1]), axis=0)


def slot_stats(base, rel, slots):
    top = None
    hit = None
    for n, ref in slots:
        piece = ref[...]
        target = rel == base[n]
        found = fold(jnp.where(target, piece, 0.0), jnp.sum)
        piece = piece + jnp.where(base[n] < 0, NEG, 0.0)
        high = fold(piece, jnp.max)
        top = high if top is None else jnp.maximum(top, high)
        hit = found if hit is None else hit + found
    return jnp.max(top, axis=0, keepdims=True), jnp.sum(hit, axis=0, keepdims=True)


def slot_power(base, n, ref, top):
    piece = ref[...] + jnp.where(base[n] < 0, NEG, 0.0)
    return jnp.exp2((piece - top) * EXP_SCALE)


def relative(pos, lanes):
    line = lax.broadcasted_iota(jnp.int32, (TILE, lanes), 0)
    return pos - line


def own_kernel(group, cap, lanes, base, x, pos, *refs):
    rows = refs[:group]
    logits = refs[group : 2 * group]
    top_out, sum_out, hit_out = refs[2 * group :]
    count = x.shape[0]
    for j in range(0, count, lanes):
        xs = x[j : j + lanes, :]
        at = pl.ds(j, lanes)
        for s in range(group):
            logits[s][:, at] = lax.dot_general(
                rows[s][...], xs, (((1,), (1,)), ((), ())), preferred_element_type=F32
            )
        slots = [
            (s * cap + k, logits[s].at[pl.ds(k * TILE, TILE), at])
            for s in range(group)
            for k in range(cap)
        ]
        top, hit = slot_stats(base, relative(pos[:, at], lanes), slots)
        total = None
        for n, ref in slots:
            part = fold(slot_power(base, n, ref, top), jnp.sum)
            total = part if total is None else total + part
        top_out[:, at] = top
        hit_out[:, at] = hit
        sum_out[:, at] = jnp.sum(total, axis=0, keepdims=True)


def own_logits(base, x, pos, rows, cap, lanes=256):
    group = len(rows)
    count = x.shape[0]
    line = (1, count)
    shape = (rows[0].shape[0], count)
    return pl.pallas_call(
        functools.partial(own_kernel, group, cap, lanes),
        out_shape=[jax.ShapeDtypeStruct(shape, F32)] * group
        + [jax.ShapeDtypeStruct(line, F32)] * 3,
        in_specs=[SM] + [VM] * (2 + group),
        out_specs=[VM] * (group + 3),
        compiler_params=PARAMS,
        name="own_logits",
    )(base, x, pos, *rows)


def far_kernel(group, cap, lanes, parts, base, x, pos, top_own, sum_own, hit_own, *refs):
    rows = refs[:group]
    losses, top_out, inv_out = refs[group : group + 3]
    grads = refs[group + 3 : 2 * group + 3]
    tiles = refs[2 * group + 3 : -1]
    logits = refs[-1]
    count, width = x.shape
    scale = D ** (-0.5)
    for j in range(0, count, lanes):
        turn = (j // lanes) % 2
        xs = x[j : j + lanes, :]
        at = pl.ds(j, lanes)
        for s in range(group):
            logits[turn, s * cap * TILE : (s + 1) * cap * TILE, :] = lax.dot_general(
                rows[s][...], xs, (((1,), (1,)), ((), ())), preferred_element_type=F32
            )
        slots = [
            (n, logits.at[turn, pl.ds(n * TILE, TILE), :]) for n in range(group * cap)
        ]
        rel = relative(pos[:, at], lanes)
        top, hit = slot_stats(base, rel, slots)
        mine = top_own[:, at]
        both = jnp.maximum(top, mine)
        total = None
        for n, ref in slots:
            power = slot_power(base, n, ref, both)
            ref[...] = power
            part = fold(power, jnp.sum)
            total = part if total is None else total + part
        total = jnp.sum(total, axis=0, keepdims=True)
        total = total + sum_own[:, at] * jnp.exp2((mine - both) * EXP_SCALE)
        losses[:, at] = both * scale + jnp.log(total) - (hit + hit_own[:, at]) * scale
        inv = 1.0 / total
        top_out[:, at] = both
        inv_out[:, at] = inv
        for n, ref in slots:
            s, k = n // cap, n % cap
            target = jnp.where(rel == base[n], 1.0, 0.0)
            grads[s][k * TILE : (k + 1) * TILE, at] = (ref[...] * inv - target).astype(BF)
    step = width // parts
    for i in range(parts):
        for s in range(group):
            tiles[i * group + s][...] = jnp.dot(
                grads[s][...], x[:, i * step : (i + 1) * step], preferred_element_type=F32
            ).astype(BF)


def far_grads(base, x, pos, stats, rows, cap, parts, lanes=256):
    group = len(rows)
    count, width = x.shape
    size = rows[0].shape[0]
    outs = [((1, count), F32)] * 3 + [((size, count), BF)] * group
    outs += [((size, width // parts), BF)] * (group * parts)
    got = pl.pallas_call(
        functools.partial(far_kernel, group, cap, lanes, parts),
        out_shape=[jax.ShapeDtypeStruct(*o) for o in outs],
        in_specs=[SM] + [VM] * (5 + group),
        out_specs=[VM] * len(outs),
        scratch_shapes=[pltpu.VMEM((2, group * size, lanes), F32)],
        compiler_params=PARAMS,
        name="far_grads",
    )(base, x, pos, *stats, *rows)
    tiles = got[3 + group :]
    return got[:3], got[3 : 3 + group], [tiles[i * group : (i + 1) * group] for i in range(parts)]


def own_grad_kernel(cap, parts, base, x, pos, top, inv, logits, grad, *tiles):
    count, width = x.shape
    rel = relative(pos[...], count)
    for k in range(cap):
        ref = logits.at[pl.ds(k * TILE, TILE), :]
        power = slot_power(base, k, ref, top[...])
        target = jnp.where(rel == base[k], 1.0, 0.0)
        grad[k * TILE : (k + 1) * TILE, :] = (power * inv[...] - target).astype(BF)
    step = width // parts
    for i in range(parts):
        tiles[i][...] = jnp.dot(
            grad[...], x[:, i * step : (i + 1) * step], preferred_element_type=F32
        ).astype(BF)


def own_grad(base, x, pos, top, inv, logits, cap, parts):
    count, width = x.shape
    size = logits.shape[0]
    outs = [((size, count), BF)] + [((size, width // parts), BF)] * parts
    got = pl.pallas_call(
        functools.partial(own_grad_kernel, cap, parts),
        out_shape=[jax.ShapeDtypeStruct(*o) for o in outs],
        in_specs=[SM] + [VM] * 5,
        out_specs=[VM] * len(outs),
        compiler_params=PARAMS,
        name="own_grad",
    )(base, x, pos, top, inv, logits)
    return got[0], got[1:]


def design_grad_kernel(n, *refs):
    grads, rows, out = refs[:n], refs[n : 2 * n], refs[2 * n]
    acc = None
    for g, r in zip(grads, rows):
        part = lax.dot_general(
            g[...], r[...], (((0,), (0,)), ((), ())), preferred_element_type=F32
        )
        acc = part if acc is None else acc + part
    out[...] = acc.astype(BF)


def design_grad(grads, rows, chunk=256):
    n = len(grads)
    cols, count = grads[0].shape
    width = rows[0].shape[1]
    return pl.pallas_call(
        functools.partial(design_grad_kernel, n),
        out_shape=jax.ShapeDtypeStruct((count, width), BF),
        grid=(count // chunk,),
        in_specs=[pl.BlockSpec((cols, chunk), lambda i: (0, i))] * n
        + [pl.BlockSpec((cols, width), lambda i: (0, 0))] * n,
        out_specs=pl.BlockSpec((chunk, width), lambda i: (i, 0)),
        compiler_params=WIDE,
        name="design_grad",
    )(*grads, *rows)


def collect_kernel(n, cap, spot, *refs):
    parts = refs[:n]
    keep, give, acc = refs[n:]
    kept = keep.shape[0]
    acc[...] = jnp.zeros_like(acc)
    for i in range(n * cap):

        @pl.when(spot[i] >= 0)
        def _():
            s, k = i // cap, i % cap
            acc[spot[i]] += parts[s][k * TILE : (k + 1) * TILE, :].astype(F32)

    keep[...] = acc[:kept]
    give[...] = acc[kept:].astype(BF)


def collect(spot, parts, cap, kept):
    n = len(parts)
    width = parts[0].shape[1]
    shape = (kept, TILE, width)
    return pl.pallas_call(
        functools.partial(collect_kernel, n, cap),
        out_shape=[jax.ShapeDtypeStruct(shape, F32), jax.ShapeDtypeStruct(shape, BF)],
        in_specs=[SM] + [VM] * n,
        out_specs=[VM] * 2,
        scratch_shapes=[pltpu.VMEM((2 * kept, TILE, width), F32)],
        compiler_params=PARAMS,
        name="collect",
    )(spot, *parts)


def body(designs, prototypes, candidates, positives):
    proto_count = lax.axis_size("proto")
    design_axis = lax.axis_size("design")
    half = proto_count // 2
    lanes = design_axis // 2
    cand_count = candidates.shape[1]
    width = designs.shape[1]
    count = designs.shape[0]
    blocks_dev = prototypes.shape[0] // TILE
    quarter = blocks_dev // design_axis
    cap = max(2, (4 * cand_count + 3 * proto_count - 1) // (3 * proto_count))
    parts = PARTS
    p = lax.axis_index("proto").astype(jnp.int32)
    d = lax.axis_index("design").astype(jnp.int32)
    q = p % half
    h = p // half
    y = d // 2
    c = d % 2
    shifts = list(range(half - 1, 0, -1))

    shard = prototypes.reshape(blocks_dev, TILE, width)
    mine = lax.dynamic_slice_in_dim(shard, d * quarter, quarter, axis=0).astype(BF)
    last = quarter - 1
    wanted = request_table(candidates[0], blocks_dev, cap, proto_count)
    wanted = wanted.reshape(2, half, cap)
    wanted = jnp.stack([wanted[h], wanted[1 - h]], axis=1)
    asked = [lax.dynamic_index_in_dim(wanted, q ^ s, 0, keepdims=False) for s in range(half)]
    asking = {0: asked[0], **{s: xor_proto(asked[s], s) for s in shifts}}
    far_parts = [xor_proto(mine[:last], half), xor_proto(mine[last:], half)]

    out_own = gather_round([asking[s] for s in shifts], shard)
    own_rows = {s: xor_proto(o, s) for s, o in zip(shifts, out_own)}
    (own_rows[0],) = gather_round([asking[0]], shard)
    own_rows = [own_rows[s].reshape(cap * TILE, width) for s in range(half)]

    held = {}
    for i, part in enumerate(far_parts):
        held[0, 0, i] = part
        for ys in range(1, lanes):
            held[0, ys, i] = xor_design(part, 2 * ys)
        for ys in range(lanes):
            held[1, ys, i] = xor_design(held[0, ys, i], 1)
    srcs = [held[k] for k in sorted(held)]

    me = d.reshape(1)
    out_far = gather_far(me, [asking[s] for s in shifts], srcs, quarter, lanes)
    far_rows = {s: xor_proto(o, s) for s, o in zip(shifts, out_far)}
    (far_rows[0],) = gather_far(me, [asking[0]], srcs, quarter, lanes)
    far_rows = [far_rows[s].reshape(cap * TILE, width) for s in range(half)]

    def bases(f):
        out = []
        for s in range(half):
            first = ((h if f == 0 else 1 - h) * half + (q ^ s)) * blocks_dev
            out.append(jnp.where(asked[s][f] >= 0, (first + asked[s][f]) * TILE, -(2**30)))
        return jnp.concatenate(out)

    pos = positives.reshape(1, count)
    own_base = bases(0)
    *logits, top, total, hit = own_logits(own_base, designs, pos, own_rows, cap)
    stats, far_g, far_tiles = far_grads(
        bases(1), designs, pos, (top, total, hit), far_rows, cap, parts
    )
    losses, top, inv = stats
    own_base = own_base.reshape(half, cap)
    own_g, own_tiles = [], []
    for s in range(half):
        g, t = own_grad(own_base[s], designs, pos, top, inv, logits[s], cap, parts)
        own_g.append(g)
        own_tiles.append(t)
    own_tiles = [[own_tiles[s][i] for s in range(half)] for i in range(parts)]

    kept = lanes * quarter

    def spots(f):
        table = jnp.concatenate([asking[s][f] for s in range(half)])
        owner = table // quarter
        at = ((owner // 2) ^ y) * quarter + table % quarter
        at = at + jnp.where(owner % 2 == c, 0, kept)
        return jnp.where(table >= 0, at, -1)

    def send_back(tiles):
        got = {s: xor_proto(tiles[s], s) for s in shifts}
        return [tiles[0]] + [got[s] for s in range(1, half)]

    def reduce_shard(spot, tiles):
        keep, give = collect(spot, tiles, cap, kept)
        keep = keep + xor_design(give, 1).astype(F32)
        keep = keep.reshape(lanes, quarter, TILE, keep.shape[-1])
        total = keep[0]
        for ys in range(1, lanes):
            back = xor_design(keep[ys].astype(BF), 2 * ys)
            total = total + back.astype(F32)
        return total

    crossed, result = [], []
    for i in range(parts):
        back = send_back(far_tiles[i])
        far_total = reduce_shard(spots(1), back)
        crossed.append(xor_proto(far_total.astype(BF), half))
    dgrad = design_grad(own_g + list(far_g), own_rows + far_rows)
    for i in range(parts):
        back = send_back(own_tiles[i])
        own_total = reduce_shard(spots(0), back)
        result.append(own_total + crossed[i].astype(F32))
    result = jnp.concatenate(result, axis=-1).reshape(quarter * TILE, width)
    return (losses.reshape(count), dgrad, result)


def solution(mesh):
    return jax.shard_map(
        body,
        mesh=mesh,
        in_specs=(
            P(("proto", "design"), None),
            P("proto", None),
            P(("proto", "design"), None),
            P(("proto", "design")),
        ),
        out_specs=(
            P(("proto", "design")),
            P(("proto", "design"), None),
            P(("proto", "design"), None),
        ),
        check_vma=False,
    )
```

```python
import functools

import jax
import jax.numpy as jnp
from jax import lax
from jax.experimental import pallas as pl
from jax.experimental.pallas import tpu as pltpu
from jax.sharding import PartitionSpec as P


D = 1024
TILE = 128
BF = jnp.bfloat16
F32 = jnp.float32
NEG = -1e30
PARTS = 2


def xor_proto(x, shift):
    count = lax.axis_size("proto")
    return lax.ppermute(x, "proto", [(i, i ^ shift) for i in range(count)])


def xor_design(x, shift):
    count = lax.axis_size("design")
    return lax.ppermute(x, "design", [(i, i ^ shift) for i in range(count)])


def request_table(block_list, blocks_dev, capacity, proto_count):
    owners = block_list // blocks_dev
    local_ids = block_list % blocks_dev
    ids = jnp.arange(block_list.shape[0], dtype=jnp.int32)
    earlier = (owners[:, None] == owners[None, :]) & (ids[None, :] < ids[:, None])
    rank_of = jnp.sum(earlier.astype(jnp.int32), axis=1)
    slot_of = owners * capacity + rank_of
    slots = jnp.arange(proto_count * capacity, dtype=jnp.int32)
    hit = slot_of[None, :] == slots[:, None]
    return jnp.sum(jnp.where(hit, local_ids[None, :] + 1, 0), axis=1) - 1


HBM = pl.BlockSpec(memory_space=pl.ANY)
VM = pl.BlockSpec(memory_space=pltpu.VMEM)
SM = pl.BlockSpec(memory_space=pltpu.SMEM)
WIDE = pltpu.CompilerParams(vmem_limit_bytes=40 << 20)
PARAMS = pltpu.CompilerParams(vmem_limit_bytes=16 << 20)


def gather_round_kernel(parts, table, src, *refs):
    outs, buf, sems = refs[:parts], refs[parts], refs[parts + 1]
    cap, _, step = outs[0].shape
    copies = []
    for k in range(cap):
        row = jnp.maximum(table[k], 0)
        copies.append(pltpu.make_async_copy(src.at[row], buf.at[k], sems.at[k]))
    for copy in copies:
        copy.start()
    for k, copy in enumerate(copies):
        copy.wait()
        for i in range(parts):
            outs[i][k] = buf[k, :, i * step : (i + 1) * step].astype(BF)


def gather_round(table, shard, parts):
    cap = table.shape[0]
    _, tile, width = shard.shape
    return pl.pallas_call(
        functools.partial(gather_round_kernel, parts),
        out_shape=[jax.ShapeDtypeStruct((cap, tile, width // parts), BF)] * parts,
        in_specs=[SM, HBM],
        out_specs=[VM] * parts,
        scratch_shapes=[
            pltpu.VMEM((cap, tile, width), F32),
            pltpu.SemaphoreType.DMA((cap,)),
        ],
        compiler_params=PARAMS,
        name="gather_round",
    )(table, shard)


def gather_held_kernel(n_src, n_out, quarter, lanes, me, *refs):
    tables, srcs = refs[:n_out], refs[n_out : n_out + n_src]
    outs, sems = refs[n_out + n_src : -1], refs[-1]
    cap = outs[0].shape[0]
    y, c = me[0] // 2, me[0] % 2
    for i in range(n_out * cap):
        row = jnp.maximum(tables[i // cap][i % cap], 0)
        owner, inside = row // quarter, row % quarter
        which = ((owner % 2) ^ c) * lanes + ((owner // 2) ^ y)
        for a in range(n_src):

            @pl.when(which == a)
            def _():
                pltpu.make_async_copy(
                    srcs[a].at[inside], outs[i // cap].at[i % cap], sems.at[i]
                ).start()

    for i in range(n_out * cap):
        pltpu.make_async_copy(srcs[0].at[0], outs[i // cap].at[i % cap], sems.at[i]).wait()


def gather_held(me, tables, srcs, lanes):
    n = len(tables)
    cap = tables[0].shape[0]
    quarter = srcs[0].shape[0]
    shape = (cap,) + srcs[0].shape[1:]
    return pl.pallas_call(
        functools.partial(gather_held_kernel, len(srcs), n, quarter, lanes),
        out_shape=[jax.ShapeDtypeStruct(shape, BF)] * n,
        in_specs=[SM] * (n + 1) + [HBM] * len(srcs),
        out_specs=[VM] * n,
        scratch_shapes=[pltpu.SemaphoreType.DMA((n * cap,))],
        compiler_params=PARAMS,
        name="gather_held",
    )(me, *tables, *srcs)


def contract(rows, x, lanes):
    step = rows[0].shape[1]
    total = None
    for i, part in enumerate(rows):
        got = lax.dot_general(
            part[...],
            x[lanes, i * step : (i + 1) * step],
            (((1,), (1,)), ((), ())),
            preferred_element_type=F32,
        )
        total = got if total is None else total + got
    return total


EXP_SCALE = (D ** (-0.5)) * 1.4426950408889634


def fold(tile, op):
    return op(tile.reshape(tile.shape[0] // 8, 8, tile.shape[1]), axis=0)


def slot_stats(base, rel, slots):
    top = None
    hit = None
    for n, ref in slots:
        piece = ref[...]
        target = rel == base[n]
        found = fold(jnp.where(target, piece, 0.0), jnp.sum)
        piece = piece + jnp.where(base[n] < 0, NEG, 0.0)
        high = fold(piece, jnp.max)
        top = high if top is None else jnp.maximum(top, high)
        hit = found if hit is None else hit + found
    return jnp.max(top, axis=0, keepdims=True), jnp.sum(hit, axis=0, keepdims=True)


def slot_power(base, n, ref, top):
    piece = ref[...] + jnp.where(base[n] < 0, NEG, 0.0)
    return jnp.exp2((piece - top) * EXP_SCALE)


def relative(pos, lanes):
    line = lax.broadcasted_iota(jnp.int32, (TILE, lanes), 0)
    return pos - line


def own_kernel(group, cap, lanes, parts, base, x, pos, *refs):
    rows = [refs[s * parts : (s + 1) * parts] for s in range(group)]
    logits = refs[group * parts : group * (parts + 1)]
    top_out, sum_out, hit_out = refs[group * (parts + 1) :]
    count = x.shape[0]
    for j in range(0, count, lanes):
        at = pl.ds(j, lanes)
        for s in range(group):
            logits[s][:, at] = contract(rows[s], x, slice(j, j + lanes))
        slots = [
            (s * cap + k, logits[s].at[pl.ds(k * TILE, TILE), at])
            for s in range(group)
            for k in range(cap)
        ]
        top, hit = slot_stats(base, relative(pos[:, at], lanes), slots)
        total = None
        for n, ref in slots:
            part = fold(slot_power(base, n, ref, top), jnp.sum)
            total = part if total is None else total + part
        top_out[:, at] = top
        hit_out[:, at] = hit
        sum_out[:, at] = jnp.sum(total, axis=0, keepdims=True)


def own_logits(base, x, pos, rows, cap, lanes=256):
    group, parts = len(rows), len(rows[0])
    rows = [r for row in rows for r in row]
    count = x.shape[0]
    line = (1, count)
    shape = (rows[0].shape[0], count)
    return pl.pallas_call(
        functools.partial(own_kernel, group, cap, lanes, parts),
        out_shape=[jax.ShapeDtypeStruct(shape, F32)] * group
        + [jax.ShapeDtypeStruct(line, F32)] * 3,
        in_specs=[SM] + [VM] * (2 + len(rows)),
        out_specs=[VM] * (group + 3),
        compiler_params=PARAMS,
        name="own_logits",
    )(base, x, pos, *rows)


def far_kernel(group, cap, lanes, parts, base, x, pos, top_own, sum_own, hit_own, *refs):
    rows = [refs[s * parts : (s + 1) * parts] for s in range(group)]
    refs = refs[group * parts :]
    losses, top_out, inv_out = refs[:3]
    grads = refs[3 : group + 3]
    tiles = refs[group + 3 : -1]
    logits = refs[-1]
    count, width = x.shape
    scale = D ** (-0.5)
    for j in range(0, count, lanes):
        turn = (j // lanes) % 2
        at = pl.ds(j, lanes)
        for s in range(group):
            logits[turn, s * cap * TILE : (s + 1) * cap * TILE, :] = contract(
                rows[s], x, slice(j, j + lanes)
            )
        slots = [
            (n, logits.at[turn, pl.ds(n * TILE, TILE), :]) for n in range(group * cap)
        ]
        rel = relative(pos[:, at], lanes)
        top, hit = slot_stats(base, rel, slots)
        mine = top_own[:, at]
        both = jnp.maximum(top, mine)
        total = None
        for n, ref in slots:
            power = slot_power(base, n, ref, both)
            ref[...] = power
            part = fold(power, jnp.sum)
            total = part if total is None else total + part
        total = jnp.sum(total, axis=0, keepdims=True)
        total = total + sum_own[:, at] * jnp.exp2((mine - both) * EXP_SCALE)
        losses[:, at] = both * scale + jnp.log(total) - (hit + hit_own[:, at]) * scale
        inv = 1.0 / total
        top_out[:, at] = both
        inv_out[:, at] = inv
        for n, ref in slots:
            s, k = n // cap, n % cap
            target = jnp.where(rel == base[n], 1.0, 0.0)
            grads[s][k * TILE : (k + 1) * TILE, at] = (ref[...] * inv - target).astype(BF)
    step = width // parts
    for i in range(parts):
        for s in range(group):
            tiles[i * group + s][...] = jnp.dot(
                grads[s][...], x[:, i * step : (i + 1) * step], preferred_element_type=F32
            ).astype(BF)


def far_grads(base, x, pos, stats, rows, cap, parts, lanes=256):
    group = len(rows)
    rows = [r for row in rows for r in row]
    count, width = x.shape
    size = rows[0].shape[0]
    outs = [((1, count), F32)] * 3 + [((size, count), BF)] * group
    outs += [((size, width // parts), BF)] * (group * parts)
    got = pl.pallas_call(
        functools.partial(far_kernel, group, cap, lanes, parts),
        out_shape=[jax.ShapeDtypeStruct(*o) for o in outs],
        in_specs=[SM] + [VM] * (5 + len(rows)),
        out_specs=[VM] * len(outs),
        scratch_shapes=[pltpu.VMEM((2, group * size, lanes), F32)],
        compiler_params=PARAMS,
        name="far_grads",
    )(base, x, pos, *stats, *rows)
    tiles = got[3 + group :]
    return got[:3], got[3 : 3 + group], [tiles[i * group : (i + 1) * group] for i in range(parts)]


def own_grad_kernel(cap, parts, base, x, pos, top, inv, logits, grad, *tiles):
    count, width = x.shape
    rel = relative(pos[...], count)
    for k in range(cap):
        ref = logits.at[pl.ds(k * TILE, TILE), :]
        power = slot_power(base, k, ref, top[...])
        target = jnp.where(rel == base[k], 1.0, 0.0)
        grad[k * TILE : (k + 1) * TILE, :] = (power * inv[...] - target).astype(BF)
    step = width // parts
    for i in range(parts):
        tiles[i][...] = jnp.dot(
            grad[...], x[:, i * step : (i + 1) * step], preferred_element_type=F32
        ).astype(BF)


def own_grad(base, x, pos, top, inv, logits, cap, parts):
    count, width = x.shape
    size = logits.shape[0]
    outs = [((size, count), BF)] + [((size, width // parts), BF)] * parts
    got = pl.pallas_call(
        functools.partial(own_grad_kernel, cap, parts),
        out_shape=[jax.ShapeDtypeStruct(*o) for o in outs],
        in_specs=[SM] + [VM] * 5,
        out_specs=[VM] * len(outs),
        compiler_params=PARAMS,
        name="own_grad",
    )(base, x, pos, top, inv, logits)
    return got[0], got[1:]


def design_grad_kernel(n, *refs):
    grads, rows, out = refs[:n], refs[n : 2 * n], refs[2 * n]
    acc = None
    for g, r in zip(grads, rows):
        part = lax.dot_general(
            g[...], r[...], (((0,), (0,)), ((), ())), preferred_element_type=F32
        )
        acc = part if acc is None else acc + part
    out[...] = acc.astype(BF)


def design_grad(grads, rows, chunk=256):
    n = len(grads)
    cols, count = grads[0].shape
    width = rows[0].shape[1]
    return pl.pallas_call(
        functools.partial(design_grad_kernel, n),
        out_shape=jax.ShapeDtypeStruct((count, width), BF),
        grid=(count // chunk,),
        in_specs=[pl.BlockSpec((cols, chunk), lambda i: (0, i))] * n
        + [pl.BlockSpec((cols, width), lambda i: (0, 0))] * n,
        out_specs=pl.BlockSpec((chunk, width), lambda i: (i, 0)),
        compiler_params=WIDE,
        name="design_grad",
    )(*grads, *rows)


def collect_kernel(n, cap, spot, *refs):
    parts = refs[:n]
    keep, give, acc = refs[n:]
    kept = keep.shape[0]
    acc[...] = jnp.zeros_like(acc)
    for i in range(n * cap):

        @pl.when(spot[i] >= 0)
        def _():
            s, k = i // cap, i % cap
            acc[spot[i]] += parts[s][k * TILE : (k + 1) * TILE, :].astype(F32)

    keep[...] = acc[:kept]
    give[...] = acc[kept:].astype(BF)


def collect(spot, parts, cap, kept):
    n = len(parts)
    width = parts[0].shape[1]
    shape = (kept, TILE, width)
    return pl.pallas_call(
        functools.partial(collect_kernel, n, cap),
        out_shape=[jax.ShapeDtypeStruct(shape, F32), jax.ShapeDtypeStruct(shape, BF)],
        in_specs=[SM] + [VM] * n,
        out_specs=[VM] * 2,
        scratch_shapes=[pltpu.VMEM((2 * kept, TILE, width), F32)],
        compiler_params=PARAMS,
        name="collect",
    )(spot, *parts)


def body(designs, prototypes, candidates, positives):
    proto_count = lax.axis_size("proto")
    design_axis = lax.axis_size("design")
    half = proto_count // 2
    lanes = design_axis // 2
    cand_count = candidates.shape[1]
    width = designs.shape[1]
    count = designs.shape[0]
    blocks_dev = prototypes.shape[0] // TILE
    quarter = blocks_dev // design_axis
    cap = max(2, (4 * cand_count + 3 * proto_count - 1) // (3 * proto_count))
    parts = PARTS
    step = width // parts
    p = lax.axis_index("proto").astype(jnp.int32)
    d = lax.axis_index("design").astype(jnp.int32)
    q = p % half
    h = p // half
    y = d // 2
    c = d % 2
    me = d.reshape(1)
    shifts = list(range(half - 1, 0, -1))
    evens = list(range(2, half, 2))
    columns = [slice(i * step, (i + 1) * step) for i in range(parts)]

    wanted = request_table(candidates[0], blocks_dev, cap, proto_count)
    wanted = wanted.reshape(2, half, cap)
    near = [wanted[h, q ^ s] for s in range(half)]
    other = [wanted[1 - h, q ^ s] for s in range(half)]
    asking = {0: other[0]}
    for s in shifts:
        if s == 1:
            note = jnp.stack([other[1]] + [near[u ^ 1] for u in [0] + evens])
            note = xor_proto(note, 1)
            asking[1] = note[0]
            beside = {u: note[1 + n] for n, u in enumerate([0] + evens)}
        else:
            asking[s] = xor_proto(other[s], s)

    shard = prototypes.reshape(blocks_dev, TILE, width)
    mine = lax.dynamic_slice_in_dim(shard, d * quarter, quarter, axis=0).astype(BF)
    sent = {}
    for i in range(parts):
        piece = mine[:, :, columns[i]]
        for u in evens:
            sent[u, i] = xor_proto(piece, u)
        sent["far", i] = xor_proto(piece, half)

    def share(piece):
        held = [piece]
        for ys in range(1, lanes):
            held.append(xor_design(piece, 2 * ys))
        return held + [xor_design(held[ys], 1) for ys in range(lanes)]

    def flat(piece):
        return piece.reshape(cap * TILE, step)

    own_rows = [[None] * parts for _ in range(half)]
    far_rows = [[None] * parts for _ in range(half)]
    out = gather_round(beside[0], shard, parts)
    for i in range(parts):
        own_rows[1][i] = flat(xor_proto(out[i], 1))
    out = gather_round(near[0], shard, parts)
    for i in range(parts):
        own_rows[0][i] = flat(out[i])
    for i in range(parts):
        for u in evens:
            held = share(sent[u, i])
            (out,) = gather_held(me, [beside[u]], held, lanes)
            own_rows[u ^ 1][i] = flat(xor_proto(out, 1))
            (out,) = gather_held(me, [near[u]], held, lanes)
            own_rows[u][i] = flat(out)
        held = share(sent["far", i])
        outs = gather_held(me, [asking[s] for s in shifts], held, lanes)
        for s, out in zip(shifts, outs):
            far_rows[s][i] = flat(xor_proto(out, s))
        (out,) = gather_held(me, [asking[0]], held, lanes)
        far_rows[0][i] = flat(out)

    def bases(lists, which_half):
        out = []
        for s in range(half):
            first = (which_half * half + (q ^ s)) * blocks_dev
            out.append(jnp.where(lists[s] >= 0, (first + lists[s]) * TILE, -(2**30)))
        return jnp.concatenate(out)

    pos = positives.reshape(1, count)
    own_base = bases(near, h)
    *logits, top, total, hit = own_logits(own_base, designs, pos, own_rows, cap)
    stats, far_g, far_tiles = far_grads(
        bases(other, 1 - h), designs, pos, (top, total, hit), far_rows, cap, parts
    )
    losses, top, inv = stats
    own_base = own_base.reshape(half, cap)
    own_g, own_tiles = [], []
    for s in range(half):
        g, t = own_grad(own_base[s], designs, pos, top, inv, logits[s], cap, parts)
        own_g.append(g)
        own_tiles.append(t)

    kept = lanes * quarter

    def spots(tables):
        table = jnp.concatenate(tables)
        owner = table // quarter
        at = ((owner // 2) ^ y) * quarter + table % quarter
        at = at + jnp.where(owner % 2 == c, 0, kept)
        return jnp.where(table >= 0, at, -1)

    def reduce_shard(tables, tiles):
        keep, give = collect(spots(tables), tiles, cap, kept)
        keep = keep + xor_design(give, 1).astype(F32)
        keep = keep.reshape(lanes, quarter, TILE, step)
        total = keep[0]
        for ys in range(1, lanes):
            back = xor_design(keep[ys].astype(BF), 2 * ys)
            total = total + back.astype(F32)
        return total

    result = []
    dgrad = []
    far_tables = [asking[s] for s in range(half)]
    for i in range(parts):
        tiles = [far_tiles[i][0]]
        tiles += [xor_proto(far_tiles[i][s], s) for s in range(1, half)]
        total = reduce_shard(far_tables, tiles)
        landed = [xor_proto(total.astype(BF), half)]
        for u in evens:
            tile = xor_proto(own_tiles[u ^ 1][i], 1)
            total = reduce_shard([near[u], beside[u]], [own_tiles[u][i], tile])
            landed.append(xor_proto(total.astype(BF), u))
        tile = xor_proto(own_tiles[1][i], 1)
        total = reduce_shard([near[0], beside[0]], [own_tiles[0][i], tile])
        for piece in landed:
            total = total + piece.astype(F32)
        result.append(total)
        dgrad.append(
            design_grad(own_g + list(far_g), [r[i] for r in own_rows + far_rows])
        )
    result = jnp.concatenate(result, axis=-1).reshape(quarter * TILE, width)
    return (losses.reshape(count), jnp.concatenate(dgrad, axis=-1), result)


def solution(mesh):
    return jax.shard_map(
        body,
        mesh=mesh,
        in_specs=(
            P(("proto", "design"), None),
            P("proto", None),
            P(("proto", "design"), None),
            P(("proto", "design")),
        ),
        out_specs=(
            P(("proto", "design")),
            P(("proto", "design"), None),
            P(("proto", "design"), None),
        ),
        check_vma=False,
    )
```

```python
import functools

import jax
import jax.numpy as jnp
from jax import lax
from jax.experimental import pallas as pl
from jax.experimental.pallas import tpu as pltpu
from jax.sharding import PartitionSpec as P


D = 1024
TILE = 128
BF = jnp.bfloat16
F32 = jnp.float32
NEG = -1e30
PARTS = 2


def xor_proto(x, shift):
    count = lax.axis_size("proto")
    return lax.ppermute(x, "proto", [(i, i ^ shift) for i in range(count)])


def xor_design(x, shift):
    count = lax.axis_size("design")
    return lax.ppermute(x, "design", [(i, i ^ shift) for i in range(count)])


def request_table(block_list, blocks_dev, capacity, proto_count):
    owners = block_list // blocks_dev
    local_ids = block_list % blocks_dev
    ids = jnp.arange(block_list.shape[0], dtype=jnp.int32)
    earlier = (owners[:, None] == owners[None, :]) & (ids[None, :] < ids[:, None])
    rank_of = jnp.sum(earlier.astype(jnp.int32), axis=1)
    slot_of = owners * capacity + rank_of
    slots = jnp.arange(proto_count * capacity, dtype=jnp.int32)
    hit = slot_of[None, :] == slots[:, None]
    return jnp.sum(jnp.where(hit, local_ids[None, :] + 1, 0), axis=1) - 1


HBM = pl.BlockSpec(memory_space=pl.ANY)
VM = pl.BlockSpec(memory_space=pltpu.VMEM)
SM = pl.BlockSpec(memory_space=pltpu.SMEM)
FIXED = pl.BlockSpec(memory_space=pltpu.HBM)


def grant(mib):
    return pltpu.CompilerParams(vmem_limit_bytes=mib << 20)


def gather_round_kernel(parts, table, src, *refs):
    outs, buf, sems = refs[:parts], refs[parts], refs[parts + 1]
    cap, _, step = outs[0].shape
    copies = []
    for k in range(cap):
        row = jnp.maximum(table[k], 0)
        copies.append(pltpu.make_async_copy(src.at[row], buf.at[k], sems.at[k]))
    for copy in copies:
        copy.start()
    for k, copy in enumerate(copies):
        copy.wait()
        for i in range(parts):
            outs[i][k] = buf[k, :, i * step : (i + 1) * step].astype(BF)


def gather_round(table, shard, parts):
    cap = table.shape[0]
    _, tile, width = shard.shape
    return pl.pallas_call(
        functools.partial(gather_round_kernel, parts),
        out_shape=[jax.ShapeDtypeStruct((cap, tile, width // parts), BF)] * parts,
        in_specs=[SM, FIXED],
        out_specs=[VM] * parts,
        scratch_shapes=[
            pltpu.VMEM((cap, tile, width), F32),
            pltpu.SemaphoreType.DMA((cap,)),
        ],
        compiler_params=grant(6),
        name="gather_round",
    )(table, shard)


def gather_held_kernel(n_src, n_out, quarter, lanes, me, *refs):
    tables, srcs = refs[:n_out], refs[n_out : n_out + n_src]
    outs, sems = refs[n_out + n_src : -1], refs[-1]
    cap = outs[0].shape[0]
    y, c = me[0] // 2, me[0] % 2
    for n in range(n_out):

        @pl.loop(0, cap)
        def _(k):
            row = jnp.maximum(tables[n][k], 0)
            owner, inside = row // quarter, row % quarter
            which = ((owner % 2) ^ c) * lanes + ((owner // 2) ^ y)
            for a in range(n_src):

                @pl.when(which == a)
                def _():
                    pltpu.make_async_copy(
                        srcs[a].at[inside], outs[n].at[k], sems.at[n * cap + k]
                    ).start()

    for n in range(n_out):

        @pl.loop(0, cap)
        def _(k):
            pltpu.make_async_copy(srcs[0].at[0], outs[n].at[k], sems.at[n * cap + k]).wait()


def gather_held(me, tables, srcs, lanes):
    n = len(tables)
    cap = tables[0].shape[0]
    quarter = srcs[0].shape[0]
    shape = (cap,) + srcs[0].shape[1:]
    return pl.pallas_call(
        functools.partial(gather_held_kernel, len(srcs), n, quarter, lanes),
        out_shape=[jax.ShapeDtypeStruct(shape, BF)] * n,
        in_specs=[SM] * (n + 1) + [HBM] * len(srcs),
        out_specs=[VM] * n,
        scratch_shapes=[pltpu.SemaphoreType.DMA((n * cap,))],
        compiler_params=grant(2),
        name="gather_held",
    )(me, *tables, *srcs)


def contract(rows, x, lanes):
    step = rows[0].shape[1]
    total = None
    for i, part in enumerate(rows):
        got = lax.dot_general(
            part[...],
            x[lanes, i * step : (i + 1) * step],
            (((1,), (1,)), ((), ())),
            preferred_element_type=F32,
        )
        total = got if total is None else total + got
    return total


EXP_SCALE = (D ** (-0.5)) * 1.4426950408889634


def fold(tile, op):
    return op(tile.reshape(tile.shape[0] // 8, 8, tile.shape[1]), axis=0)


def slot_stats(base, rel, slots):
    top = None
    hit = None
    for n, ref in slots:
        piece = ref[...]
        target = rel == base[n]
        found = fold(jnp.where(target, piece, 0.0), jnp.sum)
        piece = piece + jnp.where(base[n] < 0, NEG, 0.0)
        high = fold(piece, jnp.max)
        top = high if top is None else jnp.maximum(top, high)
        hit = found if hit is None else hit + found
    return jnp.max(top, axis=0, keepdims=True), jnp.sum(hit, axis=0, keepdims=True)


def slot_power(base, n, ref, top):
    piece = ref[...] + jnp.where(base[n] < 0, NEG, 0.0)
    return jnp.exp2((piece - top) * EXP_SCALE)


def relative(pos, lanes):
    line = lax.broadcasted_iota(jnp.int32, (TILE, lanes), 0)
    return pos - line


def own_kernel(group, cap, lanes, parts, base, x, pos, *refs):
    rows = [refs[s * parts : (s + 1) * parts] for s in range(group)]
    kept = refs[group * parts : group * (parts + 1)]
    top_out, sum_out, hit_out, logits, sems = refs[group * (parts + 1) :]
    count = x.shape[0]

    def copy_out(s, j):
        at = pl.ds(pl.multiple_of(j * lanes, lanes), lanes)
        return pltpu.make_async_copy(logits.at[s, :, at], kept[s].at[:, at], sems.at[s, j])

    @pl.loop(0, count // lanes)
    def _(j):
        at = pl.ds(pl.multiple_of(j * lanes, lanes), lanes)
        for s in range(group):
            logits[s, :, at] = contract(rows[s], x, at)
            copy_out(s, j).start()
        slots = [
            (s * cap + k, logits.at[s, pl.ds(k * TILE, TILE), at])
            for s in range(group)
            for k in range(cap)
        ]
        top, hit = slot_stats(base, relative(pos[:, at], lanes), slots)
        total = None
        for n, ref in slots:
            part = fold(slot_power(base, n, ref, top), jnp.sum)
            total = part if total is None else total + part
        top_out[:, at] = top
        hit_out[:, at] = hit
        sum_out[:, at] = jnp.sum(total, axis=0, keepdims=True)

    @pl.loop(0, count // lanes)
    def _(j):
        for s in range(group):
            copy_out(s, j).wait()


def own_logits(base, x, pos, rows, cap, lanes=256):
    group, parts = len(rows), len(rows[0])
    rows = [r for row in rows for r in row]
    count = x.shape[0]
    line = (1, count)
    shape = (rows[0].shape[0], count)
    return pl.pallas_call(
        functools.partial(own_kernel, group, cap, lanes, parts),
        out_shape=[jax.ShapeDtypeStruct(shape, F32)] * group
        + [jax.ShapeDtypeStruct(line, F32)] * 3,
        in_specs=[SM] + [VM] * (2 + len(rows)),
        out_specs=[FIXED] * group + [VM] * 3,
        scratch_shapes=[
            pltpu.VMEM((group,) + shape, F32),
            pltpu.SemaphoreType.DMA((group, count // lanes)),
        ],
        compiler_params=grant(12),
        name="own_logits",
    )(base, x, pos, *rows)


def far_kernel(group, cap, lanes, parts, n_stats, base, x, pos, *refs):
    stats = [refs[3 * i : 3 * i + 3] for i in range(n_stats)]
    refs = refs[3 * n_stats :]
    rows = [refs[s * parts : (s + 1) * parts] for s in range(group)]
    refs = refs[group * parts :]
    losses, top_out, inv_out = refs[:3]
    kept = refs[3:-4]
    logits, grads, tiles, sems = refs[-4:]
    count, width = x.shape
    scale = D ** (-0.5)
    for j in range(0, count, lanes):
        turn = (j // lanes) % 2
        at = pl.ds(j, lanes)
        for s in range(group):
            logits[turn, s * cap * TILE : (s + 1) * cap * TILE, :] = contract(
                rows[s], x, pl.ds(j, lanes)
            )
        slots = [
            (n, logits.at[turn, pl.ds(n * TILE, TILE), :]) for n in range(group * cap)
        ]
        rel = relative(pos[:, at], lanes)
        top, hit = slot_stats(base, rel, slots)
        both = top
        for top_own, _, _ in stats:
            both = jnp.maximum(both, top_own[:, at])
        total = None
        for n, ref in slots:
            power = slot_power(base, n, ref, both)
            ref[...] = power
            part = fold(power, jnp.sum)
            total = part if total is None else total + part
        total = jnp.sum(total, axis=0, keepdims=True)
        for top_own, sum_own, hit_own in stats:
            total = total + sum_own[:, at] * jnp.exp2((top_own[:, at] - both) * EXP_SCALE)
            hit = hit + hit_own[:, at]
        losses[:, at] = both * scale + jnp.log(total) - hit * scale
        inv = 1.0 / total
        top_out[:, at] = both
        inv_out[:, at] = inv
        for n, ref in slots:
            s, k = n // cap, n % cap
            target = jnp.where(rel == base[n], 1.0, 0.0)
            grads[s, k * TILE : (k + 1) * TILE, at] = (ref[...] * inv - target).astype(BF)
    step = width // parts
    sources = [grads.at[s] for s in range(group)]
    sources += [tiles.at[n] for n in range(parts * group)]
    copies = [pltpu.make_async_copy(a, b, sems.at[n]) for n, (a, b) in enumerate(zip(sources, kept))]
    for copy in copies[:group]:
        copy.start()
    for i in range(parts):
        for s in range(group):
            n = i * group + s
            tiles[n] = jnp.dot(
                grads[s], x[:, i * step : (i + 1) * step], preferred_element_type=F32
            ).astype(BF)
            copies[group + n].start()
    for copy in copies:
        copy.wait()


def far_grads(base, x, pos, stats, rows, cap, parts, lanes=256):
    group = len(rows)
    rows = [r for row in rows for r in row]
    count, width = x.shape
    size = rows[0].shape[0]
    outs = [((1, count), F32)] * 3 + [((size, count), BF)] * group
    outs += [((size, width // parts), BF)] * (group * parts)
    got = pl.pallas_call(
        functools.partial(far_kernel, group, cap, lanes, parts, len(stats) // 3),
        out_shape=[jax.ShapeDtypeStruct(*o) for o in outs],
        in_specs=[SM] + [VM] * (2 + len(stats) + len(rows)),
        out_specs=[VM] * 3 + [FIXED] * (len(outs) - 3),
        scratch_shapes=[
            pltpu.VMEM((2, group * size, lanes), F32),
            pltpu.VMEM((group, size, count), BF),
            pltpu.VMEM((group * parts, size, width // parts), BF),
            pltpu.SemaphoreType.DMA((group * (1 + parts),)),
        ],
        compiler_params=grant(20),
        name="far_grads",
    )(base, x, pos, *stats, *rows)
    tiles = got[3 + group :]
    return got[:3], got[3 : 3 + group], [tiles[i * group : (i + 1) * group] for i in range(parts)]


def own_grad_kernel(cap, parts, base, x, pos, top, inv, logits, grad, *tiles):
    count, width = x.shape
    rel = relative(pos[...], count)
    for k in range(cap):
        ref = logits.at[pl.ds(k * TILE, TILE), :]
        power = slot_power(base, k, ref, top[...])
        target = jnp.where(rel == base[k], 1.0, 0.0)
        grad[k * TILE : (k + 1) * TILE, :] = (power * inv[...] - target).astype(BF)
    step = width // parts
    for i in range(parts):
        tiles[i][...] = jnp.dot(
            grad[...], x[:, i * step : (i + 1) * step], preferred_element_type=F32
        ).astype(BF)


def own_grad(base, x, pos, top, inv, logits, cap, parts):
    count, width = x.shape
    size = logits.shape[0]
    outs = [((size, count), BF)] + [((size, width // parts), BF)] * parts
    got = pl.pallas_call(
        functools.partial(own_grad_kernel, cap, parts),
        out_shape=[jax.ShapeDtypeStruct(*o) for o in outs],
        in_specs=[SM] + [VM] * 5,
        out_specs=[VM] * len(outs),
        compiler_params=grant(6),
        name="own_grad",
    )(base, x, pos, top, inv, logits)
    return got[0], got[1:]


def design_grad_kernel(n, chunk, *refs):
    grads, rows, out = refs[:n], refs[n : 2 * n], refs[2 * n]

    @pl.loop(0, out.shape[0] // chunk)
    def _(j):
        at = pl.ds(pl.multiple_of(j * chunk, chunk), chunk)
        acc = None
        for g, r in zip(grads, rows):
            part = lax.dot_general(
                g[:, at], r[...], (((0,), (0,)), ((), ())), preferred_element_type=F32
            )
            acc = part if acc is None else acc + part
        out[at, :] = acc.astype(BF)


def design_grad(grads, rows, chunk=256):
    n = len(grads)
    return pl.pallas_call(
        functools.partial(design_grad_kernel, n, chunk),
        out_shape=jax.ShapeDtypeStruct((grads[0].shape[1], rows[0].shape[1]), BF),
        in_specs=[VM] * (2 * n),
        out_specs=VM,
        compiler_params=grant(8),
        name="design_grad",
    )(*grads, *rows)


def collect_kernel(n, cap, spot, *refs):
    parts = refs[:n]
    keep, give, acc = refs[n:]
    kept = keep.shape[0]
    acc[...] = jnp.zeros_like(acc)
    for i in range(n * cap):

        @pl.when(spot[i] >= 0)
        def _():
            s, k = i // cap, i % cap
            acc[spot[i]] += parts[s][k * TILE : (k + 1) * TILE, :].astype(F32)

    keep[...] = acc[:kept]
    give[...] = acc[kept:].astype(BF)


def collect(spot, parts, cap, kept):
    n = len(parts)
    width = parts[0].shape[1]
    shape = (kept, TILE, width)
    return pl.pallas_call(
        functools.partial(collect_kernel, n, cap),
        out_shape=[jax.ShapeDtypeStruct(shape, F32), jax.ShapeDtypeStruct(shape, BF)],
        in_specs=[SM] + [VM] * n,
        out_specs=[VM] * 2,
        scratch_shapes=[pltpu.VMEM((2 * kept, TILE, width), F32)],
        compiler_params=grant(8),
        name="collect",
    )(spot, *parts)


def body(designs, prototypes, candidates, positives):
    proto_count = lax.axis_size("proto")
    design_axis = lax.axis_size("design")
    half = proto_count // 2
    lanes = design_axis // 2
    cand_count = candidates.shape[1]
    width = designs.shape[1]
    count = designs.shape[0]
    blocks_dev = prototypes.shape[0] // TILE
    quarter = blocks_dev // design_axis
    cap = max(2, (4 * cand_count + 3 * proto_count - 1) // (3 * proto_count))
    parts = PARTS
    step = width // parts
    p = lax.axis_index("proto").astype(jnp.int32)
    d = lax.axis_index("design").astype(jnp.int32)
    q = p % half
    h = p // half
    y = d // 2
    c = d % 2
    me = d.reshape(1)
    shifts = list(range(half - 1, 0, -1))
    evens = list(range(2, half, 2))
    columns = [slice(i * step, (i + 1) * step) for i in range(parts)]

    wanted = request_table(candidates[0], blocks_dev, cap, proto_count)
    wanted = wanted.reshape(2, half, cap)
    near = [wanted[h, q ^ s] for s in range(half)]
    other = [wanted[1 - h, q ^ s] for s in range(half)]
    asking = {0: other[0]}
    for s in shifts:
        if s == 1:
            note = jnp.stack([other[1]] + [near[u ^ 1] for u in [0] + evens])
            note = xor_proto(note, 1)
            asking[1] = note[0]
            beside = {u: note[1 + n] for n, u in enumerate([0] + evens)}
        else:
            asking[s] = xor_proto(other[s], s)

    shard = prototypes.reshape(blocks_dev, TILE, width)
    mine = lax.dynamic_slice_in_dim(shard, d * quarter, quarter, axis=0).astype(BF)
    sent = {}
    for i in range(parts):
        piece = mine[:, :, columns[i]]
        for u in evens:
            sent[u, i] = xor_proto(piece, u)
        sent["far", i] = xor_proto(piece, half)

    def share(piece):
        held = [piece]
        for ys in range(1, lanes):
            held.append(xor_design(piece, 2 * ys))
        return held + [xor_design(held[ys], 1) for ys in range(lanes)]

    def flat(piece):
        return piece.reshape(cap * TILE, step)

    own_rows = [[None] * parts for _ in range(half)]
    far_rows = [[None] * parts for _ in range(half)]
    out = gather_round(beside[0], shard, parts)
    for i in range(parts):
        own_rows[1][i] = flat(xor_proto(out[i], 1))
    out = gather_round(near[0], shard, parts)
    for i in range(parts):
        own_rows[0][i] = flat(out[i])
    for i in range(parts):
        for u in evens:
            held = share(sent[u, i])
            (out,) = gather_held(me, [beside[u]], held, lanes)
            own_rows[u ^ 1][i] = flat(xor_proto(out, 1))
            (out,) = gather_held(me, [near[u]], held, lanes)
            own_rows[u][i] = flat(out)
        held = share(sent["far", i])
        outs = gather_held(me, [asking[s] for s in shifts], held, lanes)
        for s, out in zip(shifts, outs):
            far_rows[s][i] = flat(xor_proto(out, s))
        (out,) = gather_held(me, [asking[0]], held, lanes)
        far_rows[0][i] = flat(out)

    def bases(lists, which_half, group):
        out = []
        for s in group:
            first = (which_half * half + (q ^ s)) * blocks_dev
            out.append(jnp.where(lists[s] >= 0, (first + lists[s]) * TILE, -(2**30)))
        return jnp.concatenate(out)

    pos = positives.reshape(1, count)
    logits, sums = {}, []
    for group in groups_of(half).values():
        *got, top, total, hit = own_logits(
            bases(near, h, group), designs, pos, [own_rows[s] for s in group], cap
        )
        logits.update(zip(group, got))
        sums += [top, total, hit]
    stats, far_g, far_tiles = far_grads(
        bases(other, 1 - h, range(half)), designs, pos, sums, far_rows, cap, parts
    )
    losses, top, inv = stats
    own_g, own_tiles = [], []
    for s in range(half):
        g, t = own_grad(
            bases(near, h, [s]), designs, pos, top, inv, logits[s], cap, parts
        )
        own_g.append(g)
        own_tiles.append(t)

    kept = lanes * quarter

    def spots(tables):
        table = jnp.concatenate(tables)
        owner = table // quarter
        at = ((owner // 2) ^ y) * quarter + table % quarter
        at = at + jnp.where(owner % 2 == c, 0, kept)
        return jnp.where(table >= 0, at, -1)

    def reduce_shard(tables, tiles):
        keep, give = collect(spots(tables), tiles, cap, kept)
        keep = keep + xor_design(give, 1).astype(F32)
        keep = keep.reshape(lanes, quarter, TILE, step)
        total = keep[0]
        for ys in range(1, lanes):
            back = xor_design(keep[ys].astype(BF), 2 * ys)
            total = total + back.astype(F32)
        return total

    result = []
    dgrad = []
    far_tables = [asking[s] for s in range(half)]
    for i in range(parts):
        tiles = [far_tiles[i][0]]
        tiles += [xor_proto(far_tiles[i][s], s) for s in range(1, half)]
        total = reduce_shard(far_tables, tiles)
        landed = [xor_proto(total.astype(BF), half)]
        for u in evens:
            tile = xor_proto(own_tiles[u ^ 1][i], 1)
            total = reduce_shard([near[u], beside[u]], [own_tiles[u][i], tile])
            landed.append(xor_proto(total.astype(BF), u))
        tile = xor_proto(own_tiles[1][i], 1)
        total = reduce_shard([near[0], beside[0]], [own_tiles[0][i], tile])
        for piece in landed:
            total = total + piece.astype(F32)
        result.append(total)
        dgrad.append(
            design_grad(own_g + list(far_g), [r[i] for r in own_rows + far_rows])
        )
    result = jnp.concatenate(result, axis=-1).reshape(quarter * TILE, width)
    return (losses.reshape(count), jnp.concatenate(dgrad, axis=-1), result)


def groups_of(half):
    late = list(range(3, half, 2))
    return {"own_a": [s for s in range(half) if s not in late], "own_b": late}


def solution(mesh):
    return jax.shard_map(
        body,
        mesh=mesh,
        in_specs=(
            P(("proto", "design"), None),
            P("proto", None),
            P(("proto", "design"), None),
            P(("proto", "design")),
        ),
        out_specs=(
            P(("proto", "design")),
            P(("proto", "design"), None),
            P(("proto", "design"), None),
        ),
        check_vma=False,
    )
```

```python
import functools

import jax
import jax.numpy as jnp
from jax import lax
from jax.experimental import pallas as pl
from jax.experimental.pallas import tpu as pltpu
from jax.sharding import PartitionSpec as P


D = 1024
TILE = 128
BF = jnp.bfloat16
F32 = jnp.float32
NEG = -1e30
PARTS = 2


def xor_proto(x, shift):
    count = lax.axis_size("proto")
    return lax.ppermute(x, "proto", [(i, i ^ shift) for i in range(count)])


def xor_design(x, shift):
    count = lax.axis_size("design")
    return lax.ppermute(x, "design", [(i, i ^ shift) for i in range(count)])


def request_table(block_list, blocks_dev, capacity, proto_count):
    owners = block_list // blocks_dev
    local_ids = block_list % blocks_dev
    ids = jnp.arange(block_list.shape[0], dtype=jnp.int32)
    earlier = (owners[:, None] == owners[None, :]) & (ids[None, :] < ids[:, None])
    rank_of = jnp.sum(earlier.astype(jnp.int32), axis=1)
    slot_of = owners * capacity + rank_of
    slots = jnp.arange(proto_count * capacity, dtype=jnp.int32)
    hit = slot_of[None, :] == slots[:, None]
    return jnp.sum(jnp.where(hit, local_ids[None, :] + 1, 0), axis=1) - 1


HBM = pl.BlockSpec(memory_space=pl.ANY)
VM = pl.BlockSpec(memory_space=pltpu.VMEM)
SM = pl.BlockSpec(memory_space=pltpu.SMEM)
FIXED = pl.BlockSpec(memory_space=pltpu.HBM)


def grant(mib):
    return pltpu.CompilerParams(vmem_limit_bytes=mib << 20)


def gather_round_kernel(parts, table, src, *refs):
    outs, buf, sems = refs[:parts], refs[parts], refs[parts + 1]
    cap, _, step = outs[0].shape
    copies = []
    for k in range(cap):
        row = jnp.maximum(table[k], 0)
        copies.append(pltpu.make_async_copy(src.at[row], buf.at[k], sems.at[k]))
    for copy in copies:
        copy.start()
    for k, copy in enumerate(copies):
        copy.wait()
        for i in range(parts):
            outs[i][k] = buf[k, :, i * step : (i + 1) * step].astype(BF)


def gather_round(table, shard, parts):
    cap = table.shape[0]
    _, tile, width = shard.shape
    return pl.pallas_call(
        functools.partial(gather_round_kernel, parts),
        out_shape=[jax.ShapeDtypeStruct((cap, tile, width // parts), BF)] * parts,
        in_specs=[SM, FIXED],
        out_specs=[VM] * parts,
        scratch_shapes=[
            pltpu.VMEM((cap, tile, width), F32),
            pltpu.SemaphoreType.DMA((cap,)),
        ],
        compiler_params=grant(6),
        name="gather_round",
    )(table, shard)


def gather_held_kernel(n_src, n_out, quarter, lanes, me, *refs):
    tables, srcs = refs[:n_out], refs[n_out : n_out + n_src]
    outs, sems = refs[n_out + n_src : -1], refs[-1]
    cap = outs[0].shape[0]
    y, c = me[0] // 2, me[0] % 2
    for n in range(n_out):

        @pl.loop(0, cap)
        def _(k):
            row = jnp.maximum(tables[n][k], 0)
            owner, inside = row // quarter, row % quarter
            which = ((owner % 2) ^ c) * lanes + ((owner // 2) ^ y)
            for a in range(n_src):

                @pl.when(which == a)
                def _():
                    pltpu.make_async_copy(
                        srcs[a].at[inside], outs[n].at[k], sems.at[n * cap + k]
                    ).start()

    for n in range(n_out):

        @pl.loop(0, cap)
        def _(k):
            pltpu.make_async_copy(srcs[0].at[0], outs[n].at[k], sems.at[n * cap + k]).wait()


def gather_held(me, tables, srcs, lanes):
    n = len(tables)
    cap = tables[0].shape[0]
    quarter = srcs[0].shape[0]
    shape = (cap,) + srcs[0].shape[1:]
    return pl.pallas_call(
        functools.partial(gather_held_kernel, len(srcs), n, quarter, lanes),
        out_shape=[jax.ShapeDtypeStruct(shape, BF)] * n,
        in_specs=[SM] * (n + 1) + [HBM] * len(srcs),
        out_specs=[VM] * n,
        scratch_shapes=[pltpu.SemaphoreType.DMA((n * cap,))],
        compiler_params=grant(2),
        name="gather_held",
    )(me, *tables, *srcs)


def contract(rows, x, lanes):
    step = rows[0].shape[1]
    total = None
    for i, part in enumerate(rows):
        got = lax.dot_general(
            part[...],
            x[lanes, i * step : (i + 1) * step],
            (((1,), (1,)), ((), ())),
            preferred_element_type=F32,
        )
        total = got if total is None else total + got
    return total


EXP_SCALE = (D ** (-0.5)) * 1.4426950408889634


def fold(tile, op):
    return op(tile.reshape(tile.shape[0] // 8, 8, tile.shape[1]), axis=0)


def slot_stats(base, rel, slots):
    top = None
    hit = None
    for n, ref in slots:
        piece = ref[...]
        target = rel == base[n]
        found = fold(jnp.where(target, piece, 0.0), jnp.sum)
        piece = piece + jnp.where(base[n] < 0, NEG, 0.0)
        high = fold(piece, jnp.max)
        top = high if top is None else jnp.maximum(top, high)
        hit = found if hit is None else hit + found
    return jnp.max(top, axis=0, keepdims=True), jnp.sum(hit, axis=0, keepdims=True)


def slot_power(base, n, ref, top):
    piece = ref[...] + jnp.where(base[n] < 0, NEG, 0.0)
    return jnp.exp2((piece - top) * EXP_SCALE)


def relative(pos, lanes):
    line = lax.broadcasted_iota(jnp.int32, (TILE, lanes), 0)
    return pos - line


def own_kernel(group, cap, lanes, parts, base, x, pos, *refs):
    rows = [refs[s * parts : (s + 1) * parts] for s in range(group)]
    kept = refs[group * parts : group * (parts + 1)]
    top_out, sum_out, hit_out, logits, sems = refs[group * (parts + 1) :]
    count = x.shape[0]

    def copy_out(s, j):
        at = pl.ds(pl.multiple_of(j * lanes, lanes), lanes)
        return pltpu.make_async_copy(logits.at[s, :, at], kept[s].at[:, at], sems.at[s, j])

    @pl.loop(0, count // lanes)
    def _(j):
        at = pl.ds(pl.multiple_of(j * lanes, lanes), lanes)
        for s in range(group):
            logits[s, :, at] = contract(rows[s], x, at)
            copy_out(s, j).start()
        slots = [
            (s * cap + k, logits.at[s, pl.ds(k * TILE, TILE), at])
            for s in range(group)
            for k in range(cap)
        ]
        top, hit = slot_stats(base, relative(pos[:, at], lanes), slots)
        total = None
        for n, ref in slots:
            part = fold(slot_power(base, n, ref, top), jnp.sum)
            total = part if total is None else total + part
        top_out[:, at] = top
        hit_out[:, at] = hit
        sum_out[:, at] = jnp.sum(total, axis=0, keepdims=True)

    @pl.loop(0, count // lanes)
    def _(j):
        for s in range(group):
            copy_out(s, j).wait()


def own_logits(base, x, pos, rows, cap, lanes=256):
    group, parts = len(rows), len(rows[0])
    rows = [r for row in rows for r in row]
    count = x.shape[0]
    line = (1, count)
    shape = (rows[0].shape[0], count)
    return pl.pallas_call(
        functools.partial(own_kernel, group, cap, lanes, parts),
        out_shape=[pltpu.HBM(shape, F32)] * group + [jax.ShapeDtypeStruct(line, F32)] * 3,
        in_specs=[SM] + [VM] * (2 + len(rows)),
        out_specs=[FIXED] * group + [VM] * 3,
        scratch_shapes=[
            pltpu.VMEM((group,) + shape, F32),
            pltpu.SemaphoreType.DMA((group, count // lanes)),
        ],
        compiler_params=grant(12),
        name="own_logits",
    )(base, x, pos, *rows)


def far_kernel(group, cap, lanes, parts, n_stats, base, x, pos, *refs):
    stats = [refs[3 * i : 3 * i + 3] for i in range(n_stats)]
    refs = refs[3 * n_stats :]
    rows = [refs[s * parts : (s + 1) * parts] for s in range(group)]
    refs = refs[group * parts :]
    losses, top_out, inv_out = refs[:3]
    kept = refs[3:-4]
    logits, grads, tiles, sems = refs[-4:]
    count, width = x.shape
    scale = D ** (-0.5)
    for j in range(0, count, lanes):
        turn = (j // lanes) % 2
        at = pl.ds(j, lanes)
        for s in range(group):
            logits[turn, s * cap * TILE : (s + 1) * cap * TILE, :] = contract(
                rows[s], x, pl.ds(j, lanes)
            )
        slots = [
            (n, logits.at[turn, pl.ds(n * TILE, TILE), :]) for n in range(group * cap)
        ]
        rel = relative(pos[:, at], lanes)
        top, hit = slot_stats(base, rel, slots)
        both = top
        for top_own, _, _ in stats:
            both = jnp.maximum(both, top_own[:, at])
        total = None
        for n, ref in slots:
            power = slot_power(base, n, ref, both)
            ref[...] = power
            part = fold(power, jnp.sum)
            total = part if total is None else total + part
        total = jnp.sum(total, axis=0, keepdims=True)
        for top_own, sum_own, hit_own in stats:
            total = total + sum_own[:, at] * jnp.exp2((top_own[:, at] - both) * EXP_SCALE)
            hit = hit + hit_own[:, at]
        losses[:, at] = both * scale + jnp.log(total) - hit * scale
        inv = 1.0 / total
        top_out[:, at] = both
        inv_out[:, at] = inv
        for n, ref in slots:
            s, k = n // cap, n % cap
            target = jnp.where(rel == base[n], 1.0, 0.0)
            grads[s, k * TILE : (k + 1) * TILE, at] = (ref[...] * inv - target).astype(BF)
    step = width // parts
    sources = [grads.at[s] for s in range(group)]
    sources += [tiles.at[n] for n in range(parts * group)]
    copies = [pltpu.make_async_copy(a, b, sems.at[n]) for n, (a, b) in enumerate(zip(sources, kept))]
    for copy in copies[:group]:
        copy.start()
    for i in range(parts):
        for s in range(group):
            n = i * group + s
            tiles[n] = jnp.dot(
                grads[s], x[:, i * step : (i + 1) * step], preferred_element_type=F32
            ).astype(BF)
            copies[group + n].start()
    for copy in copies:
        copy.wait()


def far_grads(base, x, pos, stats, rows, cap, parts, lanes=256):
    group = len(rows)
    rows = [r for row in rows for r in row]
    count, width = x.shape
    size = rows[0].shape[0]
    outs = [((1, count), F32)] * 3 + [((size, count), BF)] * group
    outs += [((size, width // parts), BF)] * (group * parts)
    got = pl.pallas_call(
        functools.partial(far_kernel, group, cap, lanes, parts, len(stats) // 3),
        out_shape=[jax.ShapeDtypeStruct(*o) for o in outs[:3]]
        + [pltpu.HBM(*o) for o in outs[3:]],
        in_specs=[SM] + [VM] * (2 + len(stats) + len(rows)),
        out_specs=[VM] * 3 + [FIXED] * (len(outs) - 3),
        scratch_shapes=[
            pltpu.VMEM((2, group * size, lanes), F32),
            pltpu.VMEM((group, size, count), BF),
            pltpu.VMEM((group * parts, size, width // parts), BF),
            pltpu.SemaphoreType.DMA((group * (1 + parts),)),
        ],
        compiler_params=grant(20),
        name="far_grads",
    )(base, x, pos, *stats, *rows)
    tiles = got[3 + group :]
    return got[:3], got[3 : 3 + group], [tiles[i * group : (i + 1) * group] for i in range(parts)]


def own_grad_kernel(cap, parts, base, x, pos, top, inv, logits, grad, *tiles):
    count, width = x.shape
    rel = relative(pos[...], count)
    for k in range(cap):
        ref = logits.at[pl.ds(k * TILE, TILE), :]
        power = slot_power(base, k, ref, top[...])
        target = jnp.where(rel == base[k], 1.0, 0.0)
        grad[k * TILE : (k + 1) * TILE, :] = (power * inv[...] - target).astype(BF)
    step = width // parts
    for i in range(parts):
        tiles[i][...] = jnp.dot(
            grad[...], x[:, i * step : (i + 1) * step], preferred_element_type=F32
        ).astype(BF)


def own_grad(base, x, pos, top, inv, logits, cap, parts):
    count, width = x.shape
    size = logits.shape[0]
    outs = [((size, count), BF)] + [((size, width // parts), BF)] * parts
    got = pl.pallas_call(
        functools.partial(own_grad_kernel, cap, parts),
        out_shape=[jax.ShapeDtypeStruct(*o) for o in outs],
        in_specs=[SM] + [VM] * 5,
        out_specs=[VM] * len(outs),
        compiler_params=grant(6),
        name="own_grad",
    )(base, x, pos, top, inv, logits)
    return got[0], got[1:]


def design_grad_kernel(n, chunk, *refs):
    grads, rows, out = refs[:n], refs[n : 2 * n], refs[2 * n]

    @pl.loop(0, out.shape[0] // chunk)
    def _(j):
        at = pl.ds(pl.multiple_of(j * chunk, chunk), chunk)
        acc = None
        for g, r in zip(grads, rows):
            part = lax.dot_general(
                g[:, at], r[...], (((0,), (0,)), ((), ())), preferred_element_type=F32
            )
            acc = part if acc is None else acc + part
        out[at, :] = acc.astype(BF)


def design_grad(grads, rows, chunk=256):
    n = len(grads)
    return pl.pallas_call(
        functools.partial(design_grad_kernel, n, chunk),
        out_shape=jax.ShapeDtypeStruct((grads[0].shape[1], rows[0].shape[1]), BF),
        in_specs=[VM] * (2 * n),
        out_specs=VM,
        compiler_params=grant(8),
        name="design_grad",
    )(*grads, *rows)


def collect_kernel(n, cap, spot, *refs):
    parts = refs[:n]
    keep, give, acc = refs[n:]
    kept = keep.shape[0]
    acc[...] = jnp.zeros_like(acc)
    for i in range(n * cap):

        @pl.when(spot[i] >= 0)
        def _():
            s, k = i // cap, i % cap
            acc[spot[i]] += parts[s][k * TILE : (k + 1) * TILE, :].astype(F32)

    keep[...] = acc[:kept]
    give[...] = acc[kept:].astype(BF)


def collect(spot, parts, cap, kept):
    n = len(parts)
    width = parts[0].shape[1]
    shape = (kept, TILE, width)
    return pl.pallas_call(
        functools.partial(collect_kernel, n, cap),
        out_shape=[jax.ShapeDtypeStruct(shape, F32), jax.ShapeDtypeStruct(shape, BF)],
        in_specs=[SM] + [VM] * n,
        out_specs=[VM] * 2,
        scratch_shapes=[pltpu.VMEM((2 * kept, TILE, width), F32)],
        compiler_params=grant(8),
        name="collect",
    )(spot, *parts)


def body(designs, prototypes, candidates, positives):
    proto_count = lax.axis_size("proto")
    design_axis = lax.axis_size("design")
    half = proto_count // 2
    lanes = design_axis // 2
    cand_count = candidates.shape[1]
    width = designs.shape[1]
    count = designs.shape[0]
    blocks_dev = prototypes.shape[0] // TILE
    quarter = blocks_dev // design_axis
    cap = max(2, (4 * cand_count + 3 * proto_count - 1) // (3 * proto_count))
    parts = PARTS
    step = width // parts
    p = lax.axis_index("proto").astype(jnp.int32)
    d = lax.axis_index("design").astype(jnp.int32)
    q = p % half
    h = p // half
    y = d // 2
    c = d % 2
    me = d.reshape(1)
    shifts = list(range(half - 1, 0, -1))
    evens = list(range(2, half, 2))
    columns = [slice(i * step, (i + 1) * step) for i in range(parts)]

    wanted = request_table(candidates[0], blocks_dev, cap, proto_count)
    wanted = wanted.reshape(2, half, cap)
    near = [wanted[h, q ^ s] for s in range(half)]
    other = [wanted[1 - h, q ^ s] for s in range(half)]
    asking = {0: other[0]}
    for s in shifts:
        if s == 1:
            note = jnp.stack([other[1]] + [near[u ^ 1] for u in [0] + evens])
            note = xor_proto(note, 1)
            asking[1] = note[0]
            beside = {u: note[1 + n] for n, u in enumerate([0] + evens)}
        else:
            asking[s] = xor_proto(other[s], s)

    shard = prototypes.reshape(blocks_dev, TILE, width)
    mine = lax.dynamic_slice_in_dim(shard, d * quarter, quarter, axis=0).astype(BF)
    sent = {}
    for i in range(parts):
        piece = mine[:, :, columns[i]]
        for u in evens:
            sent[u, i] = xor_proto(piece, u)
        sent["far", i] = xor_proto(piece, half)

    def share(piece):
        held = [piece]
        for ys in range(1, lanes):
            held.append(xor_design(piece, 2 * ys))
        return held + [xor_design(held[ys], 1) for ys in range(lanes)]

    def flat(piece):
        return piece.reshape(cap * TILE, step)

    own_rows = [[None] * parts for _ in range(half)]
    far_rows = [[None] * parts for _ in range(half)]
    out = gather_round(beside[0], shard, parts)
    for i in range(parts):
        own_rows[1][i] = flat(xor_proto(out[i], 1))
    out = gather_round(near[0], shard, parts)
    for i in range(parts):
        own_rows[0][i] = flat(out[i])
    for i in range(parts):
        for u in evens:
            held = share(sent[u, i])
            (out,) = gather_held(me, [beside[u]], held, lanes)
            own_rows[u ^ 1][i] = flat(xor_proto(out, 1))
            (out,) = gather_held(me, [near[u]], held, lanes)
            own_rows[u][i] = flat(out)
        held = share(sent["far", i])
        outs = gather_held(me, [asking[s] for s in shifts], held, lanes)
        for s, out in zip(shifts, outs):
            far_rows[s][i] = flat(xor_proto(out, s))
        (out,) = gather_held(me, [asking[0]], held, lanes)
        far_rows[0][i] = flat(out)

    def bases(lists, which_half, group):
        out = []
        for s in group:
            first = (which_half * half + (q ^ s)) * blocks_dev
            out.append(jnp.where(lists[s] >= 0, (first + lists[s]) * TILE, -(2**30)))
        return jnp.concatenate(out)

    pos = positives.reshape(1, count)
    logits, sums = {}, []
    for group in groups_of(half).values():
        *got, top, total, hit = own_logits(
            bases(near, h, group), designs, pos, [own_rows[s] for s in group], cap
        )
        logits.update(zip(group, got))
        sums += [top, total, hit]
    stats, far_g, far_tiles = far_grads(
        bases(other, 1 - h, range(half)), designs, pos, sums, far_rows, cap, parts
    )
    losses, top, inv = stats
    own_g, own_tiles = [], []
    for s in range(half):
        g, t = own_grad(
            bases(near, h, [s]), designs, pos, top, inv, logits[s], cap, parts
        )
        own_g.append(g)
        own_tiles.append(t)

    kept = lanes * quarter

    def spots(tables):
        table = jnp.concatenate(tables)
        owner = table // quarter
        at = ((owner // 2) ^ y) * quarter + table % quarter
        at = at + jnp.where(owner % 2 == c, 0, kept)
        return jnp.where(table >= 0, at, -1)

    def reduce_shard(tables, tiles):
        keep, give = collect(spots(tables), tiles, cap, kept)
        keep = keep + xor_design(give, 1).astype(F32)
        keep = keep.reshape(lanes, quarter, TILE, step)
        total = keep[0]
        for ys in range(1, lanes):
            back = xor_design(keep[ys].astype(BF), 2 * ys)
            total = total + back.astype(F32)
        return total

    result = []
    dgrad = []
    far_tables = [asking[s] for s in range(half)]
    for i in range(parts):
        tiles = [far_tiles[i][0]]
        tiles += [xor_proto(far_tiles[i][s], s) for s in range(1, half)]
        total = reduce_shard(far_tables, tiles)
        landed = [xor_proto(total.astype(BF), half)]
        for u in evens:
            tile = xor_proto(own_tiles[u ^ 1][i], 1)
            total = reduce_shard([near[u], beside[u]], [own_tiles[u][i], tile])
            landed.append(xor_proto(total.astype(BF), u))
        tile = xor_proto(own_tiles[1][i], 1)
        total = reduce_shard([near[0], beside[0]], [own_tiles[0][i], tile])
        for piece in landed:
            total = total + piece.astype(F32)
        result.append(total)
        dgrad.append(
            design_grad(own_g + list(far_g), [r[i] for r in own_rows + far_rows])
        )
    result = jnp.concatenate(result, axis=-1).reshape(quarter * TILE, width)
    return (losses.reshape(count), jnp.concatenate(dgrad, axis=-1), result)


def groups_of(half):
    late = list(range(3, half, 2))
    return {"own_a": [s for s in range(half) if s not in late], "own_b": late}


def solution(mesh):
    return jax.shard_map(
        body,
        mesh=mesh,
        in_specs=(
            P(("proto", "design"), None),
            P("proto", None),
            P(("proto", "design"), None),
            P(("proto", "design")),
        ),
        out_specs=(
            P(("proto", "design")),
            P(("proto", "design"), None),
            P(("proto", "design"), None),
        ),
        check_vma=False,
    )
```

```python
import functools

import jax
import jax.numpy as jnp
from jax import lax
from jax.experimental import pallas as pl
from jax.experimental.pallas import tpu as pltpu
from jax.sharding import PartitionSpec as P


D = 1024
TILE = 128
BF = jnp.bfloat16
F32 = jnp.float32
NEG = -1e30
PARTS = 2


def xor_proto(x, shift):
    count = lax.axis_size("proto")
    return lax.ppermute(x, "proto", [(i, i ^ shift) for i in range(count)])


def xor_design(x, shift):
    count = lax.axis_size("design")
    return lax.ppermute(x, "design", [(i, i ^ shift) for i in range(count)])


def request_table(block_list, blocks_dev, capacity, proto_count):
    owners = block_list // blocks_dev
    local_ids = block_list % blocks_dev
    ids = jnp.arange(block_list.shape[0], dtype=jnp.int32)
    earlier = (owners[:, None] == owners[None, :]) & (ids[None, :] < ids[:, None])
    rank_of = jnp.sum(earlier.astype(jnp.int32), axis=1)
    slot_of = owners * capacity + rank_of
    slots = jnp.arange(proto_count * capacity, dtype=jnp.int32)
    hit = slot_of[None, :] == slots[:, None]
    return jnp.sum(jnp.where(hit, local_ids[None, :] + 1, 0), axis=1) - 1


HBM = pl.BlockSpec(memory_space=pl.ANY)
VM = pl.BlockSpec(memory_space=pltpu.VMEM)
SM = pl.BlockSpec(memory_space=pltpu.SMEM)
FIXED = pl.BlockSpec(memory_space=pltpu.HBM)


def grant(mib):
    return pltpu.CompilerParams(vmem_limit_bytes=mib << 20)


def gather_round_kernel(parts, table, src, *refs):
    outs, buf, sems = refs[:parts], refs[parts], refs[parts + 1]
    cap, _, step = outs[0].shape
    copies = []
    for k in range(cap):
        row = jnp.maximum(table[k], 0)
        copies.append(pltpu.make_async_copy(src.at[row], buf.at[k], sems.at[k]))
    for copy in copies:
        copy.start()
    for k, copy in enumerate(copies):
        copy.wait()
        for i in range(parts):
            outs[i][k] = buf[k, :, i * step : (i + 1) * step].astype(BF)


def gather_round(table, shard, parts):
    cap = table.shape[0]
    _, tile, width = shard.shape
    return pl.pallas_call(
        functools.partial(gather_round_kernel, parts),
        out_shape=[jax.ShapeDtypeStruct((cap, tile, width // parts), BF)] * parts,
        in_specs=[SM, FIXED],
        out_specs=[VM] * parts,
        scratch_shapes=[
            pltpu.VMEM((cap, tile, width), F32),
            pltpu.SemaphoreType.DMA((cap,)),
        ],
        compiler_params=grant(6),
        name="gather_round",
    )(table, shard)


def gather_held_kernel(n_src, n_out, quarter, lanes, me, *refs):
    tables, srcs = refs[:n_out], refs[n_out : n_out + n_src]
    outs, sems = refs[n_out + n_src : -1], refs[-1]
    cap = outs[0].shape[0]
    y, c = me[0] // 2, me[0] % 2
    for n in range(n_out):

        @pl.loop(0, cap)
        def _(k):
            row = jnp.maximum(tables[n][k], 0)
            owner, inside = row // quarter, row % quarter
            which = ((owner % 2) ^ c) * lanes + ((owner // 2) ^ y)
            for a in range(n_src):

                @pl.when(which == a)
                def _():
                    pltpu.make_async_copy(
                        srcs[a].at[inside], outs[n].at[k], sems.at[n * cap + k]
                    ).start()

    for n in range(n_out):

        @pl.loop(0, cap)
        def _(k):
            pltpu.make_async_copy(srcs[0].at[0], outs[n].at[k], sems.at[n * cap + k]).wait()


def gather_held(me, tables, srcs, lanes):
    n = len(tables)
    cap = tables[0].shape[0]
    quarter = srcs[0].shape[0]
    shape = (cap,) + srcs[0].shape[1:]
    return pl.pallas_call(
        functools.partial(gather_held_kernel, len(srcs), n, quarter, lanes),
        out_shape=[jax.ShapeDtypeStruct(shape, BF)] * n,
        in_specs=[SM] * (n + 1) + [HBM] * len(srcs),
        out_specs=[VM] * n,
        scratch_shapes=[pltpu.SemaphoreType.DMA((n * cap,))],
        compiler_params=grant(2),
        name="gather_held",
    )(me, *tables, *srcs)


def contract(rows, x, lanes):
    step = rows[0].shape[1]
    total = None
    for i, part in enumerate(rows):
        got = lax.dot_general(
            part[...],
            x[lanes, i * step : (i + 1) * step],
            (((1,), (1,)), ((), ())),
            preferred_element_type=F32,
        )
        total = got if total is None else total + got
    return total


EXP_SCALE = (D ** (-0.5)) * 1.4426950408889634


def fold(tile, op):
    return op(tile.reshape(tile.shape[0] // 8, 8, tile.shape[1]), axis=0)


def slot_stats(base, rel, slots):
    top = None
    hit = None
    for n, ref in slots:
        piece = ref[...]
        target = rel == base[n]
        found = fold(jnp.where(target, piece, 0.0), jnp.sum)
        piece = piece + jnp.where(base[n] < 0, NEG, 0.0)
        high = fold(piece, jnp.max)
        top = high if top is None else jnp.maximum(top, high)
        hit = found if hit is None else hit + found
    return jnp.max(top, axis=0, keepdims=True), jnp.sum(hit, axis=0, keepdims=True)


def slot_power(base, n, ref, top):
    piece = ref[...] + jnp.where(base[n] < 0, NEG, 0.0)
    return jnp.exp2((piece - top) * EXP_SCALE)


def relative(pos, lanes):
    line = lax.broadcasted_iota(jnp.int32, (TILE, lanes), 0)
    return pos - line


def own_kernel(group, cap, lanes, parts, base, x, pos, *refs):
    rows = [refs[s * parts : (s + 1) * parts] for s in range(group)]
    kept = refs[group * parts : group * (parts + 1)]
    top_out, sum_out, hit_out, logits, sems = refs[group * (parts + 1) :]
    count = x.shape[0]

    def copy_out(s, j):
        at = pl.ds(pl.multiple_of(j * lanes, lanes), lanes)
        return pltpu.make_async_copy(logits.at[s, :, at], kept[s].at[:, at], sems.at[s, j])

    @pl.loop(0, count // lanes)
    def _(j):
        at = pl.ds(pl.multiple_of(j * lanes, lanes), lanes)
        for s in range(group):
            logits[s, :, at] = contract(rows[s], x, at)
            copy_out(s, j).start()
        slots = [
            (s * cap + k, logits.at[s, pl.ds(k * TILE, TILE), at])
            for s in range(group)
            for k in range(cap)
        ]
        top, hit = slot_stats(base, relative(pos[:, at], lanes), slots)
        total = None
        for n, ref in slots:
            part = fold(slot_power(base, n, ref, top), jnp.sum)
            total = part if total is None else total + part
        top_out[:, at] = top
        hit_out[:, at] = hit
        sum_out[:, at] = jnp.sum(total, axis=0, keepdims=True)

    @pl.loop(0, count // lanes)
    def _(j):
        for s in range(group):
            copy_out(s, j).wait()


def own_logits(base, x, pos, rows, cap, lanes=256):
    group, parts = len(rows), len(rows[0])
    rows = [r for row in rows for r in row]
    count = x.shape[0]
    line = (1, count)
    shape = (rows[0].shape[0], count)
    return pl.pallas_call(
        functools.partial(own_kernel, group, cap, lanes, parts),
        out_shape=[pltpu.HBM(shape, F32)] * group + [jax.ShapeDtypeStruct(line, F32)] * 3,
        in_specs=[SM] + [VM] * (2 + len(rows)),
        out_specs=[FIXED] * group + [VM] * 3,
        scratch_shapes=[
            pltpu.VMEM((group,) + shape, F32),
            pltpu.SemaphoreType.DMA((group, count // lanes)),
        ],
        compiler_params=grant(12),
        name="own_logits",
    )(base, x, pos, *rows)


def far_kernel(group, cap, lanes, parts, n_stats, base, x, pos, *refs):
    stats = [refs[3 * i : 3 * i + 3] for i in range(n_stats)]
    refs = refs[3 * n_stats :]
    rows = [refs[s * parts : (s + 1) * parts] for s in range(group)]
    refs = refs[group * parts :]
    losses, top_out, inv_out = refs[:3]
    kept = refs[3:-4]
    logits, grads, tiles, sems = refs[-4:]
    count, width = x.shape
    scale = D ** (-0.5)
    for j in range(0, count, lanes):
        turn = (j // lanes) % 2
        at = pl.ds(j, lanes)
        for s in range(group):
            logits[turn, s * cap * TILE : (s + 1) * cap * TILE, :] = contract(
                rows[s], x, pl.ds(j, lanes)
            )
        slots = [
            (n, logits.at[turn, pl.ds(n * TILE, TILE), :]) for n in range(group * cap)
        ]
        rel = relative(pos[:, at], lanes)
        top, hit = slot_stats(base, rel, slots)
        both = top
        for top_own, _, _ in stats:
            both = jnp.maximum(both, top_own[:, at])
        total = None
        for n, ref in slots:
            power = slot_power(base, n, ref, both)
            ref[...] = power
            part = fold(power, jnp.sum)
            total = part if total is None else total + part
        total = jnp.sum(total, axis=0, keepdims=True)
        for top_own, sum_own, hit_own in stats:
            total = total + sum_own[:, at] * jnp.exp2((top_own[:, at] - both) * EXP_SCALE)
            hit = hit + hit_own[:, at]
        losses[:, at] = both * scale + jnp.log(total) - hit * scale
        inv = 1.0 / total
        top_out[:, at] = both
        inv_out[:, at] = inv
        for n, ref in slots:
            s, k = n // cap, n % cap
            target = jnp.where(rel == base[n], 1.0, 0.0)
            grads[s, k * TILE : (k + 1) * TILE, at] = (ref[...] * inv - target).astype(BF)
    step = width // parts
    sources = [grads.at[s] for s in range(group)] + [tiles.at[s] for s in range(group)]
    copies = [
        pltpu.make_async_copy(a, b, sems.at[n]) for n, (a, b) in enumerate(zip(sources, kept))
    ]
    for copy in copies[:group]:
        copy.start()
    for s in reversed(range(group)):
        tiles[s] = jnp.dot(grads[s], x[:, :step], preferred_element_type=F32).astype(BF)
        copies[group + s].start()
    for copy in copies:
        copy.wait()


def far_grads(base, x, pos, stats, rows, cap, parts, lanes=256):
    group = len(rows)
    rows = [r for row in rows for r in row]
    count, width = x.shape
    size = rows[0].shape[0]
    outs = [((1, count), F32)] * 3 + [((size, count), BF)] * group
    outs += [((size, width // parts), BF)] * group
    got = pl.pallas_call(
        functools.partial(far_kernel, group, cap, lanes, parts, len(stats) // 3),
        out_shape=[jax.ShapeDtypeStruct(*o) for o in outs[:3]]
        + [pltpu.HBM(*o) for o in outs[3:]],
        in_specs=[SM] + [VM] * (2 + len(stats) + len(rows)),
        out_specs=[VM] * 3 + [FIXED] * (len(outs) - 3),
        scratch_shapes=[
            pltpu.VMEM((2, group * size, lanes), F32),
            pltpu.VMEM((group, size, count), BF),
            pltpu.VMEM((group, size, width // parts), BF),
            pltpu.SemaphoreType.DMA((2 * group,)),
        ],
        compiler_params=grant(20),
        name="far_grads",
    )(base, x, pos, *stats, *rows)
    return got[:3], got[3 : 3 + group], got[3 + group :]


def far_tiles_kernel(group, first, x, *refs):
    grads, tiles = refs[:group], refs[group:]
    step = tiles[0].shape[1]
    for n, tile in enumerate(tiles):
        i = first + n // group
        tile[...] = jnp.dot(
            grads[n % group][...], x[:, i * step : (i + 1) * step], preferred_element_type=F32
        ).astype(BF)


def far_tiles(x, grads, parts):
    group = len(grads)
    shape = (grads[0].shape[0], x.shape[1] // parts)
    got = pl.pallas_call(
        functools.partial(far_tiles_kernel, group, 1),
        out_shape=[jax.ShapeDtypeStruct(shape, BF)] * (group * (parts - 1)),
        in_specs=[VM] * (1 + group),
        out_specs=[VM] * (group * (parts - 1)),
        compiler_params=grant(6),
        name="far_tiles",
    )(x, *grads)
    return [got[i : i + group] for i in range(0, len(got), group)]


def own_grad_kernel(cap, parts, base, x, pos, top, inv, logits, grad, *tiles):
    count, width = x.shape
    rel = relative(pos[...], count)
    for k in range(cap):
        ref = logits.at[pl.ds(k * TILE, TILE), :]
        power = slot_power(base, k, ref, top[...])
        target = jnp.where(rel == base[k], 1.0, 0.0)
        grad[k * TILE : (k + 1) * TILE, :] = (power * inv[...] - target).astype(BF)
    step = width // parts
    for i in range(parts):
        tiles[i][...] = jnp.dot(
            grad[...], x[:, i * step : (i + 1) * step], preferred_element_type=F32
        ).astype(BF)


def own_grad(base, x, pos, top, inv, logits, cap, parts):
    count, width = x.shape
    size = logits.shape[0]
    outs = [((size, count), BF)] + [((size, width // parts), BF)] * parts
    got = pl.pallas_call(
        functools.partial(own_grad_kernel, cap, parts),
        out_shape=[jax.ShapeDtypeStruct(*o) for o in outs],
        in_specs=[SM] + [VM] * 5,
        out_specs=[VM] * len(outs),
        compiler_params=grant(6),
        name="own_grad",
    )(base, x, pos, top, inv, logits)
    return got[0], got[1:]


def design_grad_kernel(n, chunk, *refs):
    grads, rows, out = refs[:n], refs[n : 2 * n], refs[2 * n]

    @pl.loop(0, out.shape[0] // chunk)
    def _(j):
        at = pl.ds(pl.multiple_of(j * chunk, chunk), chunk)
        acc = None
        for g, r in zip(grads, rows):
            part = lax.dot_general(
                g[:, at], r[...], (((0,), (0,)), ((), ())), preferred_element_type=F32
            )
            acc = part if acc is None else acc + part
        out[at, :] = acc.astype(BF)


def design_grad(grads, rows, chunk=256):
    n = len(grads)
    return pl.pallas_call(
        functools.partial(design_grad_kernel, n, chunk),
        out_shape=jax.ShapeDtypeStruct((grads[0].shape[1], rows[0].shape[1]), BF),
        in_specs=[VM] * (2 * n),
        out_specs=VM,
        compiler_params=grant(8),
        name="design_grad",
    )(*grads, *rows)


def collect_kernel(n, cap, spot, *refs):
    parts = refs[:n]
    keep, give, acc = refs[n:]
    kept = keep.shape[0]
    acc[...] = jnp.zeros_like(acc)
    for i in range(n * cap):

        @pl.when(spot[i] >= 0)
        def _():
            s, k = i // cap, i % cap
            acc[spot[i]] += parts[s][k * TILE : (k + 1) * TILE, :].astype(F32)

    keep[...] = acc[:kept]
    give[...] = acc[kept:].astype(BF)


def collect(spot, parts, cap, kept):
    n = len(parts)
    width = parts[0].shape[1]
    shape = (kept, TILE, width)
    return pl.pallas_call(
        functools.partial(collect_kernel, n, cap),
        out_shape=[jax.ShapeDtypeStruct(shape, F32), jax.ShapeDtypeStruct(shape, BF)],
        in_specs=[SM] + [VM] * n,
        out_specs=[VM] * 2,
        scratch_shapes=[pltpu.VMEM((2 * kept, TILE, width), F32)],
        compiler_params=grant(8),
        name="collect",
    )(spot, *parts)


def body(designs, prototypes, candidates, positives):
    proto_count = lax.axis_size("proto")
    design_axis = lax.axis_size("design")
    half = proto_count // 2
    lanes = design_axis // 2
    cand_count = candidates.shape[1]
    width = designs.shape[1]
    count = designs.shape[0]
    blocks_dev = prototypes.shape[0] // TILE
    quarter = blocks_dev // design_axis
    cap = max(2, (4 * cand_count + 3 * proto_count - 1) // (3 * proto_count))
    parts = PARTS
    step = width // parts
    p = lax.axis_index("proto").astype(jnp.int32)
    d = lax.axis_index("design").astype(jnp.int32)
    q = p % half
    h = p // half
    y = d // 2
    c = d % 2
    me = d.reshape(1)
    shifts = list(range(half - 1, 0, -1))
    evens = list(range(2, half, 2))
    columns = [slice(i * step, (i + 1) * step) for i in range(parts)]

    wanted = request_table(candidates[0], blocks_dev, cap, proto_count)
    wanted = wanted.reshape(2, half, cap)
    near = [wanted[h, q ^ s] for s in range(half)]
    other = [wanted[1 - h, q ^ s] for s in range(half)]
    asking = {0: other[0]}
    for s in shifts:
        if s == 1:
            note = jnp.stack([other[1]] + [near[u ^ 1] for u in [0] + evens])
            note = xor_proto(note, 1)
            asking[1] = note[0]
            beside = {u: note[1 + n] for n, u in enumerate([0] + evens)}
        else:
            asking[s] = xor_proto(other[s], s)

    shard = prototypes.reshape(blocks_dev, TILE, width)
    mine = lax.dynamic_slice_in_dim(shard, d * quarter, quarter, axis=0).astype(BF)
    sent = {}
    for i in range(parts):
        piece = mine[:, :, columns[i]]
        for u in evens:
            sent[u, i] = xor_proto(piece, u)
        sent["far", i] = xor_proto(piece, half)

    def share(piece):
        held = [piece]
        for ys in range(1, lanes):
            held.append(xor_design(piece, 2 * ys))
        return held + [xor_design(held[ys], 1) for ys in range(lanes)]

    def flat(piece):
        return piece.reshape(cap * TILE, step)

    own_rows = [[None] * parts for _ in range(half)]
    far_rows = [[None] * parts for _ in range(half)]
    out = gather_round(beside[0], shard, parts)
    for i in range(parts):
        own_rows[1][i] = flat(xor_proto(out[i], 1))
    out = gather_round(near[0], shard, parts)
    for i in range(parts):
        own_rows[0][i] = flat(out[i])
    for i in range(parts):
        for u in evens:
            held = share(sent[u, i])
            (out,) = gather_held(me, [beside[u]], held, lanes)
            own_rows[u ^ 1][i] = flat(xor_proto(out, 1))
            (out,) = gather_held(me, [near[u]], held, lanes)
            own_rows[u][i] = flat(out)
        held = share(sent["far", i])
        outs = gather_held(me, [asking[s] for s in shifts], held, lanes)
        for s, out in zip(shifts, outs):
            far_rows[s][i] = flat(xor_proto(out, s))
        (out,) = gather_held(me, [asking[0]], held, lanes)
        far_rows[0][i] = flat(out)

    def bases(lists, which_half, group):
        out = []
        for s in group:
            first = (which_half * half + (q ^ s)) * blocks_dev
            out.append(jnp.where(lists[s] >= 0, (first + lists[s]) * TILE, -(2**30)))
        return jnp.concatenate(out)

    pos = positives.reshape(1, count)
    logits, sums = {}, []
    for group in groups_of(half).values():
        *got, top, total, hit = own_logits(
            bases(near, h, group), designs, pos, [own_rows[s] for s in group], cap
        )
        logits.update(zip(group, got))
        sums += [top, total, hit]
    stats, far_g, first = far_grads(
        bases(other, 1 - h, range(half)), designs, pos, sums, far_rows, cap, parts
    )
    back_tiles = [first] + far_tiles(designs, far_g, parts)
    losses, top, inv = stats
    own_g, own_tiles = [], []
    for s in range(half):
        g, t = own_grad(
            bases(near, h, [s]), designs, pos, top, inv, logits[s], cap, parts
        )
        own_g.append(g)
        own_tiles.append(t)

    kept = lanes * quarter

    def spots(tables):
        table = jnp.concatenate(tables)
        owner = table // quarter
        at = ((owner // 2) ^ y) * quarter + table % quarter
        at = at + jnp.where(owner % 2 == c, 0, kept)
        return jnp.where(table >= 0, at, -1)

    def reduce_shard(tables, tiles):
        keep, give = collect(spots(tables), tiles, cap, kept)
        keep = keep + xor_design(give, 1).astype(F32)
        keep = keep.reshape(lanes, quarter, TILE, step)
        total = keep[0]
        for ys in range(1, lanes):
            back = xor_design(keep[ys].astype(BF), 2 * ys)
            total = total + back.astype(F32)
        return total

    result = []
    dgrad = []
    far_tables = [asking[s] for s in range(half)]
    for i in range(parts):
        tiles = [back_tiles[i][0]]
        tiles += [xor_proto(back_tiles[i][s], s) for s in range(1, half)]
        total = reduce_shard(far_tables, tiles)
        landed = [xor_proto(total.astype(BF), half)]
        for u in evens:
            tile = xor_proto(own_tiles[u ^ 1][i], 1)
            total = reduce_shard([near[u], beside[u]], [own_tiles[u][i], tile])
            landed.append(xor_proto(total.astype(BF), u))
        tile = xor_proto(own_tiles[1][i], 1)
        total = reduce_shard([near[0], beside[0]], [own_tiles[0][i], tile])
        for piece in landed:
            total = total + piece.astype(F32)
        result.append(total)
        dgrad.append(
            design_grad(own_g + list(far_g), [r[i] for r in own_rows + far_rows])
        )
    result = jnp.concatenate(result, axis=-1).reshape(quarter * TILE, width)
    return (losses.reshape(count), jnp.concatenate(dgrad, axis=-1), result)


def groups_of(half):
    late = list(range(3, half, 2))
    return {"own_a": [s for s in range(half) if s not in late], "own_b": late}


def solution(mesh):
    return jax.shard_map(
        body,
        mesh=mesh,
        in_specs=(
            P(("proto", "design"), None),
            P("proto", None),
            P(("proto", "design"), None),
            P(("proto", "design")),
        ),
        out_specs=(
            P(("proto", "design")),
            P(("proto", "design"), None),
            P(("proto", "design"), None),
        ),
        check_vma=False,
    )
```

```python
import functools

import jax
import jax.numpy as jnp
from jax import lax
from jax.experimental import pallas as pl
from jax.experimental.pallas import tpu as pltpu
from jax.sharding import PartitionSpec as P


D = 1024
TILE = 128
BF = jnp.bfloat16
F32 = jnp.float32
NEG = -1e30
PARTS = 2


def xor_proto(x, shift):
    count = lax.axis_size("proto")
    return lax.ppermute(x, "proto", [(i, i ^ shift) for i in range(count)])


def xor_design(x, shift):
    count = lax.axis_size("design")
    return lax.ppermute(x, "design", [(i, i ^ shift) for i in range(count)])


def request_table(block_list, blocks_dev, capacity, proto_count):
    owners = block_list // blocks_dev
    local_ids = block_list % blocks_dev
    ids = jnp.arange(block_list.shape[0], dtype=jnp.int32)
    earlier = (owners[:, None] == owners[None, :]) & (ids[None, :] < ids[:, None])
    rank_of = jnp.sum(earlier.astype(jnp.int32), axis=1)
    slot_of = owners * capacity + rank_of
    slots = jnp.arange(proto_count * capacity, dtype=jnp.int32)
    hit = slot_of[None, :] == slots[:, None]
    return jnp.sum(jnp.where(hit, local_ids[None, :] + 1, 0), axis=1) - 1


HBM = pl.BlockSpec(memory_space=pl.ANY)
VM = pl.BlockSpec(memory_space=pltpu.VMEM)
SM = pl.BlockSpec(memory_space=pltpu.SMEM)
FIXED = pl.BlockSpec(memory_space=pltpu.HBM)


def grant(mib):
    return pltpu.CompilerParams(vmem_limit_bytes=mib << 20)


def gather_round_kernel(parts, table, src, *refs):
    outs, buf, sems = refs[:parts], refs[parts], refs[parts + 1]
    cap, _, step = outs[0].shape
    copies = []
    for k in range(cap):
        row = jnp.maximum(table[k], 0)
        copies.append(pltpu.make_async_copy(src.at[row], buf.at[k], sems.at[k]))
    for copy in copies:
        copy.start()
    for k, copy in enumerate(copies):
        copy.wait()
        for i in range(parts):
            outs[i][k] = buf[k, :, i * step : (i + 1) * step].astype(BF)


def gather_round(table, shard, parts):
    cap = table.shape[0]
    _, tile, width = shard.shape
    return pl.pallas_call(
        functools.partial(gather_round_kernel, parts),
        out_shape=[jax.ShapeDtypeStruct((cap, tile, width // parts), BF)] * parts,
        in_specs=[SM, FIXED],
        out_specs=[VM] * parts,
        scratch_shapes=[
            pltpu.VMEM((cap, tile, width), F32),
            pltpu.SemaphoreType.DMA((cap,)),
        ],
        compiler_params=grant(6),
        name="gather_round",
    )(table, shard)


def gather_held_kernel(n_src, n_out, quarter, lanes, me, *refs):
    tables, srcs = refs[:n_out], refs[n_out : n_out + n_src]
    outs, sems = refs[n_out + n_src : -1], refs[-1]
    cap = outs[0].shape[0]
    y, c = me[0] // 2, me[0] % 2
    for n in range(n_out):

        @pl.loop(0, cap)
        def _(k):
            row = jnp.maximum(tables[n][k], 0)
            owner, inside = row // quarter, row % quarter
            which = ((owner % 2) ^ c) * lanes + ((owner // 2) ^ y)
            for a in range(n_src):

                @pl.when(which == a)
                def _():
                    pltpu.make_async_copy(
                        srcs[a].at[inside], outs[n].at[k], sems.at[n * cap + k]
                    ).start()

    for n in range(n_out):

        @pl.loop(0, cap)
        def _(k):
            pltpu.make_async_copy(srcs[0].at[0], outs[n].at[k], sems.at[n * cap + k]).wait()


def gather_held(me, tables, srcs, lanes):
    n = len(tables)
    cap = tables[0].shape[0]
    quarter = srcs[0].shape[0]
    shape = (cap,) + srcs[0].shape[1:]
    return pl.pallas_call(
        functools.partial(gather_held_kernel, len(srcs), n, quarter, lanes),
        out_shape=[jax.ShapeDtypeStruct(shape, BF)] * n,
        in_specs=[SM] * (n + 1) + [HBM] * len(srcs),
        out_specs=[VM] * n,
        scratch_shapes=[pltpu.SemaphoreType.DMA((n * cap,))],
        compiler_params=grant(2),
        name="gather_held",
    )(me, *tables, *srcs)


def contract(rows, x, lanes):
    step = rows[0].shape[1]
    total = None
    for i, part in enumerate(rows):
        got = lax.dot_general(
            part[...],
            x[lanes, i * step : (i + 1) * step],
            (((1,), (1,)), ((), ())),
            preferred_element_type=F32,
        )
        total = got if total is None else total + got
    return total


EXP_SCALE = (D ** (-0.5)) * 1.4426950408889634


def fold(tile, op):
    return op(tile.reshape(tile.shape[0] // 8, 8, tile.shape[1]), axis=0)


def slot_stats(base, rel, slots):
    top = None
    hit = None
    for n, ref in slots:
        piece = ref[...]
        target = rel == base[n]
        found = fold(jnp.where(target, piece, 0.0), jnp.sum)
        piece = piece + jnp.where(base[n] < 0, NEG, 0.0)
        high = fold(piece, jnp.max)
        top = high if top is None else jnp.maximum(top, high)
        hit = found if hit is None else hit + found
    return jnp.max(top, axis=0, keepdims=True), jnp.sum(hit, axis=0, keepdims=True)


def slot_power(base, n, ref, top):
    piece = ref[...] + jnp.where(base[n] < 0, NEG, 0.0)
    return jnp.exp2((piece - top) * EXP_SCALE)


def relative(pos, lanes):
    line = lax.broadcasted_iota(jnp.int32, (TILE, lanes), 0)
    return pos - line


def own_kernel(group, cap, lanes, parts, base, x, pos, *refs):
    rows = [refs[s * parts : (s + 1) * parts] for s in range(group)]
    kept = refs[group * parts : group * (parts + 1)]
    top_out, sum_out, hit_out, logits, sems = refs[group * (parts + 1) :]
    count = x.shape[0]

    def copy_out(s, j):
        at = pl.ds(pl.multiple_of(j * lanes, lanes), lanes)
        return pltpu.make_async_copy(logits.at[s, :, at], kept[s].at[:, at], sems.at[s, j])

    @pl.loop(0, count // lanes)
    def _(j):
        at = pl.ds(pl.multiple_of(j * lanes, lanes), lanes)
        for s in range(group):
            logits[s, :, at] = contract(rows[s], x, at)
            copy_out(s, j).start()
        slots = [
            (s * cap + k, logits.at[s, pl.ds(k * TILE, TILE), at])
            for s in range(group)
            for k in range(cap)
        ]
        top, hit = slot_stats(base, relative(pos[:, at], lanes), slots)
        total = None
        for n, ref in slots:
            part = fold(slot_power(base, n, ref, top), jnp.sum)
            total = part if total is None else total + part
        top_out[:, at] = top
        hit_out[:, at] = hit
        sum_out[:, at] = jnp.sum(total, axis=0, keepdims=True)

    @pl.loop(0, count // lanes)
    def _(j):
        for s in range(group):
            copy_out(s, j).wait()


def own_logits(base, x, pos, rows, cap, lanes=256):
    group, parts = len(rows), len(rows[0])
    rows = [r for row in rows for r in row]
    count = x.shape[0]
    line = (1, count)
    shape = (rows[0].shape[0], count)
    return pl.pallas_call(
        functools.partial(own_kernel, group, cap, lanes, parts),
        out_shape=[pltpu.HBM(shape, F32)] * group + [jax.ShapeDtypeStruct(line, F32)] * 3,
        in_specs=[SM] + [VM] * (2 + len(rows)),
        out_specs=[FIXED] * group + [VM] * 3,
        scratch_shapes=[
            pltpu.VMEM((group,) + shape, F32),
            pltpu.SemaphoreType.DMA((group, count // lanes)),
        ],
        compiler_params=grant(12),
        name="own_logits",
    )(base, x, pos, *rows)


def far_kernel(group, cap, lanes, parts, n_stats, base, x, pos, *refs):
    stats = [refs[3 * i : 3 * i + 3] for i in range(n_stats)]
    refs = refs[3 * n_stats :]
    rows = [refs[s * parts : (s + 1) * parts] for s in range(group)]
    refs = refs[group * parts :]
    losses, top_out, inv_out = refs[:3]
    kept = refs[3:-4]
    logits, grads, tiles, sems = refs[-4:]
    count, width = x.shape
    scale = D ** (-0.5)
    for j in range(0, count, lanes):
        turn = (j // lanes) % 2
        at = pl.ds(j, lanes)
        for s in range(group):
            logits[turn, s * cap * TILE : (s + 1) * cap * TILE, :] = contract(
                rows[s], x, pl.ds(j, lanes)
            )
        slots = [
            (n, logits.at[turn, pl.ds(n * TILE, TILE), :]) for n in range(group * cap)
        ]
        rel = relative(pos[:, at], lanes)
        top, hit = slot_stats(base, rel, slots)
        both = top
        for top_own, _, _ in stats:
            both = jnp.maximum(both, top_own[:, at])
        total = None
        for n, ref in slots:
            power = slot_power(base, n, ref, both)
            ref[...] = power
            part = fold(power, jnp.sum)
            total = part if total is None else total + part
        total = jnp.sum(total, axis=0, keepdims=True)
        for top_own, sum_own, hit_own in stats:
            total = total + sum_own[:, at] * jnp.exp2((top_own[:, at] - both) * EXP_SCALE)
            hit = hit + hit_own[:, at]
        losses[:, at] = both * scale + jnp.log(total) - hit * scale
        inv = 1.0 / total
        top_out[:, at] = both
        inv_out[:, at] = inv
        for n, ref in slots:
            s, k = n // cap, n % cap
            target = jnp.where(rel == base[n], 1.0, 0.0)
            grads[s, k * TILE : (k + 1) * TILE, at] = (ref[...] * inv - target).astype(BF)
    step = width // parts
    sources = [grads.at[s] for s in range(group)] + [tiles.at[s] for s in range(group)]
    copies = [
        pltpu.make_async_copy(a, b, sems.at[n]) for n, (a, b) in enumerate(zip(sources, kept))
    ]
    for copy in copies[:group]:
        copy.start()
    for s in reversed(range(group)):
        tiles[s] = jnp.dot(grads[s], x[:, :step], preferred_element_type=F32).astype(BF)
        copies[group + s].start()
    for copy in copies:
        copy.wait()


def far_grads(base, x, pos, stats, rows, cap, parts, lanes=256):
    group = len(rows)
    rows = [r for row in rows for r in row]
    count, width = x.shape
    size = rows[0].shape[0]
    outs = [((1, count), F32)] * 3 + [((size, count), BF)] * group
    outs += [((size, width // parts), BF)] * group
    got = pl.pallas_call(
        functools.partial(far_kernel, group, cap, lanes, parts, len(stats) // 3),
        out_shape=[jax.ShapeDtypeStruct(*o) for o in outs[:3]]
        + [pltpu.HBM(*o) for o in outs[3:]],
        in_specs=[SM] + [VM] * (2 + len(stats) + len(rows)),
        out_specs=[VM] * 3 + [FIXED] * (len(outs) - 3),
        scratch_shapes=[
            pltpu.VMEM((2, group * size, lanes), F32),
            pltpu.VMEM((group, size, count), BF),
            pltpu.VMEM((group, size, width // parts), BF),
            pltpu.SemaphoreType.DMA((2 * group,)),
        ],
        compiler_params=grant(20),
        name="far_grads",
    )(base, x, pos, *stats, *rows)
    return got[:3], got[3 : 3 + group], got[3 + group :]


def far_tiles_kernel(group, first, x, *refs):
    grads, tiles = refs[:group], refs[group:]
    step = tiles[0].shape[1]
    for n, tile in enumerate(tiles):
        i = first + n // group
        tile[...] = jnp.dot(
            grads[n % group][...], x[:, i * step : (i + 1) * step], preferred_element_type=F32
        ).astype(BF)


def far_tiles(x, grads, parts):
    group = len(grads)
    shape = (grads[0].shape[0], x.shape[1] // parts)
    got = pl.pallas_call(
        functools.partial(far_tiles_kernel, group, 1),
        out_shape=[jax.ShapeDtypeStruct(shape, BF)] * (group * (parts - 1)),
        in_specs=[VM] * (1 + group),
        out_specs=[VM] * (group * (parts - 1)),
        compiler_params=grant(6),
        name="far_tiles",
    )(x, *grads)
    return [got[i : i + group] for i in range(0, len(got), group)]


def own_grad_kernel(cap, parts, base, x, pos, top, inv, logits, grad, *tiles):
    count, width = x.shape
    rel = relative(pos[...], count)
    for k in range(cap):
        ref = logits.at[pl.ds(k * TILE, TILE), :]
        power = slot_power(base, k, ref, top[...])
        target = jnp.where(rel == base[k], 1.0, 0.0)
        grad[k * TILE : (k + 1) * TILE, :] = (power * inv[...] - target).astype(BF)
    step = width // parts
    for i in range(parts):
        tiles[i][...] = jnp.dot(
            grad[...], x[:, i * step : (i + 1) * step], preferred_element_type=F32
        ).astype(BF)


def own_grad(base, x, pos, top, inv, logits, cap, parts):
    count, width = x.shape
    size = logits.shape[0]
    outs = [((size, count), BF)] + [((size, width // parts), BF)] * parts
    got = pl.pallas_call(
        functools.partial(own_grad_kernel, cap, parts),
        out_shape=[jax.ShapeDtypeStruct(*o) for o in outs],
        in_specs=[SM] + [VM] * 5,
        out_specs=[VM] * len(outs),
        compiler_params=grant(6),
        name="own_grad",
    )(base, x, pos, top, inv, logits)
    return got[0], got[1:]


def design_grad_kernel(n, chunk, *refs):
    grads, rows, out = refs[:n], refs[n : 2 * n], refs[2 * n]

    @pl.loop(0, out.shape[0] // chunk)
    def _(j):
        at = pl.ds(pl.multiple_of(j * chunk, chunk), chunk)
        acc = None
        for g, r in zip(grads, rows):
            part = lax.dot_general(
                g[:, at], r[...], (((0,), (0,)), ((), ())), preferred_element_type=F32
            )
            acc = part if acc is None else acc + part
        out[at, :] = acc.astype(BF)


def design_grad(grads, rows, chunk=256):
    n = len(grads)
    return pl.pallas_call(
        functools.partial(design_grad_kernel, n, chunk),
        out_shape=jax.ShapeDtypeStruct((grads[0].shape[1], rows[0].shape[1]), BF),
        in_specs=[VM] * (2 * n),
        out_specs=VM,
        compiler_params=grant(8),
        name="design_grad",
    )(*grads, *rows)


def collect_kernel(n, cap, spot, *refs):
    parts = refs[:n]
    keep, give, acc = refs[n:]
    kept = keep.shape[0]
    acc[...] = jnp.zeros_like(acc)
    for i in range(n * cap):

        @pl.when(spot[i] >= 0)
        def _():
            s, k = i // cap, i % cap
            acc[spot[i]] += parts[s][k * TILE : (k + 1) * TILE, :].astype(F32)

    keep[...] = acc[:kept]
    give[...] = acc[kept:].astype(BF)


def collect(spot, parts, cap, kept):
    n = len(parts)
    width = parts[0].shape[1]
    shape = (kept, TILE, width)
    return pl.pallas_call(
        functools.partial(collect_kernel, n, cap),
        out_shape=[jax.ShapeDtypeStruct(shape, F32), jax.ShapeDtypeStruct(shape, BF)],
        in_specs=[SM] + [VM] * n,
        out_specs=[VM] * 2,
        scratch_shapes=[pltpu.VMEM((2 * kept, TILE, width), F32)],
        compiler_params=grant(8),
        name="collect",
    )(spot, *parts)


def body(designs, prototypes, candidates, positives):
    proto_count = lax.axis_size("proto")
    design_axis = lax.axis_size("design")
    half = proto_count // 2
    lanes = design_axis // 2
    cand_count = candidates.shape[1]
    width = designs.shape[1]
    count = designs.shape[0]
    blocks_dev = prototypes.shape[0] // TILE
    quarter = blocks_dev // design_axis
    cap = max(2, (4 * cand_count + 3 * proto_count - 1) // (3 * proto_count))
    parts = PARTS
    step = width // parts
    p = lax.axis_index("proto").astype(jnp.int32)
    d = lax.axis_index("design").astype(jnp.int32)
    q = p % half
    h = p // half
    y = d // 2
    c = d % 2
    me = d.reshape(1)
    shifts = list(range(half - 1, 0, -1))
    evens = list(range(2, half, 2))
    columns = [slice(i * step, (i + 1) * step) for i in range(parts)]

    wanted = request_table(candidates[0], blocks_dev, cap, proto_count)
    wanted = wanted.reshape(2, half, cap)
    near = [wanted[h, q ^ s] for s in range(half)]
    other = [wanted[1 - h, q ^ s] for s in range(half)]
    asking = {0: other[0]}
    for s in shifts:
        if s == 1:
            note = jnp.stack([other[1]] + [near[u ^ 1] for u in [0] + evens])
            note = xor_proto(note, 1)
            asking[1] = note[0]
            beside = {u: note[1 + n] for n, u in enumerate([0] + evens)}
        else:
            asking[s] = xor_proto(other[s], s)

    shard = prototypes.reshape(blocks_dev, TILE, width)
    mine = lax.dynamic_slice_in_dim(shard, d * quarter, quarter, axis=0).astype(BF)
    sent = {}
    for i in range(parts):
        piece = mine[:, :, columns[i]]
        for u in evens:
            sent[u, i] = xor_proto(piece, u)
        sent["far", i] = xor_proto(piece, half)

    def share(piece):
        held = [piece]
        for ys in range(1, lanes):
            held.append(xor_design(piece, 2 * ys))
        return held + [xor_design(held[ys], 1) for ys in range(lanes)]

    def flat(piece):
        return piece.reshape(cap * TILE, step)

    own_rows = [[None] * parts for _ in range(half)]
    far_rows = [[None] * parts for _ in range(half)]
    out = gather_round(beside[0], shard, parts)
    for i in range(parts):
        own_rows[1][i] = flat(xor_proto(out[i], 1))
    out = gather_round(near[0], shard, parts)
    for i in range(parts):
        own_rows[0][i] = flat(out[i])
    for i in range(parts):
        for u in evens:
            held = share(sent[u, i])
            (out,) = gather_held(me, [beside[u]], held, lanes)
            own_rows[u ^ 1][i] = flat(xor_proto(out, 1))
            (out,) = gather_held(me, [near[u]], held, lanes)
            own_rows[u][i] = flat(out)
        held = share(sent["far", i])
        outs = gather_held(me, [asking[s] for s in shifts], held, lanes)
        for s, out in zip(shifts, outs):
            far_rows[s][i] = flat(xor_proto(out, s))
        (out,) = gather_held(me, [asking[0]], held, lanes)
        far_rows[0][i] = flat(out)

    def bases(lists, which_half, group):
        out = []
        for s in group:
            first = (which_half * half + (q ^ s)) * blocks_dev
            out.append(jnp.where(lists[s] >= 0, (first + lists[s]) * TILE, -(2**30)))
        return jnp.concatenate(out)

    pos = positives.reshape(1, count)
    logits, sums = {}, []
    for group in groups_of(half).values():
        *got, top, total, hit = own_logits(
            bases(near, h, group), designs, pos, [own_rows[s] for s in group], cap
        )
        logits.update(zip(group, got))
        sums += [top, total, hit]
    stats, far_g, first = far_grads(
        bases(other, 1 - h, range(half)), designs, pos, sums, far_rows, cap, parts
    )
    back_tiles = [first] + far_tiles(designs, far_g, parts)
    losses, top, inv = stats
    own_g, own_tiles = [], []
    for s in range(half):
        g, t = own_grad(
            bases(near, h, [s]), designs, pos, top, inv, logits[s], cap, parts
        )
        own_g.append(g)
        own_tiles.append(t)

    kept = lanes * quarter

    def spots(tables):
        table = jnp.concatenate(tables)
        owner = table // quarter
        at = ((owner // 2) ^ y) * quarter + table % quarter
        at = at + jnp.where(owner % 2 == c, 0, kept)
        return jnp.where(table >= 0, at, -1)

    def reduce_shard(tables, tiles):
        keep, give = collect(spots(tables), tiles, cap, kept)
        came = xor_design(give, 1)
        keep = keep + came.astype(F32)
        keep = keep.reshape(lanes, quarter, TILE, step)
        onward = [keep[ys].astype(BF) for ys in range(1, lanes)]
        total = keep[0]
        for ys in range(1, lanes):
            back = xor_design(onward[ys - 1], 2 * ys)
            total = total + back.astype(F32)
        return total

    result = []
    dgrad = []
    far_tables = [asking[s] for s in range(half)]
    for i in range(parts):
        tiles = [back_tiles[i][0]]
        tiles += [xor_proto(back_tiles[i][s], s) for s in range(1, half)]
        total = reduce_shard(far_tables, tiles)
        landed = [xor_proto(total.astype(BF), half)]
        for u in evens:
            tile = xor_proto(own_tiles[u ^ 1][i], 1)
            total = reduce_shard([near[u], beside[u]], [own_tiles[u][i], tile])
            landed.append(xor_proto(total.astype(BF), u))
        tile = xor_proto(own_tiles[1][i], 1)
        total = reduce_shard([near[0], beside[0]], [own_tiles[0][i], tile])
        for piece in landed:
            total = total + piece.astype(F32)
        result.append(total)
        dgrad.append(
            design_grad(own_g + list(far_g), [r[i] for r in own_rows + far_rows])
        )
    result = jnp.concatenate(result, axis=-1).reshape(quarter * TILE, width)
    return (losses.reshape(count), jnp.concatenate(dgrad, axis=-1), result)


def groups_of(half):
    late = list(range(3, half, 2))
    return {"own_a": [s for s in range(half) if s not in late], "own_b": late}


def solution(mesh):
    return jax.shard_map(
        body,
        mesh=mesh,
        in_specs=(
            P(("proto", "design"), None),
            P("proto", None),
            P(("proto", "design"), None),
            P(("proto", "design")),
        ),
        out_specs=(
            P(("proto", "design")),
            P(("proto", "design"), None),
            P(("proto", "design"), None),
        ),
        check_vma=False,
    )
```

```python
import functools

import jax
import jax.numpy as jnp
from jax import lax
from jax.experimental import pallas as pl
from jax.experimental.pallas import tpu as pltpu
from jax.sharding import PartitionSpec as P


D = 1024
TILE = 128
BF = jnp.bfloat16
F32 = jnp.float32
NEG = -1e30
PARTS = 2


def xor_proto(x, shift):
    count = lax.axis_size("proto")
    return lax.ppermute(x, "proto", [(i, i ^ shift) for i in range(count)])


def xor_design(x, shift):
    count = lax.axis_size("design")
    return lax.ppermute(x, "design", [(i, i ^ shift) for i in range(count)])


def request_table(block_list, blocks_dev, capacity, proto_count):
    owners = block_list // blocks_dev
    local_ids = block_list % blocks_dev
    ids = jnp.arange(block_list.shape[0], dtype=jnp.int32)
    earlier = (owners[:, None] == owners[None, :]) & (ids[None, :] < ids[:, None])
    rank_of = jnp.sum(earlier.astype(jnp.int32), axis=1)
    slot_of = owners * capacity + rank_of
    slots = jnp.arange(proto_count * capacity, dtype=jnp.int32)
    hit = slot_of[None, :] == slots[:, None]
    return jnp.sum(jnp.where(hit, local_ids[None, :] + 1, 0), axis=1) - 1


HBM = pl.BlockSpec(memory_space=pl.ANY)
VM = pl.BlockSpec(memory_space=pltpu.VMEM)
SM = pl.BlockSpec(memory_space=pltpu.SMEM)
FIXED = pl.BlockSpec(memory_space=pltpu.HBM)


def grant(mib):
    return pltpu.CompilerParams(vmem_limit_bytes=mib << 20)


def gather_round_kernel(parts, table, src, *refs):
    outs, buf, sems = refs[:parts], refs[parts], refs[parts + 1]
    cap, _, step = outs[0].shape
    copies = []
    for k in range(cap):
        row = jnp.maximum(table[k], 0)
        copies.append(pltpu.make_async_copy(src.at[row], buf.at[k], sems.at[k]))
    for copy in copies:
        copy.start()
    for k, copy in enumerate(copies):
        copy.wait()
        for i in range(parts):
            outs[i][k] = buf[k, :, i * step : (i + 1) * step].astype(BF)


def gather_round(table, shard, parts):
    cap = table.shape[0]
    _, tile, width = shard.shape
    return pl.pallas_call(
        functools.partial(gather_round_kernel, parts),
        out_shape=[jax.ShapeDtypeStruct((cap, tile, width // parts), BF)] * parts,
        in_specs=[SM, FIXED],
        out_specs=[VM] * parts,
        scratch_shapes=[
            pltpu.VMEM((cap, tile, width), F32),
            pltpu.SemaphoreType.DMA((cap,)),
        ],
        compiler_params=grant(6),
        name="gather_round",
    )(table, shard)


def gather_held_kernel(n_src, n_out, quarter, lanes, me, *refs):
    tables, srcs = refs[:n_out], refs[n_out : n_out + n_src]
    outs, sems = refs[n_out + n_src : -1], refs[-1]
    cap = outs[0].shape[0]
    y, c = me[0] // 2, me[0] % 2
    for n in range(n_out):

        @pl.loop(0, cap)
        def _(k):
            row = jnp.maximum(tables[n][k], 0)
            owner, inside = row // quarter, row % quarter
            which = ((owner % 2) ^ c) * lanes + ((owner // 2) ^ y)
            for a in range(n_src):

                @pl.when(which == a)
                def _():
                    pltpu.make_async_copy(
                        srcs[a].at[inside], outs[n].at[k], sems.at[n * cap + k]
                    ).start()

    for n in range(n_out):

        @pl.loop(0, cap)
        def _(k):
            pltpu.make_async_copy(srcs[0].at[0], outs[n].at[k], sems.at[n * cap + k]).wait()


def gather_held(me, tables, srcs, lanes):
    n = len(tables)
    cap = tables[0].shape[0]
    quarter = srcs[0].shape[0]
    shape = (cap,) + srcs[0].shape[1:]
    return pl.pallas_call(
        functools.partial(gather_held_kernel, len(srcs), n, quarter, lanes),
        out_shape=[jax.ShapeDtypeStruct(shape, BF)] * n,
        in_specs=[SM] * (n + 1) + [HBM] * len(srcs),
        out_specs=[VM] * n,
        scratch_shapes=[pltpu.SemaphoreType.DMA((n * cap,))],
        compiler_params=grant(2),
        name="gather_held",
    )(me, *tables, *srcs)


def contract(rows, x, lanes):
    step = rows[0].shape[1]
    total = None
    for i, part in enumerate(rows):
        got = lax.dot_general(
            part[...],
            x[lanes, i * step : (i + 1) * step],
            (((1,), (1,)), ((), ())),
            preferred_element_type=F32,
        )
        total = got if total is None else total + got
    return total


EXP_SCALE = (D ** (-0.5)) * 1.4426950408889634


def fold(tile, op):
    return op(tile.reshape(tile.shape[0] // 8, 8, tile.shape[1]), axis=0)


def slot_stats(base, rel, slots):
    top = None
    hit = None
    for n, ref in slots:
        piece = ref[...]
        target = rel == base[n]
        found = fold(jnp.where(target, piece, 0.0), jnp.sum)
        piece = piece + jnp.where(base[n] < 0, NEG, 0.0)
        high = fold(piece, jnp.max)
        top = high if top is None else jnp.maximum(top, high)
        hit = found if hit is None else hit + found
    return jnp.max(top, axis=0, keepdims=True), jnp.sum(hit, axis=0, keepdims=True)


def slot_power(base, n, ref, top):
    piece = ref[...] + jnp.where(base[n] < 0, NEG, 0.0)
    return jnp.exp2((piece - top) * EXP_SCALE)


def relative(pos, lanes):
    line = lax.broadcasted_iota(jnp.int32, (TILE, lanes), 0)
    return pos - line


def own_kernel(group, cap, lanes, parts, base, x, pos, *refs):
    rows = [refs[s * parts : (s + 1) * parts] for s in range(group)]
    kept = refs[group * parts : group * (parts + 1)]
    top_out, sum_out, hit_out, logits, sems = refs[group * (parts + 1) :]
    count = x.shape[0]

    def copy_out(s, j):
        at = pl.ds(pl.multiple_of(j * lanes, lanes), lanes)
        return pltpu.make_async_copy(logits.at[s, :, at], kept[s].at[:, at], sems.at[s, j])

    @pl.loop(0, count // lanes)
    def _(j):
        at = pl.ds(pl.multiple_of(j * lanes, lanes), lanes)
        for s in range(group):
            logits[s, :, at] = contract(rows[s], x, at)
            copy_out(s, j).start()
        slots = [
            (s * cap + k, logits.at[s, pl.ds(k * TILE, TILE), at])
            for s in range(group)
            for k in range(cap)
        ]
        top, hit = slot_stats(base, relative(pos[:, at], lanes), slots)
        total = None
        for n, ref in slots:
            part = fold(slot_power(base, n, ref, top), jnp.sum)
            total = part if total is None else total + part
        top_out[:, at] = top
        hit_out[:, at] = hit
        sum_out[:, at] = jnp.sum(total, axis=0, keepdims=True)

    @pl.loop(0, count // lanes)
    def _(j):
        for s in range(group):
            copy_out(s, j).wait()


def own_logits(base, x, pos, rows, cap, lanes=256):
    group, parts = len(rows), len(rows[0])
    rows = [r for row in rows for r in row]
    count = x.shape[0]
    line = (1, count)
    shape = (rows[0].shape[0], count)
    return pl.pallas_call(
        functools.partial(own_kernel, group, cap, lanes, parts),
        out_shape=[pltpu.HBM(shape, F32)] * group + [jax.ShapeDtypeStruct(line, F32)] * 3,
        in_specs=[SM] + [VM] * (2 + len(rows)),
        out_specs=[FIXED] * group + [VM] * 3,
        scratch_shapes=[
            pltpu.VMEM((group,) + shape, F32),
            pltpu.SemaphoreType.DMA((group, count // lanes)),
        ],
        compiler_params=grant(12),
        name="own_logits",
    )(base, x, pos, *rows)


def far_kernel(group, cap, lanes, parts, n_stats, base, x, pos, *refs):
    stats = [refs[3 * i : 3 * i + 3] for i in range(n_stats)]
    refs = refs[3 * n_stats :]
    rows = [refs[s * parts : (s + 1) * parts] for s in range(group)]
    refs = refs[group * parts :]
    losses, top_out, inv_out = refs[:3]
    kept = refs[3:-4]
    logits, grads, tiles, sems = refs[-4:]
    count, width = x.shape
    scale = D ** (-0.5)
    for j in range(0, count, lanes):
        turn = (j // lanes) % 2
        at = pl.ds(j, lanes)
        for s in range(group):
            logits[turn, s * cap * TILE : (s + 1) * cap * TILE, :] = contract(
                rows[s], x, pl.ds(j, lanes)
            )
        slots = [
            (n, logits.at[turn, pl.ds(n * TILE, TILE), :]) for n in range(group * cap)
        ]
        rel = relative(pos[:, at], lanes)
        top, hit = slot_stats(base, rel, slots)
        both = top
        for top_own, _, _ in stats:
            both = jnp.maximum(both, top_own[:, at])
        total = None
        for n, ref in slots:
            power = slot_power(base, n, ref, both)
            ref[...] = power
            part = fold(power, jnp.sum)
            total = part if total is None else total + part
        total = jnp.sum(total, axis=0, keepdims=True)
        for top_own, sum_own, hit_own in stats:
            total = total + sum_own[:, at] * jnp.exp2((top_own[:, at] - both) * EXP_SCALE)
            hit = hit + hit_own[:, at]
        losses[:, at] = both * scale + jnp.log(total) - hit * scale
        inv = 1.0 / total
        top_out[:, at] = both
        inv_out[:, at] = inv
        for n, ref in slots:
            s, k = n // cap, n % cap
            target = jnp.where(rel == base[n], 1.0, 0.0)
            grads[s, k * TILE : (k + 1) * TILE, at] = (ref[...] * inv - target).astype(BF)
    step = width // parts
    sources = [grads.at[s] for s in range(group)] + [tiles.at[s] for s in range(group)]
    copies = [
        pltpu.make_async_copy(a, b, sems.at[n]) for n, (a, b) in enumerate(zip(sources, kept))
    ]
    for copy in copies[:group]:
        copy.start()
    for s in reversed(range(group)):
        tiles[s] = jnp.dot(grads[s], x[:, :step], preferred_element_type=F32).astype(BF)
        copies[group + s].start()
    for copy in copies:
        copy.wait()


def far_grads(base, x, pos, stats, rows, cap, parts, lanes=256):
    group = len(rows)
    rows = [r for row in rows for r in row]
    count, width = x.shape
    size = rows[0].shape[0]
    outs = [((1, count), F32)] * 3 + [((size, count), BF)] * group
    outs += [((size, width // parts), BF)] * group
    got = pl.pallas_call(
        functools.partial(far_kernel, group, cap, lanes, parts, len(stats) // 3),
        out_shape=[jax.ShapeDtypeStruct(*o) for o in outs[:3]]
        + [pltpu.HBM(*o) for o in outs[3:]],
        in_specs=[SM] + [VM] * (2 + len(stats) + len(rows)),
        out_specs=[VM] * 3 + [FIXED] * (len(outs) - 3),
        scratch_shapes=[
            pltpu.VMEM((2, group * size, lanes), F32),
            pltpu.VMEM((group, size, count), BF),
            pltpu.VMEM((group, size, width // parts), BF),
            pltpu.SemaphoreType.DMA((2 * group,)),
        ],
        compiler_params=grant(20),
        name="far_grads",
    )(base, x, pos, *stats, *rows)
    return got[:3], got[3 : 3 + group], got[3 + group :]


def far_tiles_kernel(group, first, x, *refs):
    grads, tiles = refs[:group], refs[group:]
    step = tiles[0].shape[1]
    for n, tile in enumerate(tiles):
        i = first + n // group
        tile[...] = jnp.dot(
            grads[n % group][...], x[:, i * step : (i + 1) * step], preferred_element_type=F32
        ).astype(BF)


def far_tiles(x, grads, parts):
    group = len(grads)
    shape = (grads[0].shape[0], x.shape[1] // parts)
    got = pl.pallas_call(
        functools.partial(far_tiles_kernel, group, 1),
        out_shape=[jax.ShapeDtypeStruct(shape, BF)] * (group * (parts - 1)),
        in_specs=[VM] * (1 + group),
        out_specs=[VM] * (group * (parts - 1)),
        compiler_params=grant(6),
        name="far_tiles",
    )(x, *grads)
    return [got[i : i + group] for i in range(0, len(got), group)]


def own_grad_kernel(cap, parts, base, x, pos, top, inv, logits, grad, *tiles):
    count, width = x.shape
    rel = relative(pos[...], count)
    for k in range(cap):
        ref = logits.at[pl.ds(k * TILE, TILE), :]
        power = slot_power(base, k, ref, top[...])
        target = jnp.where(rel == base[k], 1.0, 0.0)
        grad[k * TILE : (k + 1) * TILE, :] = (power * inv[...] - target).astype(BF)
    step = width // parts
    for i in range(parts):
        tiles[i][...] = jnp.dot(
            grad[...], x[:, i * step : (i + 1) * step], preferred_element_type=F32
        ).astype(BF)


def own_grad(base, x, pos, top, inv, logits, cap, parts):
    count, width = x.shape
    size = logits.shape[0]
    outs = [((size, count), BF)] + [((size, width // parts), BF)] * parts
    got = pl.pallas_call(
        functools.partial(own_grad_kernel, cap, parts),
        out_shape=[jax.ShapeDtypeStruct(*o) for o in outs],
        in_specs=[SM] + [VM] * 5,
        out_specs=[VM] * len(outs),
        compiler_params=grant(6),
        name="own_grad",
    )(base, x, pos, top, inv, logits)
    return got[0], got[1:]


def design_grad_kernel(n, chunk, *refs):
    grads, rows, out = refs[:n], refs[n : 2 * n], refs[2 * n]

    @pl.loop(0, out.shape[0] // chunk)
    def _(j):
        at = pl.ds(pl.multiple_of(j * chunk, chunk), chunk)
        acc = None
        for g, r in zip(grads, rows):
            part = lax.dot_general(
                g[:, at], r[...], (((0,), (0,)), ((), ())), preferred_element_type=F32
            )
            acc = part if acc is None else acc + part
        out[at, :] = acc.astype(BF)


def design_grad(grads, rows, chunk=256):
    n = len(grads)
    return pl.pallas_call(
        functools.partial(design_grad_kernel, n, chunk),
        out_shape=jax.ShapeDtypeStruct((grads[0].shape[1], rows[0].shape[1]), BF),
        in_specs=[VM] * (2 * n),
        out_specs=VM,
        compiler_params=grant(8),
        name="design_grad",
    )(*grads, *rows)


def collect_kernel(n, cap, spot, *refs):
    parts = refs[:n]
    keep, give, acc = refs[n:]
    kept = keep.shape[0]
    acc[...] = jnp.zeros_like(acc)
    for i in range(n * cap):

        @pl.when(spot[i] >= 0)
        def _():
            s, k = i // cap, i % cap
            acc[spot[i]] += parts[s][k * TILE : (k + 1) * TILE, :].astype(F32)

    keep[...] = acc[:kept]
    give[...] = acc[kept:].astype(BF)


def collect(spot, parts, cap, kept):
    n = len(parts)
    width = parts[0].shape[1]
    shape = (kept, TILE, width)
    return pl.pallas_call(
        functools.partial(collect_kernel, n, cap),
        out_shape=[jax.ShapeDtypeStruct(shape, F32), jax.ShapeDtypeStruct(shape, BF)],
        in_specs=[SM] + [VM] * n,
        out_specs=[VM] * 2,
        scratch_shapes=[pltpu.VMEM((2 * kept, TILE, width), F32)],
        compiler_params=grant(8),
        name="collect",
    )(spot, *parts)


def body(designs, prototypes, candidates, positives):
    proto_count = lax.axis_size("proto")
    design_axis = lax.axis_size("design")
    half = proto_count // 2
    lanes = design_axis // 2
    cand_count = candidates.shape[1]
    width = designs.shape[1]
    count = designs.shape[0]
    blocks_dev = prototypes.shape[0] // TILE
    quarter = blocks_dev // design_axis
    cap = max(2, (4 * cand_count + 3 * proto_count - 1) // (3 * proto_count))
    parts = PARTS
    step = width // parts
    p = lax.axis_index("proto").astype(jnp.int32)
    d = lax.axis_index("design").astype(jnp.int32)
    q = p % half
    h = p // half
    y = d // 2
    c = d % 2
    me = d.reshape(1)
    shifts = list(range(half - 1, 0, -1))
    evens = list(range(2, half, 2))
    flip = half // 2
    across = half + flip
    columns = [slice(i * step, (i + 1) * step) for i in range(parts)]

    wanted = request_table(candidates[0], blocks_dev, cap, proto_count)
    wanted = wanted.reshape(2, half, cap)
    near = [wanted[h, q ^ s] for s in range(half)]
    other = [wanted[1 - h, q ^ s ^ flip] for s in range(half)]
    asking = {0: other[0]}
    for s in shifts:
        if s == 1:
            note = jnp.stack([other[1]] + [near[u ^ 1] for u in [0] + evens])
            note = xor_proto(note, 1)
            asking[1] = note[0]
            beside = {u: note[1 + n] for n, u in enumerate([0] + evens)}
        else:
            asking[s] = xor_proto(other[s], s)

    shard = prototypes.reshape(blocks_dev, TILE, width)
    mine = lax.dynamic_slice_in_dim(shard, d * quarter, quarter, axis=0).astype(BF)
    sent = {}
    for i in range(parts):
        piece = mine[:, :, columns[i]]
        for u in evens:
            sent[u, i] = xor_proto(piece, u)
        sent["far", i] = xor_proto(piece, across)

    def share(piece):
        held = [piece]
        for ys in range(1, lanes):
            held.append(xor_design(piece, 2 * ys))
        return held + [xor_design(held[ys], 1) for ys in range(lanes)]

    def flat(piece):
        return piece.reshape(cap * TILE, step)

    own_rows = [[None] * parts for _ in range(half)]
    far_rows = [[None] * parts for _ in range(half)]
    out = gather_round(beside[0], shard, parts)
    for i in range(parts):
        own_rows[1][i] = flat(xor_proto(out[i], 1))
    out = gather_round(near[0], shard, parts)
    for i in range(parts):
        own_rows[0][i] = flat(out[i])
    for i in range(parts):
        for u in evens:
            held = share(sent[u, i])
            (out,) = gather_held(me, [beside[u]], held, lanes)
            own_rows[u ^ 1][i] = flat(xor_proto(out, 1))
            (out,) = gather_held(me, [near[u]], held, lanes)
            own_rows[u][i] = flat(out)
        held = share(sent["far", i])
        outs = gather_held(me, [asking[s] for s in shifts], held, lanes)
        for s, out in zip(shifts, outs):
            far_rows[s][i] = flat(xor_proto(out, s))
        (out,) = gather_held(me, [asking[0]], held, lanes)
        far_rows[0][i] = flat(out)

    def bases(lists, which_half, group, turn=0):
        out = []
        for s in group:
            first = (which_half * half + (q ^ s ^ turn)) * blocks_dev
            out.append(jnp.where(lists[s] >= 0, (first + lists[s]) * TILE, -(2**30)))
        return jnp.concatenate(out)

    pos = positives.reshape(1, count)
    logits, sums = {}, []
    for group in groups_of(half).values():
        *got, top, total, hit = own_logits(
            bases(near, h, group), designs, pos, [own_rows[s] for s in group], cap
        )
        logits.update(zip(group, got))
        sums += [top, total, hit]
    stats, far_g, first = far_grads(
        bases(other, 1 - h, range(half), flip), designs, pos, sums, far_rows, cap, parts
    )
    back_tiles = [first] + far_tiles(designs, far_g, parts)
    losses, top, inv = stats
    own_g, own_tiles = [], []
    for s in range(half):
        g, t = own_grad(
            bases(near, h, [s]), designs, pos, top, inv, logits[s], cap, parts
        )
        own_g.append(g)
        own_tiles.append(t)

    kept = lanes * quarter

    def spots(tables):
        table = jnp.concatenate(tables)
        owner = table // quarter
        at = ((owner // 2) ^ y) * quarter + table % quarter
        at = at + jnp.where(owner % 2 == c, 0, kept)
        return jnp.where(table >= 0, at, -1)

    def reduce_shard(tables, tiles):
        keep, give = collect(spots(tables), tiles, cap, kept)
        came = xor_design(give, 1)
        keep = keep + came.astype(F32)
        keep = keep.reshape(lanes, quarter, TILE, step)
        onward = [keep[ys].astype(BF) for ys in range(1, lanes)]
        total = keep[0]
        for ys in range(1, lanes):
            back = xor_design(onward[ys - 1], 2 * ys)
            total = total + back.astype(F32)
        return total

    result = []
    dgrad = []
    far_tables = [asking[s] for s in range(half)]
    for i in range(parts):
        tiles = [back_tiles[i][0]]
        tiles += [xor_proto(back_tiles[i][s], s) for s in range(1, half)]
        total = reduce_shard(far_tables, tiles)
        landed = [xor_proto(total.astype(BF), across)]
        for u in evens:
            tile = xor_proto(own_tiles[u ^ 1][i], 1)
            total = reduce_shard([near[u], beside[u]], [own_tiles[u][i], tile])
            landed.append(xor_proto(total.astype(BF), u))
        tile = xor_proto(own_tiles[1][i], 1)
        total = reduce_shard([near[0], beside[0]], [own_tiles[0][i], tile])
        for piece in landed:
            total = total + piece.astype(F32)
        result.append(total)
        dgrad.append(
            design_grad(own_g + list(far_g), [r[i] for r in own_rows + far_rows])
        )
    result = jnp.concatenate(result, axis=-1).reshape(quarter * TILE, width)
    return (losses.reshape(count), jnp.concatenate(dgrad, axis=-1), result)


def groups_of(half):
    late = list(range(3, half, 2))
    return {"own_a": [s for s in range(half) if s not in late], "own_b": late}


def solution(mesh):
    return jax.shard_map(
        body,
        mesh=mesh,
        in_specs=(
            P(("proto", "design"), None),
            P("proto", None),
            P(("proto", "design"), None),
            P(("proto", "design")),
        ),
        out_specs=(
            P(("proto", "design")),
            P(("proto", "design"), None),
            P(("proto", "design"), None),
        ),
        check_vma=False,
    )
```

```python
import functools

import jax
import jax.numpy as jnp
from jax import lax
from jax.experimental import pallas as pl
from jax.experimental.pallas import tpu as pltpu
from jax.sharding import PartitionSpec as P


D = 1024
TILE = 128
BF = jnp.bfloat16
F32 = jnp.float32
NEG = -1e30
PARTS = 2


def xor_proto(x, shift):
    count = lax.axis_size("proto")
    return lax.ppermute(x, "proto", [(i, i ^ shift) for i in range(count)])


def xor_design(x, shift):
    count = lax.axis_size("design")
    return lax.ppermute(x, "design", [(i, i ^ shift) for i in range(count)])


def request_table(block_list, blocks_dev, capacity, proto_count):
    owners = block_list // blocks_dev
    local_ids = block_list % blocks_dev
    ids = jnp.arange(block_list.shape[0], dtype=jnp.int32)
    earlier = (owners[:, None] == owners[None, :]) & (ids[None, :] < ids[:, None])
    rank_of = jnp.sum(earlier.astype(jnp.int32), axis=1)
    slot_of = owners * capacity + rank_of
    slots = jnp.arange(proto_count * capacity, dtype=jnp.int32)
    hit = slot_of[None, :] == slots[:, None]
    return jnp.sum(jnp.where(hit, local_ids[None, :] + 1, 0), axis=1) - 1


HBM = pl.BlockSpec(memory_space=pl.ANY)
VM = pl.BlockSpec(memory_space=pltpu.VMEM)
SM = pl.BlockSpec(memory_space=pltpu.SMEM)
FIXED = pl.BlockSpec(memory_space=pltpu.HBM)


def grant(mib):
    return pltpu.CompilerParams(vmem_limit_bytes=mib << 20)


def gather_round_kernel(parts, table, src, *refs):
    outs, buf, sems = refs[:parts], refs[parts], refs[parts + 1]
    cap, _, step = outs[0].shape
    copies = []
    for k in range(cap):
        row = jnp.maximum(table[k], 0)
        copies.append(pltpu.make_async_copy(src.at[row], buf.at[k], sems.at[k]))
    for copy in copies:
        copy.start()
    for k, copy in enumerate(copies):
        copy.wait()
        for i in range(parts):
            outs[i][k] = buf[k, :, i * step : (i + 1) * step].astype(BF)


def gather_round(table, shard, parts):
    cap = table.shape[0]
    _, tile, width = shard.shape
    return pl.pallas_call(
        functools.partial(gather_round_kernel, parts),
        out_shape=[jax.ShapeDtypeStruct((cap, tile, width // parts), BF)] * parts,
        in_specs=[SM, FIXED],
        out_specs=[VM] * parts,
        scratch_shapes=[
            pltpu.VMEM((cap, tile, width), F32),
            pltpu.SemaphoreType.DMA((cap,)),
        ],
        compiler_params=grant(6),
        name="gather_round",
    )(table, shard)


def gather_held_kernel(n_src, n_out, quarter, lanes, me, *refs):
    tables, srcs = refs[:n_out], refs[n_out : n_out + n_src]
    outs, sems = refs[n_out + n_src : -1], refs[-1]
    cap = outs[0].shape[0]
    y, c = me[0] // 2, me[0] % 2
    for n in range(n_out):

        @pl.loop(0, cap)
        def _(k):
            row = jnp.maximum(tables[n][k], 0)
            owner, inside = row // quarter, row % quarter
            which = ((owner % 2) ^ c) * lanes + ((owner // 2) ^ y)
            for a in range(n_src):

                @pl.when(which == a)
                def _():
                    pltpu.make_async_copy(
                        srcs[a].at[inside], outs[n].at[k], sems.at[n * cap + k]
                    ).start()

    for n in range(n_out):

        @pl.loop(0, cap)
        def _(k):
            pltpu.make_async_copy(srcs[0].at[0], outs[n].at[k], sems.at[n * cap + k]).wait()


def gather_held(me, tables, srcs, lanes):
    n = len(tables)
    cap = tables[0].shape[0]
    quarter = srcs[0].shape[0]
    shape = (cap,) + srcs[0].shape[1:]
    return pl.pallas_call(
        functools.partial(gather_held_kernel, len(srcs), n, quarter, lanes),
        out_shape=[jax.ShapeDtypeStruct(shape, BF)] * n,
        in_specs=[SM] * (n + 1) + [HBM] * len(srcs),
        out_specs=[VM] * n,
        scratch_shapes=[pltpu.SemaphoreType.DMA((n * cap,))],
        compiler_params=grant(2),
        name="gather_held",
    )(me, *tables, *srcs)


def contract(rows, x, lanes):
    step = rows[0].shape[1]
    total = None
    for i, part in enumerate(rows):
        got = lax.dot_general(
            part[...],
            x[lanes, i * step : (i + 1) * step],
            (((1,), (1,)), ((), ())),
            preferred_element_type=F32,
        )
        total = got if total is None else total + got
    return total


EXP_SCALE = (D ** (-0.5)) * 1.4426950408889634


def fold(tile, op):
    return op(tile.reshape(tile.shape[0] // 8, 8, tile.shape[1]), axis=0)


def slot_stats(base, rel, slots):
    top = None
    hit = None
    for n, ref in slots:
        piece = ref[...]
        target = rel == base[n]
        found = fold(jnp.where(target, piece, 0.0), jnp.sum)
        piece = piece + jnp.where(base[n] < 0, NEG, 0.0)
        high = fold(piece, jnp.max)
        top = high if top is None else jnp.maximum(top, high)
        hit = found if hit is None else hit + found
    return jnp.max(top, axis=0, keepdims=True), jnp.sum(hit, axis=0, keepdims=True)


def slot_power(base, n, ref, top):
    piece = ref[...] + jnp.where(base[n] < 0, NEG, 0.0)
    return jnp.exp2((piece - top) * EXP_SCALE)


def relative(pos, lanes):
    line = lax.broadcasted_iota(jnp.int32, (TILE, lanes), 0)
    return pos - line


def own_kernel(group, cap, lanes, parts, base, x, pos, *refs):
    rows = [refs[s * parts : (s + 1) * parts] for s in range(group)]
    kept = refs[group * parts : group * (parts + 1)]
    top_out, sum_out, hit_out, logits, sems = refs[group * (parts + 1) :]
    count = x.shape[0]

    def copy_out(s, j):
        at = pl.ds(pl.multiple_of(j * lanes, lanes), lanes)
        return pltpu.make_async_copy(logits.at[s, :, at], kept[s].at[:, at], sems.at[s, j])

    @pl.loop(0, count // lanes)
    def _(j):
        at = pl.ds(pl.multiple_of(j * lanes, lanes), lanes)
        for s in range(group):
            logits[s, :, at] = contract(rows[s], x, at)
            copy_out(s, j).start()
        slots = [
            (s * cap + k, logits.at[s, pl.ds(k * TILE, TILE), at])
            for s in range(group)
            for k in range(cap)
        ]
        top, hit = slot_stats(base, relative(pos[:, at], lanes), slots)
        total = None
        for n, ref in slots:
            part = fold(slot_power(base, n, ref, top), jnp.sum)
            total = part if total is None else total + part
        top_out[:, at] = top
        hit_out[:, at] = hit
        sum_out[:, at] = jnp.sum(total, axis=0, keepdims=True)

    @pl.loop(0, count // lanes)
    def _(j):
        for s in range(group):
            copy_out(s, j).wait()


def own_logits(base, x, pos, rows, cap, lanes=256):
    group, parts = len(rows), len(rows[0])
    rows = [r for row in rows for r in row]
    count = x.shape[0]
    line = (1, count)
    shape = (rows[0].shape[0], count)
    return pl.pallas_call(
        functools.partial(own_kernel, group, cap, lanes, parts),
        out_shape=[pltpu.HBM(shape, F32)] * group + [jax.ShapeDtypeStruct(line, F32)] * 3,
        in_specs=[SM] + [VM] * (2 + len(rows)),
        out_specs=[FIXED] * group + [VM] * 3,
        scratch_shapes=[
            pltpu.VMEM((group,) + shape, F32),
            pltpu.SemaphoreType.DMA((group, count // lanes)),
        ],
        compiler_params=grant(12),
        name="own_logits",
    )(base, x, pos, *rows)


def far_kernel(group, cap, lanes, parts, n_stats, base, x, pos, *refs):
    stats = [refs[3 * i : 3 * i + 3] for i in range(n_stats)]
    refs = refs[3 * n_stats :]
    rows = [refs[s * parts : (s + 1) * parts] for s in range(group)]
    refs = refs[group * parts :]
    losses, top_out, inv_out = refs[:3]
    kept = refs[3:-4]
    logits, grads, tiles, sems = refs[-4:]
    count, width = x.shape
    scale = D ** (-0.5)
    for j in range(0, count, lanes):
        turn = (j // lanes) % 2
        at = pl.ds(j, lanes)
        for s in range(group):
            logits[turn, s * cap * TILE : (s + 1) * cap * TILE, :] = contract(
                rows[s], x, pl.ds(j, lanes)
            )
        slots = [
            (n, logits.at[turn, pl.ds(n * TILE, TILE), :]) for n in range(group * cap)
        ]
        rel = relative(pos[:, at], lanes)
        top, hit = slot_stats(base, rel, slots)
        both = top
        for top_own, _, _ in stats:
            both = jnp.maximum(both, top_own[:, at])
        total = None
        for n, ref in slots:
            power = slot_power(base, n, ref, both)
            ref[...] = power
            part = fold(power, jnp.sum)
            total = part if total is None else total + part
        total = jnp.sum(total, axis=0, keepdims=True)
        for top_own, sum_own, hit_own in stats:
            total = total + sum_own[:, at] * jnp.exp2((top_own[:, at] - both) * EXP_SCALE)
            hit = hit + hit_own[:, at]
        losses[:, at] = both * scale + jnp.log(total) - hit * scale
        inv = 1.0 / total
        top_out[:, at] = both
        inv_out[:, at] = inv
        for n, ref in slots:
            s, k = n // cap, n % cap
            target = jnp.where(rel == base[n], 1.0, 0.0)
            grads[s, k * TILE : (k + 1) * TILE, at] = (ref[...] * inv - target).astype(BF)
    step = width // parts
    sources = [grads.at[s] for s in range(group)] + [tiles.at[s] for s in range(group)]
    copies = [
        pltpu.make_async_copy(a, b, sems.at[n]) for n, (a, b) in enumerate(zip(sources, kept))
    ]
    for copy in copies[:group]:
        copy.start()
    for s in reversed(range(group)):
        tiles[s] = jnp.dot(grads[s], x[:, :step], preferred_element_type=F32).astype(BF)
        copies[group + s].start()
    for copy in copies:
        copy.wait()


def far_grads(base, x, pos, stats, rows, cap, parts, lanes=256):
    group = len(rows)
    rows = [r for row in rows for r in row]
    count, width = x.shape
    size = rows[0].shape[0]
    outs = [((1, count), F32)] * 3 + [((size, count), BF)] * group
    outs += [((size, width // parts), BF)] * group
    got = pl.pallas_call(
        functools.partial(far_kernel, group, cap, lanes, parts, len(stats) // 3),
        out_shape=[jax.ShapeDtypeStruct(*o) for o in outs[:3]]
        + [pltpu.HBM(*o) for o in outs[3:]],
        in_specs=[SM] + [VM] * (2 + len(stats) + len(rows)),
        out_specs=[VM] * 3 + [FIXED] * (len(outs) - 3),
        scratch_shapes=[
            pltpu.VMEM((2, group * size, lanes), F32),
            pltpu.VMEM((group, size, count), BF),
            pltpu.VMEM((group, size, width // parts), BF),
            pltpu.SemaphoreType.DMA((2 * group,)),
        ],
        compiler_params=grant(20),
        name="far_grads",
    )(base, x, pos, *stats, *rows)
    return got[:3], got[3 : 3 + group], got[3 + group :]


def far_tiles_kernel(group, first, x, *refs):
    grads, tiles = refs[:group], refs[group:]
    step = tiles[0].shape[1]
    for n, tile in enumerate(tiles):
        i = first + n // group
        tile[...] = jnp.dot(
            grads[n % group][...], x[:, i * step : (i + 1) * step], preferred_element_type=F32
        ).astype(BF)


def far_tiles(x, grads, parts):
    group = len(grads)
    shape = (grads[0].shape[0], x.shape[1] // parts)
    got = pl.pallas_call(
        functools.partial(far_tiles_kernel, group, 1),
        out_shape=[jax.ShapeDtypeStruct(shape, BF)] * (group * (parts - 1)),
        in_specs=[VM] * (1 + group),
        out_specs=[VM] * (group * (parts - 1)),
        compiler_params=grant(6),
        name="far_tiles",
    )(x, *grads)
    return [got[i : i + group] for i in range(0, len(got), group)]


def own_grad_kernel(cap, parts, base, x, pos, top, inv, logits, grad, *tiles):
    count, width = x.shape
    rel = relative(pos[...], count)
    for k in range(cap):
        ref = logits.at[pl.ds(k * TILE, TILE), :]
        power = slot_power(base, k, ref, top[...])
        target = jnp.where(rel == base[k], 1.0, 0.0)
        grad[k * TILE : (k + 1) * TILE, :] = (power * inv[...] - target).astype(BF)
    step = width // parts
    for i in range(parts):
        tiles[i][...] = jnp.dot(
            grad[...], x[:, i * step : (i + 1) * step], preferred_element_type=F32
        ).astype(BF)


def own_grad(base, x, pos, top, inv, logits, cap, parts):
    count, width = x.shape
    size = logits.shape[0]
    outs = [((size, count), BF)] + [((size, width // parts), BF)] * parts
    got = pl.pallas_call(
        functools.partial(own_grad_kernel, cap, parts),
        out_shape=[jax.ShapeDtypeStruct(*o) for o in outs],
        in_specs=[SM] + [VM] * 5,
        out_specs=[VM] * len(outs),
        compiler_params=grant(6),
        name="own_grad",
    )(base, x, pos, top, inv, logits)
    return got[0], got[1:]


def design_grad_kernel(n, chunk, *refs):
    grads, rows, out = refs[:n], refs[n : 2 * n], refs[2 * n]

    @pl.loop(0, out.shape[0] // chunk)
    def _(j):
        at = pl.ds(pl.multiple_of(j * chunk, chunk), chunk)
        acc = None
        for g, r in zip(grads, rows):
            part = lax.dot_general(
                g[:, at], r[...], (((0,), (0,)), ((), ())), preferred_element_type=F32
            )
            acc = part if acc is None else acc + part
        out[at, :] = acc.astype(BF)


def design_grad(grads, rows, chunk=256):
    n = len(grads)
    return pl.pallas_call(
        functools.partial(design_grad_kernel, n, chunk),
        out_shape=jax.ShapeDtypeStruct((grads[0].shape[1], rows[0].shape[1]), BF),
        in_specs=[VM] * (2 * n),
        out_specs=VM,
        compiler_params=grant(8),
        name="design_grad",
    )(*grads, *rows)


def collect_kernel(n, cap, spot, *refs):
    parts = refs[:n]
    keep, give, acc = refs[n:]
    kept = keep.shape[0]
    acc[...] = jnp.zeros_like(acc)
    for i in range(n * cap):

        @pl.when(spot[i] >= 0)
        def _():
            s, k = i // cap, i % cap
            acc[spot[i]] += parts[s][k * TILE : (k + 1) * TILE, :].astype(F32)

    keep[...] = acc[:kept]
    give[...] = acc[kept:].astype(BF)


def collect(spot, parts, cap, kept):
    n = len(parts)
    width = parts[0].shape[1]
    shape = (kept, TILE, width)
    return pl.pallas_call(
        functools.partial(collect_kernel, n, cap),
        out_shape=[jax.ShapeDtypeStruct(shape, F32), jax.ShapeDtypeStruct(shape, BF)],
        in_specs=[SM] + [VM] * n,
        out_specs=[VM] * 2,
        scratch_shapes=[pltpu.VMEM((2 * kept, TILE, width), F32)],
        compiler_params=grant(8),
        name="collect",
    )(spot, *parts)


def body(designs, prototypes, candidates, positives):
    proto_count = lax.axis_size("proto")
    design_axis = lax.axis_size("design")
    half = proto_count // 2
    lanes = design_axis // 2
    cand_count = candidates.shape[1]
    width = designs.shape[1]
    count = designs.shape[0]
    blocks_dev = prototypes.shape[0] // TILE
    quarter = blocks_dev // design_axis
    cap = max(2, (4 * cand_count + 3 * proto_count - 1) // (3 * proto_count))
    parts = PARTS
    step = width // parts
    p = lax.axis_index("proto").astype(jnp.int32)
    d = lax.axis_index("design").astype(jnp.int32)
    q = p % half
    h = p // half
    y = d // 2
    c = d % 2
    me = d.reshape(1)
    shifts = list(range(half - 1, 0, -1))
    evens = list(range(2, half, 2))
    flip = half // 2
    across = half + flip
    columns = [slice(i * step, (i + 1) * step) for i in range(parts)]

    wanted = request_table(candidates[0], blocks_dev, cap, proto_count)
    wanted = wanted.reshape(2, half, cap)
    near = [wanted[h, q ^ s] for s in range(half)]
    other = [wanted[1 - h, q ^ s ^ flip] for s in range(half)]
    asking, owed = {0: other[0]}, {0: other[flip]}
    for s in shifts:
        note = [other[s], other[s ^ flip]]
        if s == 1:
            note += [near[u ^ 1] for u in [0] + evens]
        note = xor_proto(jnp.stack(note), s)
        asking[s], owed[s] = note[0], note[1]
        if s == 1:
            beside = {u: note[2 + n] for n, u in enumerate([0] + evens)}

    shard = prototypes.reshape(blocks_dev, TILE, width)
    mine = lax.dynamic_slice_in_dim(shard, d * quarter, quarter, axis=0).astype(BF)
    sent = {}
    for i in range(parts):
        piece = mine[:, :, columns[i]]
        for u in evens:
            sent[u, i] = xor_proto(piece, u)
        sent["far", i] = xor_proto(piece, across)

    def share(piece):
        held = [piece]
        for ys in range(1, lanes):
            held.append(xor_design(piece, 2 * ys))
        return held + [xor_design(held[ys], 1) for ys in range(lanes)]

    def flat(piece):
        return piece.reshape(cap * TILE, step)

    own_rows = [[None] * parts for _ in range(half)]
    far_rows = [[None] * parts for _ in range(half)]
    out = gather_round(beside[0], shard, parts)
    for i in range(parts):
        own_rows[1][i] = flat(xor_proto(out[i], 1))
    out = gather_round(near[0], shard, parts)
    for i in range(parts):
        own_rows[0][i] = flat(out[i])
    for i in range(parts):
        for u in evens:
            held = share(sent[u, i])
            (out,) = gather_held(me, [beside[u]], held, lanes)
            own_rows[u ^ 1][i] = flat(xor_proto(out, 1))
            (out,) = gather_held(me, [near[u]], held, lanes)
            own_rows[u][i] = flat(out)
        held = share(sent["far", i])
        outs = gather_held(me, [asking[s] for s in shifts], held, lanes)
        for s, out in zip(shifts, outs):
            far_rows[s][i] = flat(xor_proto(out, s))
        (out,) = gather_held(me, [asking[0]], held, lanes)
        far_rows[0][i] = flat(out)

    def bases(lists, which_half, group, turn=0):
        out = []
        for s in group:
            first = (which_half * half + (q ^ s ^ turn)) * blocks_dev
            out.append(jnp.where(lists[s] >= 0, (first + lists[s]) * TILE, -(2**30)))
        return jnp.concatenate(out)

    pos = positives.reshape(1, count)
    logits, sums = {}, []
    for group in groups_of(half).values():
        *got, top, total, hit = own_logits(
            bases(near, h, group), designs, pos, [own_rows[s] for s in group], cap
        )
        logits.update(zip(group, got))
        sums += [top, total, hit]
    stats, far_g, first = far_grads(
        bases(other, 1 - h, range(half), flip), designs, pos, sums, far_rows, cap, parts
    )
    back_tiles = [first] + far_tiles(designs, far_g, parts)
    losses, top, inv = stats
    own_g, own_tiles = [], []
    for s in range(half):
        g, t = own_grad(
            bases(near, h, [s]), designs, pos, top, inv, logits[s], cap, parts
        )
        own_g.append(g)
        own_tiles.append(t)

    kept = lanes * quarter

    def spots(tables):
        table = jnp.concatenate(tables)
        owner = table // quarter
        at = ((owner // 2) ^ y) * quarter + table % quarter
        at = at + jnp.where(owner % 2 == c, 0, kept)
        return jnp.where(table >= 0, at, -1)

    def reduce_shard(tables, tiles):
        keep, give = collect(spots(tables), tiles, cap, kept)
        came = xor_design(give, 1)
        keep = keep + came.astype(F32)
        keep = keep.reshape(lanes, quarter, TILE, step)
        onward = [keep[ys].astype(BF) for ys in range(1, lanes)]
        total = keep[0]
        for ys in range(1, lanes):
            back = xor_design(onward[ys - 1], 2 * ys)
            total = total + back.astype(F32)
        return total

    result = []
    dgrad = []
    far_tables = [owed[s] for s in range(half)]
    for i in range(parts):
        tiles = [back_tiles[i][flip]]
        tiles += [xor_proto(back_tiles[i][s ^ flip], s) for s in range(1, half)]
        total = reduce_shard(far_tables, tiles)
        landed = [xor_proto(total.astype(BF), half)]
        for u in evens:
            tile = xor_proto(own_tiles[u ^ 1][i], 1)
            total = reduce_shard([near[u], beside[u]], [own_tiles[u][i], tile])
            landed.append(xor_proto(total.astype(BF), u))
        tile = xor_proto(own_tiles[1][i], 1)
        total = reduce_shard([near[0], beside[0]], [own_tiles[0][i], tile])
        for piece in landed:
            total = total + piece.astype(F32)
        result.append(total)
        dgrad.append(
            design_grad(own_g + list(far_g), [r[i] for r in own_rows + far_rows])
        )
    result = jnp.concatenate(result, axis=-1).reshape(quarter * TILE, width)
    return (losses.reshape(count), jnp.concatenate(dgrad, axis=-1), result)


def groups_of(half):
    late = list(range(3, half, 2))
    return {"own_a": [s for s in range(half) if s not in late], "own_b": late}


def solution(mesh):
    return jax.shard_map(
        body,
        mesh=mesh,
        in_specs=(
            P(("proto", "design"), None),
            P("proto", None),
            P(("proto", "design"), None),
            P(("proto", "design")),
        ),
        out_specs=(
            P(("proto", "design")),
            P(("proto", "design"), None),
            P(("proto", "design"), None),
        ),
        check_vma=False,
    )
```

```python
import functools

import jax
import jax.numpy as jnp
from jax import lax
from jax.experimental import pallas as pl
from jax.experimental.pallas import tpu as pltpu
from jax.sharding import PartitionSpec as P


D = 1024
TILE = 128
BF = jnp.bfloat16
F32 = jnp.float32
NEG = -1e30
PARTS = 2


def xor_proto(x, shift):
    count = lax.axis_size("proto")
    return lax.ppermute(x, "proto", [(i, i ^ shift) for i in range(count)])


def xor_design(x, shift):
    count = lax.axis_size("design")
    return lax.ppermute(x, "design", [(i, i ^ shift) for i in range(count)])


def request_table(block_list, blocks_dev, capacity, proto_count):
    owners = block_list // blocks_dev
    local_ids = block_list % blocks_dev
    ids = jnp.arange(block_list.shape[0], dtype=jnp.int32)
    earlier = (owners[:, None] == owners[None, :]) & (ids[None, :] < ids[:, None])
    rank_of = jnp.sum(earlier.astype(jnp.int32), axis=1)
    slot_of = owners * capacity + rank_of
    slots = jnp.arange(proto_count * capacity, dtype=jnp.int32)
    hit = slot_of[None, :] == slots[:, None]
    return jnp.sum(jnp.where(hit, local_ids[None, :] + 1, 0), axis=1) - 1


HBM = pl.BlockSpec(memory_space=pl.ANY)
VM = pl.BlockSpec(memory_space=pltpu.VMEM)
SM = pl.BlockSpec(memory_space=pltpu.SMEM)
FIXED = pl.BlockSpec(memory_space=pltpu.HBM)


def grant(mib):
    return pltpu.CompilerParams(vmem_limit_bytes=mib << 20)


def gather_round_kernel(parts, table, src, *refs):
    outs, buf, sems = refs[:parts], refs[parts], refs[parts + 1]
    cap, _, step = outs[0].shape
    copies = []
    for k in range(cap):
        row = jnp.maximum(table[k], 0)
        copies.append(pltpu.make_async_copy(src.at[row], buf.at[k], sems.at[k]))
    for copy in copies:
        copy.start()
    for k, copy in enumerate(copies):
        copy.wait()
        for i in range(parts):
            outs[i][k] = buf[k, :, i * step : (i + 1) * step].astype(BF)


def gather_round(table, shard, parts):
    cap = table.shape[0]
    _, tile, width = shard.shape
    return pl.pallas_call(
        functools.partial(gather_round_kernel, parts),
        out_shape=[jax.ShapeDtypeStruct((cap, tile, width // parts), BF)] * parts,
        in_specs=[SM, FIXED],
        out_specs=[VM] * parts,
        scratch_shapes=[
            pltpu.VMEM((cap, tile, width), F32),
            pltpu.SemaphoreType.DMA((cap,)),
        ],
        compiler_params=grant(6),
        name="gather_round",
    )(table, shard)


def gather_held_kernel(n_src, n_out, quarter, lanes, me, *refs):
    tables, srcs = refs[:n_out], refs[n_out : n_out + n_src]
    outs, sems = refs[n_out + n_src : -1], refs[-1]
    cap = outs[0].shape[0]
    y, c = me[0] // 2, me[0] % 2
    for n in range(n_out):

        @pl.loop(0, cap)
        def _(k):
            row = jnp.maximum(tables[n][k], 0)
            owner, inside = row // quarter, row % quarter
            which = ((owner % 2) ^ c) * lanes + ((owner // 2) ^ y)
            for a in range(n_src):

                @pl.when(which == a)
                def _():
                    pltpu.make_async_copy(
                        srcs[a].at[inside], outs[n].at[k], sems.at[n * cap + k]
                    ).start()

    for n in range(n_out):

        @pl.loop(0, cap)
        def _(k):
            pltpu.make_async_copy(srcs[0].at[0], outs[n].at[k], sems.at[n * cap + k]).wait()


def gather_held(me, tables, srcs, lanes):
    n = len(tables)
    cap = tables[0].shape[0]
    quarter = srcs[0].shape[0]
    shape = (cap,) + srcs[0].shape[1:]
    return pl.pallas_call(
        functools.partial(gather_held_kernel, len(srcs), n, quarter, lanes),
        out_shape=[jax.ShapeDtypeStruct(shape, BF)] * n,
        in_specs=[SM] * (n + 1) + [HBM] * len(srcs),
        out_specs=[VM] * n,
        scratch_shapes=[pltpu.SemaphoreType.DMA((n * cap,))],
        compiler_params=grant(2),
        name="gather_held",
    )(me, *tables, *srcs)


def contract(rows, x, lanes):
    step = rows[0].shape[1]
    total = None
    for i, part in enumerate(rows):
        got = lax.dot_general(
            part[...],
            x[lanes, i * step : (i + 1) * step],
            (((1,), (1,)), ((), ())),
            preferred_element_type=F32,
        )
        total = got if total is None else total + got
    return total


EXP_SCALE = (D ** (-0.5)) * 1.4426950408889634


def fold(tile, op):
    return op(tile.reshape(tile.shape[0] // 8, 8, tile.shape[1]), axis=0)


def slot_stats(base, rel, slots):
    top = None
    hit = None
    for n, ref in slots:
        piece = ref[...]
        target = rel == base[n]
        found = fold(jnp.where(target, piece, 0.0), jnp.sum)
        piece = piece + jnp.where(base[n] < 0, NEG, 0.0)
        high = fold(piece, jnp.max)
        top = high if top is None else jnp.maximum(top, high)
        hit = found if hit is None else hit + found
    return jnp.max(top, axis=0, keepdims=True), jnp.sum(hit, axis=0, keepdims=True)


def slot_power(base, n, ref, top):
    piece = ref[...] + jnp.where(base[n] < 0, NEG, 0.0)
    return jnp.exp2((piece - top) * EXP_SCALE)


def relative(pos, lanes):
    line = lax.broadcasted_iota(jnp.int32, (TILE, lanes), 0)
    return pos - line


def own_kernel(group, cap, lanes, parts, base, x, pos, *refs):
    rows = [refs[s * parts : (s + 1) * parts] for s in range(group)]
    kept = refs[group * parts : group * (parts + 1)]
    top_out, sum_out, hit_out, logits, sems = refs[group * (parts + 1) :]
    count = x.shape[0]

    def copy_out(s, j):
        at = pl.ds(pl.multiple_of(j * lanes, lanes), lanes)
        return pltpu.make_async_copy(logits.at[s, :, at], kept[s].at[:, at], sems.at[s, j])

    @pl.loop(0, count // lanes)
    def _(j):
        at = pl.ds(pl.multiple_of(j * lanes, lanes), lanes)
        for s in range(group):
            logits[s, :, at] = contract(rows[s], x, at)
            copy_out(s, j).start()
        slots = [
            (s * cap + k, logits.at[s, pl.ds(k * TILE, TILE), at])
            for s in range(group)
            for k in range(cap)
        ]
        top, hit = slot_stats(base, relative(pos[:, at], lanes), slots)
        total = None
        for n, ref in slots:
            part = fold(slot_power(base, n, ref, top), jnp.sum)
            total = part if total is None else total + part
        top_out[:, at] = top
        hit_out[:, at] = hit
        sum_out[:, at] = jnp.sum(total, axis=0, keepdims=True)

    @pl.loop(0, count // lanes)
    def _(j):
        for s in range(group):
            copy_out(s, j).wait()


def own_logits(base, x, pos, rows, cap, lanes=256):
    group, parts = len(rows), len(rows[0])
    rows = [r for row in rows for r in row]
    count = x.shape[0]
    line = (1, count)
    shape = (rows[0].shape[0], count)
    return pl.pallas_call(
        functools.partial(own_kernel, group, cap, lanes, parts),
        out_shape=[pltpu.HBM(shape, F32)] * group + [jax.ShapeDtypeStruct(line, F32)] * 3,
        in_specs=[SM] + [VM] * (2 + len(rows)),
        out_specs=[FIXED] * group + [VM] * 3,
        scratch_shapes=[
            pltpu.VMEM((group,) + shape, F32),
            pltpu.SemaphoreType.DMA((group, count // lanes)),
        ],
        compiler_params=grant(12),
        name="own_logits",
    )(base, x, pos, *rows)


def far_kernel(group, cap, lanes, parts, n_stats, base, x, pos, *refs):
    stats = [refs[3 * i : 3 * i + 3] for i in range(n_stats)]
    refs = refs[3 * n_stats :]
    rows = [refs[s * parts : (s + 1) * parts] for s in range(group)]
    refs = refs[group * parts :]
    losses, top_out, inv_out = refs[:3]
    kept = refs[3:-4]
    logits, grads, tiles, sems = refs[-4:]
    count, _ = x.shape
    scale = D ** (-0.5)
    for j in range(0, count, lanes):
        turn = (j // lanes) % 2
        at = pl.ds(j, lanes)
        for s in range(group):
            logits[turn, s * cap * TILE : (s + 1) * cap * TILE, :] = contract(
                rows[s], x, pl.ds(j, lanes)
            )
        slots = [
            (n, logits.at[turn, pl.ds(n * TILE, TILE), :]) for n in range(group * cap)
        ]
        rel = relative(pos[:, at], lanes)
        top, hit = slot_stats(base, rel, slots)
        both = top
        for top_own, _, _ in stats:
            both = jnp.maximum(both, top_own[:, at])
        total = None
        for n, ref in slots:
            power = slot_power(base, n, ref, both)
            ref[...] = power
            part = fold(power, jnp.sum)
            total = part if total is None else total + part
        total = jnp.sum(total, axis=0, keepdims=True)
        for top_own, sum_own, hit_own in stats:
            total = total + sum_own[:, at] * jnp.exp2((top_own[:, at] - both) * EXP_SCALE)
            hit = hit + hit_own[:, at]
        losses[:, at] = both * scale + jnp.log(total) - hit * scale
        inv = 1.0 / total
        top_out[:, at] = both
        inv_out[:, at] = inv
        for n, ref in slots:
            s, k = n // cap, n % cap
            target = jnp.where(rel == base[n], 1.0, 0.0)
            grads[s, k * TILE : (k + 1) * TILE, at] = (ref[...] * inv - target).astype(BF)
    step = tiles.shape[-1]
    sources = [grads.at[s] for s in range(group)] + [tiles.at[s] for s in range(group)]
    copies = [
        pltpu.make_async_copy(a, b, sems.at[n]) for n, (a, b) in enumerate(zip(sources, kept))
    ]
    for copy in copies[:group]:
        copy.start()
    for s in reversed(range(group)):
        tiles[s] = jnp.dot(grads[s], x[:, :step], preferred_element_type=F32).astype(BF)
        copies[group + s].start()
    for copy in copies:
        copy.wait()


def far_grads(base, x, pos, stats, rows, cap, parts, first, lanes=256):
    group = len(rows)
    rows = [r for row in rows for r in row]
    count, _ = x.shape
    size = rows[0].shape[0]
    outs = [((1, count), F32)] * 3 + [((size, count), BF)] * group
    outs += [((size, first), BF)] * group
    got = pl.pallas_call(
        functools.partial(far_kernel, group, cap, lanes, parts, len(stats) // 3),
        out_shape=[jax.ShapeDtypeStruct(*o) for o in outs[:3]]
        + [pltpu.HBM(*o) for o in outs[3:]],
        in_specs=[SM] + [VM] * (2 + len(stats) + len(rows)),
        out_specs=[VM] * 3 + [FIXED] * (len(outs) - 3),
        scratch_shapes=[
            pltpu.VMEM((2, group * size, lanes), F32),
            pltpu.VMEM((group, size, count), BF),
            pltpu.VMEM((group, size, first), BF),
            pltpu.SemaphoreType.DMA((2 * group,)),
        ],
        compiler_params=grant(20),
        name="far_grads",
    )(base, x, pos, *stats, *rows)
    return got[:3], got[3 : 3 + group], got[3 + group :]


def far_widths(width):
    most = width * 3 // 8
    return [most, most, width - 2 * most]


def far_tiles_kernel(group, first, x, *refs):
    grads, tiles = refs[:group], refs[group:]
    at = first
    for n, tile in enumerate(tiles):
        step = tile.shape[1]
        tile[...] = jnp.dot(
            grads[n % group][...], x[:, at : at + step], preferred_element_type=F32
        ).astype(BF)
        if n % group == group - 1:
            at += step


def far_tiles(x, grads, widths):
    group = len(grads)
    shapes = [(grads[0].shape[0], w) for w in widths[1:] for _ in range(group)]
    got = pl.pallas_call(
        functools.partial(far_tiles_kernel, group, widths[0]),
        out_shape=[jax.ShapeDtypeStruct(shape, BF) for shape in shapes],
        in_specs=[VM] * (1 + group),
        out_specs=[VM] * len(shapes),
        compiler_params=grant(6),
        name="far_tiles",
    )(x, *grads)
    return [got[i : i + group] for i in range(0, len(got), group)]


def own_grad_kernel(cap, parts, base, x, pos, top, inv, logits, grad, *tiles):
    count, width = x.shape
    rel = relative(pos[...], count)
    for k in range(cap):
        ref = logits.at[pl.ds(k * TILE, TILE), :]
        power = slot_power(base, k, ref, top[...])
        target = jnp.where(rel == base[k], 1.0, 0.0)
        grad[k * TILE : (k + 1) * TILE, :] = (power * inv[...] - target).astype(BF)
    step = width // parts
    for i in range(parts):
        tiles[i][...] = jnp.dot(
            grad[...], x[:, i * step : (i + 1) * step], preferred_element_type=F32
        ).astype(BF)


def own_grad(base, x, pos, top, inv, logits, cap, parts):
    count, width = x.shape
    size = logits.shape[0]
    outs = [((size, count), BF)] + [((size, width // parts), BF)] * parts
    got = pl.pallas_call(
        functools.partial(own_grad_kernel, cap, parts),
        out_shape=[jax.ShapeDtypeStruct(*o) for o in outs],
        in_specs=[SM] + [VM] * 5,
        out_specs=[VM] * len(outs),
        compiler_params=grant(6),
        name="own_grad",
    )(base, x, pos, top, inv, logits)
    return got[0], got[1:]


def design_grad_kernel(n, chunk, *refs):
    grads, rows, out = refs[:n], refs[n : 2 * n], refs[2 * n]

    @pl.loop(0, out.shape[0] // chunk)
    def _(j):
        at = pl.ds(pl.multiple_of(j * chunk, chunk), chunk)
        acc = None
        for g, r in zip(grads, rows):
            part = lax.dot_general(
                g[:, at], r[...], (((0,), (0,)), ((), ())), preferred_element_type=F32
            )
            acc = part if acc is None else acc + part
        out[at, :] = acc.astype(BF)


def design_grad(grads, rows, chunk=256):
    n = len(grads)
    return pl.pallas_call(
        functools.partial(design_grad_kernel, n, chunk),
        out_shape=jax.ShapeDtypeStruct((grads[0].shape[1], rows[0].shape[1]), BF),
        in_specs=[VM] * (2 * n),
        out_specs=VM,
        compiler_params=grant(8),
        name="design_grad",
    )(*grads, *rows)


def collect_kernel(n, cap, spot, *refs):
    parts = refs[:n]
    keep, give, acc = refs[n:]
    kept = keep.shape[0]
    acc[...] = jnp.zeros_like(acc)
    for i in range(n * cap):

        @pl.when(spot[i] >= 0)
        def _():
            s, k = i // cap, i % cap
            acc[spot[i]] += parts[s][k * TILE : (k + 1) * TILE, :].astype(F32)

    keep[...] = acc[:kept]
    give[...] = acc[kept:].astype(BF)


def collect(spot, parts, cap, kept):
    n = len(parts)
    width = parts[0].shape[1]
    shape = (kept, TILE, width)
    return pl.pallas_call(
        functools.partial(collect_kernel, n, cap),
        out_shape=[jax.ShapeDtypeStruct(shape, F32), jax.ShapeDtypeStruct(shape, BF)],
        in_specs=[SM] + [VM] * n,
        out_specs=[VM] * 2,
        scratch_shapes=[pltpu.VMEM((2 * kept, TILE, width), F32)],
        compiler_params=grant(8),
        name="collect",
    )(spot, *parts)


def body(designs, prototypes, candidates, positives):
    proto_count = lax.axis_size("proto")
    design_axis = lax.axis_size("design")
    half = proto_count // 2
    lanes = design_axis // 2
    cand_count = candidates.shape[1]
    width = designs.shape[1]
    count = designs.shape[0]
    blocks_dev = prototypes.shape[0] // TILE
    quarter = blocks_dev // design_axis
    cap = max(2, (4 * cand_count + 3 * proto_count - 1) // (3 * proto_count))
    parts = PARTS
    step = width // parts
    p = lax.axis_index("proto").astype(jnp.int32)
    d = lax.axis_index("design").astype(jnp.int32)
    q = p % half
    h = p // half
    y = d // 2
    c = d % 2
    me = d.reshape(1)
    shifts = list(range(half - 1, 0, -1))
    evens = list(range(2, half, 2))
    widths = far_widths(width)
    columns = [slice(i * step, (i + 1) * step) for i in range(parts)]

    wanted = request_table(candidates[0], blocks_dev, cap, proto_count)
    wanted = wanted.reshape(2, half, cap)
    near = [wanted[h, q ^ s] for s in range(half)]
    other = [wanted[1 - h, q ^ s] for s in range(half)]
    asking = {0: other[0]}
    for s in shifts:
        if s == 1:
            note = jnp.stack([other[1]] + [near[u ^ 1] for u in [0] + evens])
            note = xor_proto(note, 1)
            asking[1] = note[0]
            beside = {u: note[1 + n] for n, u in enumerate([0] + evens)}
        else:
            asking[s] = xor_proto(other[s], s)

    shard = prototypes.reshape(blocks_dev, TILE, width)
    mine = lax.dynamic_slice_in_dim(shard, d * quarter, quarter, axis=0).astype(BF)
    sent = {}
    for i in range(parts):
        piece = mine[:, :, columns[i]]
        for u in evens:
            sent[u, i] = xor_proto(piece, u)
        sent["far", i] = xor_proto(piece, half)

    def share(piece):
        held = [piece]
        for ys in range(1, lanes):
            held.append(xor_design(piece, 2 * ys))
        return held + [xor_design(held[ys], 1) for ys in range(lanes)]

    def flat(piece):
        return piece.reshape(cap * TILE, step)

    own_rows = [[None] * parts for _ in range(half)]
    far_rows = [[None] * parts for _ in range(half)]
    out = gather_round(beside[0], shard, parts)
    for i in range(parts):
        own_rows[1][i] = flat(xor_proto(out[i], 1))
    out = gather_round(near[0], shard, parts)
    for i in range(parts):
        own_rows[0][i] = flat(out[i])
    for i in range(parts):
        for u in evens:
            held = share(sent[u, i])
            (out,) = gather_held(me, [beside[u]], held, lanes)
            own_rows[u ^ 1][i] = flat(xor_proto(out, 1))
            (out,) = gather_held(me, [near[u]], held, lanes)
            own_rows[u][i] = flat(out)
        held = share(sent["far", i])
        outs = gather_held(me, [asking[s] for s in shifts], held, lanes)
        for s, out in zip(shifts, outs):
            far_rows[s][i] = flat(xor_proto(out, s))
        (out,) = gather_held(me, [asking[0]], held, lanes)
        far_rows[0][i] = flat(out)

    def bases(lists, which_half, group):
        out = []
        for s in group:
            first = (which_half * half + (q ^ s)) * blocks_dev
            out.append(jnp.where(lists[s] >= 0, (first + lists[s]) * TILE, -(2**30)))
        return jnp.concatenate(out)

    pos = positives.reshape(1, count)
    logits, sums = {}, []
    for group in groups_of(half).values():
        *got, top, total, hit = own_logits(
            bases(near, h, group), designs, pos, [own_rows[s] for s in group], cap
        )
        logits.update(zip(group, got))
        sums += [top, total, hit]
    stats, far_g, first = far_grads(
        bases(other, 1 - h, range(half)), designs, pos, sums, far_rows, cap, parts, widths[0]
    )
    back_tiles = [first] + far_tiles(designs, far_g, widths)
    losses, top, inv = stats
    own_g, own_tiles = [], []
    for s in range(half):
        g, t = own_grad(
            bases(near, h, [s]), designs, pos, top, inv, logits[s], cap, parts
        )
        own_g.append(g)
        own_tiles.append(t)

    kept = lanes * quarter

    def spots(tables):
        table = jnp.concatenate(tables)
        owner = table // quarter
        at = ((owner // 2) ^ y) * quarter + table % quarter
        at = at + jnp.where(owner % 2 == c, 0, kept)
        return jnp.where(table >= 0, at, -1)

    def reduce_shard(tables, tiles):
        keep, give = collect(spots(tables), tiles, cap, kept)
        came = xor_design(give, 1)
        keep = keep + came.astype(F32)
        keep = keep.reshape(lanes, quarter, TILE, keep.shape[-1])
        onward = [keep[ys].astype(BF) for ys in range(1, lanes)]
        total = keep[0]
        for ys in range(1, lanes):
            back = xor_design(onward[ys - 1], 2 * ys)
            total = total + back.astype(F32)
        return total

    result = []
    dgrad = []
    far_tables = [asking[s] for s in range(half)]
    crossed = []
    for tiles in back_tiles:
        tiles = [tiles[0]] + [xor_proto(tiles[s], s) for s in range(1, half)]
        total = reduce_shard(far_tables, tiles)
        crossed.append(xor_proto(total.astype(BF), half))
    crossed = jnp.concatenate(crossed, axis=-1)
    for i in range(parts):
        landed = [crossed[:, :, columns[i]]]
        for u in evens:
            tile = xor_proto(own_tiles[u ^ 1][i], 1)
            total = reduce_shard([near[u], beside[u]], [own_tiles[u][i], tile])
            landed.append(xor_proto(total.astype(BF), u))
        tile = xor_proto(own_tiles[1][i], 1)
        total = reduce_shard([near[0], beside[0]], [own_tiles[0][i], tile])
        for piece in landed:
            total = total + piece.astype(F32)
        result.append(total)
        dgrad.append(
            design_grad(own_g + list(far_g), [r[i] for r in own_rows + far_rows])
        )
    result = jnp.concatenate(result, axis=-1).reshape(quarter * TILE, width)
    return (losses.reshape(count), jnp.concatenate(dgrad, axis=-1), result)


def groups_of(half):
    late = list(range(3, half, 2))
    return {"own_a": [s for s in range(half) if s not in late], "own_b": late}


def solution(mesh):
    return jax.shard_map(
        body,
        mesh=mesh,
        in_specs=(
            P(("proto", "design"), None),
            P("proto", None),
            P(("proto", "design"), None),
            P(("proto", "design")),
        ),
        out_specs=(
            P(("proto", "design")),
            P(("proto", "design"), None),
            P(("proto", "design"), None),
        ),
        check_vma=False,
    )
```
